32 devices in a mesh: fsdp: 2 (over x), ctx: 4 (over y, core), tp: 4 (over z).
Axes of the slice: x: 2, y: 2, z: 4, core: 2. Of those that a mesh axis runs over, the one named last changes fastest.
Arguments:
- inputs: bfloat16 [8, 1024, 768], P('fsdp', ('ctx', 'tp')), may hold values from -6 to 6
- segments: int32 [8, 1024], P('fsdp', ('ctx', 'tp')), may hold values from 0 to 15, never falling along the last dimension, each value on 1 to 512 neighbouring positions
- ln1_gain: float32 [768], replicated, may hold values from 0.25 to 1.75
- ln1_bias: float32 [768], replicated, may hold values from -3 to 3
- query_key_value_weight: bfloat16 [768, 3, 768], P(('fsdp', 'ctx'), None, 'tp'), may hold values from -0.21875 to 0.21875
- b_qv: float32 [2, 768], P(None, 'tp'), may hold values from -3 to 3
- output_weight: bfloat16 [768, 768], P('tp', ('fsdp', 'ctx')), may hold values from -0.625 to 0.625
- output_bias: float32 [768], replicated, may hold values from -3 to 3
- ln2_gain: float32 [768], replicated, may hold values from 0.25 to 1.75
- ln2_bias: float32 [768], replicated, may hold values from -3 to 3
- up_weight: bfloat16 [768, 3072], P(('fsdp', 'ctx'), 'tp'), may hold values from -0.21875 to 0.21875
- up_bias: float32 [3072], P('tp'), may hold values from -3 to 3
- down_weight: bfloat16 [3072, 768], P('tp', ('fsdp', 'ctx')), may hold values from -0.109375 to 0.109375
- down_bias: float32 [768], replicated, may hold values from -3 to 3
- out_grad: bfloat16 [8, 1024, 768], P('fsdp', ('ctx', 'tp')), may hold values from -6 to 6
Outputs:
- output: bfloat16 [8, 1024, 768], P('fsdp', ('ctx', 'tp'))
- input_grad: float32 [8, 1024, 768], P('fsdp', ('ctx', 'tp'))
- grad_ln1_gain: float32 [768], replicated
- grad_ln1_bias: float32 [768], replicated
- grad_qkv: float32 [768, 3, 768], P(('fsdp', 'ctx'), None, 'tp')
- grad_qkv_bias: float32 [2, 768], P(None, 'tp')
- grad_out: float32 [768, 768], P('tp', ('fsdp', 'ctx'))
- grad_out_bias: float32 [768], replicated
- grad_ln2_gain: float32 [768], replicated
- grad_ln2_bias: float32 [768], replicated
- grad_up: float32 [768, 3072], P(('fsdp', 'ctx'), 'tp')
- grad_up_bias: float32 [3072], P('tp')
- grad_down: float32 [3072, 768], P('tp', ('fsdp', 'ctx'))
- grad_down_bias: float32 [768], replicated
The draws below stay inside these ranges and needn't reach their ends.
Inputs may be any that keep to these rules, and one draw needn't show every extreme that they name: `segments`: segment numbers never fall along a sequence; each number covers 1 to 512 positions of a sequence, one exactly 512.
All inputs are finite; a program needn't handle non-finite values.
Results may differ from the reference program's by a relative error of at most 0.011.
Values may be sent and summed in bfloat16 or wider, within the bound.
No kernel may reach another device: no remote copies, remote signals or barrier semaphores. Data moves between devices by JAX's collectives and lax.ppermute only.
A program may use at most 128 MiB of HBM per device.

```python
import math
from functools import partial
import jax
import jax.numpy as jnp
import numpy as np
from jax import lax

D = 768
HEADS = 12
DH = 64
FF = 3072
HD = 768
SEGS = 16
LEN = 1024
SEG_MOST = 512
SEQS = 8


def steps_of(rng, shape, split, smallest, largest):
    level, own = 1.0, jax.random.fold_in(rng, 6)
    for position, blocks in split:
        heights = jnp.exp(jax.random.uniform(jax.random.fold_in(own, position), (blocks,), jnp.float32, smallest / len(split), largest / len(split)))
        level = level * jnp.repeat(heights, shape[position] // blocks).reshape([-1 if axis == position else 1 for axis in range(len(shape))])
    return level


def split_up(number_of, total, bound, slope):
    portions = [(1 << 20) // math.isqrt(rank ** slope) + 1 for rank in range(2, number_of + 1)]
    rest, counts = total - bound - (number_of - 1), [1] * (number_of - 1)
    while rest > 0:
        candidates = [i for i in range(number_of - 1) if counts[i] < bound]
        mass, budget = sum([portions[i] for i in candidates]), rest
        for i in candidates:
            more = min(bound - counts[i], max(1, budget * portions[i] // mass), rest)
            counts[i] = counts[i] + more
            rest = rest - more
    return np.array([bound] + counts)


def uneven(own_key, count, total, reach, lean):
    if count == 2:
        one = jax.random.randint(own_key, (), max(1, total - reach), min(reach, total - 1) + 1)
        return jnp.stack([one, total - one])
    sizes = jnp.asarray(split_up(count, total, reach, lean), jnp.int32)
    twos = (count - 1) // 2
    donor, taker = sizes[1:1 + 2 * twos:2], sizes[2:2 + 2 * twos:2]
    room = jnp.minimum(donor - 1, reach - taker)
    shifted = jax.random.randint(jax.random.fold_in(own_key, 1), (twos,), 0, 1 << 20) % (room + 1)
    sizes = sizes.at[1:1 + 2 * twos:2].set(donor - shifted).at[2:2 + 2 * twos:2].set(taker + shifted)
    return sizes[jax.random.permutation(jax.random.fold_in(own_key, 2), count)]


def gaussian(rng, extent, scale, bound, shards=(), held_as=jnp.bfloat16):
    values = jax.random.normal(rng, extent, jnp.float32) * scale
    if len(shards) > 0:
        values = steps_of(rng, extent, shards, -0.22, 0.18) * values
    return jnp.clip(values, min=-bound, max=bound).astype(held_as)


def setup_inputs(seed: int = 0) -> dict:
    streams_of = jax.random.split(jax.random.key(seed), 16)
    inputs = gaussian(streams_of[0], (SEQS, LEN, D), 1.0, 6.0, ((0, 2), (1, 16)))
    segments = jax.vmap(lambda own: jnp.searchsorted(jnp.cumsum(uneven(own, SEGS, LEN, SEG_MOST, 2)), jnp.arange(LEN), side="right"))(jax.random.split(streams_of[1], SEQS)).reshape((SEQS, LEN)).astype(jnp.int32)
    ln1_gain = jnp.clip(1.0 + 0.15 * jax.random.normal(streams_of[2], (D,), jnp.float32), 0.25, 1.75)
    ln1_bias = gaussian(streams_of[3], (D,), 0.5, 3.0, (), jnp.float32)
    query_key_value_weight = gaussian(streams_of[4], (D, 3, HD), D ** -0.5, 0.21875, ((0, 8), (2, 4)))
    b_qv = gaussian(streams_of[5], (2, HD), 0.5, 3.0, ((1, 4),), jnp.float32)
    output_weight = gaussian(streams_of[6], (HD, D), (HD // 8) ** -0.5, 0.625, ((0, 4), (1, 8)))
    output_bias = gaussian(streams_of[7], (D,), 0.5, 3.0, (), jnp.float32)
    ln2_gain = jnp.clip(1.0 + 0.15 * jax.random.normal(streams_of[8], (D,), jnp.float32), 0.25, 1.75)
    ln2_bias = gaussian(streams_of[9], (D,), 0.5, 3.0, (), jnp.float32)
    up_weight = gaussian(streams_of[10], (D, FF), D ** -0.5, 0.21875, ((0, 8), (1, 4)))
    up_bias = gaussian(streams_of[11], (FF,), 0.5, 3.0, ((0, 4),), jnp.float32)
    down_weight = gaussian(streams_of[12], (FF, D), FF ** -0.5, 0.109375, ((0, 4), (1, 8)))
    down_bias = gaussian(streams_of[13], (D,), 0.5, 3.0, (), jnp.float32)
    out_grad = gaussian(streams_of[14], (SEQS, LEN, D), 1.0, 6.0, ((0, 2), (1, 16)))
    return dict(inputs=inputs, segments=segments, ln1_gain=ln1_gain, ln1_bias=ln1_bias, query_key_value_weight=query_key_value_weight, b_qv=b_qv, output_weight=output_weight, output_bias=output_bias, ln2_gain=ln2_gain, ln2_bias=ln2_bias, up_weight=up_weight, up_bias=up_bias, down_weight=down_weight, down_bias=down_bias, out_grad=out_grad)


EPS = 1e-06
HIGH_PRECISION = lax.Precision.HIGHEST

@jax.custom_vjp
def low(v):
    return lax.optimization_barrier(v.astype(jnp.bfloat16)).astype(jnp.float32)

@jax.custom_vjp
def lowered_backward(v):
    return v

def low_keep(v):
    return (low(v), None)

def low_pass(kept, grad):
    return (grad,)

def back_keep(v):
    return (v, None)

def back_low(kept, grad):
    return (low(grad),)
low.defvjp(low_keep, low_pass)
lowered_backward.defvjp(back_keep, back_low)

def layer_norm(values, gain, bias):
    mean = lax.optimization_barrier(jnp.mean(values, -1, keepdims=True))
    centred = values - mean
    variance = lax.optimization_barrier(jnp.mean(centred * centred, -1, keepdims=True))
    return centred * lax.rsqrt(variance + EPS) * gain + bias

def attend_one(packed):
    query, keyset, values, labels = packed
    scores = jnp.einsum('qhd,khd->hqk', query, keyset, precision=HIGH_PRECISION) * 0.125
    scores = lowered_backward(scores)
    same = labels[:, None] == labels[None, :]
    scores = jnp.where(same[None], scores, -1e+30)
    probs = jax.nn.softmax(scores, axis=-1)
    return jnp.einsum('hqk,khd->qhd', low(probs), values, precision=HIGH_PRECISION)

def forward(segments, inputs, ln1_gain, ln1_bias, query_key_value_weight, b_qv, output_weight, output_bias, ln2_gain, ln2_bias, up_weight, up_bias, down_weight, down_bias):
    count = inputs.shape[0]
    length = inputs.shape[1]
    normalized_input = low(layer_norm(inputs, ln1_gain, ln1_bias))
    mixed_tokens = jnp.einsum('gzr,rix->gzix', normalized_input, query_key_value_weight, precision=HIGH_PRECISION)
    query = lowered_backward(low(mixed_tokens[:, :, 0] + b_qv[0]))
    keyset = lowered_backward(low(mixed_tokens[:, :, 1]))
    values = lowered_backward(low(mixed_tokens[:, :, 2] + b_qv[1]))
    shaped = (count, length, HEADS, DH)
    attention_output = lax.map(jax.checkpoint(attend_one), (query.reshape(shaped), keyset.reshape(shaped), values.reshape(shaped), segments))
    keep = (segments > 0).astype(inputs.dtype)
    attention_output = attention_output.reshape(count, length, HD) * keep[:, :, None]
    attention_output = lowered_backward(low(attention_output))
    residual_branch = lowered_backward(jnp.einsum('tyc,cp->typ', attention_output, output_weight, precision=HIGH_PRECISION) + output_bias)
    middle_state = inputs + residual_branch
    normalized_second = low(layer_norm(middle_state, ln2_gain, ln2_bias))
    preactivation = lowered_backward(jnp.einsum('xnh,he->xne', normalized_second, up_weight, precision=HIGH_PRECISION) + up_bias)
    hidden_state = low(jax.nn.gelu(preactivation, approximate=False))
    return middle_state + jnp.einsum('qij,jm->qim', hidden_state, down_weight, precision=HIGH_PRECISION) + down_bias

def reference(inputs, segments, ln1_gain, ln1_bias, query_key_value_weight, b_qv, output_weight, output_bias, ln2_gain, ln2_bias, up_weight, up_bias, down_weight, down_bias, out_grad):
    floats = [a.astype(jnp.float32) for a in (inputs, ln1_gain, ln1_bias, query_key_value_weight, b_qv, output_weight, output_bias, ln2_gain, ln2_bias, up_weight, up_bias, down_weight, down_bias)]
    result, pullback = jax.vjp(partial(forward, segments), *floats)
    grads = pullback(out_grad.astype(jnp.float32))
    return (result.astype(jnp.bfloat16), grads[0], grads[1], grads[2], grads[3], grads[4], grads[5], grads[6], grads[7], grads[8], grads[9], grads[10], grads[11], grads[12])
```

```python
from functools import partial

import jax
import jax.numpy as jnp
from jax import lax
from jax.experimental import pallas as pl
from jax.experimental.pallas import tpu as pltpu
from jax.sharding import PartitionSpec as P

DH = 64
EPS = 1e-06
BF = jnp.bfloat16
F32 = jnp.float32
NEG = -1e30
BQ = 256


def xor_swap(x, axis, k):
    n = lax.axis_size(axis)
    return lax.ppermute(x, axis, [(i, i ^ k) for i in range(n)])


def rows_over_z(arr, z):
    n = lax.axis_size("tp")
    pieces = [lax.dynamic_index_in_dim(arr, z, 0, keepdims=False)]
    for k in range(1, n):
        pieces.append(xor_swap(lax.dynamic_index_in_dim(arr, z ^ k, 0, keepdims=False), "tp", k))
    return jnp.concatenate(pieces, 0)


def rows_back_over_z(rows, z):
    n = lax.axis_size("tp")
    pieces = rows.reshape((n, rows.shape[0] // n) + rows.shape[1:])
    out = jnp.zeros_like(pieces)
    for k in range(n):
        got = pieces[k] if k == 0 else xor_swap(pieces[k], "tp", k)
        out = lax.dynamic_update_index_in_dim(out, got, z ^ k, 0)
    return out


def gather_ctx(own):
    half = jnp.concatenate([own, xor_swap(own, "ctx", 2)], 0)
    return jnp.concatenate([half, xor_swap(half, "ctx", 1)], 0)


def core_sum(partial_rows):
    n = partial_rows.shape[0] // 2
    got = xor_swap(partial_rows[n:].astype(BF), "ctx", 1)
    return partial_rows[:n].astype(F32) + got.astype(F32)


def sum_pair(partial_rows):
    s = core_sum(partial_rows)
    n = s.shape[0] // 2
    got = xor_swap(s.astype(BF), "ctx", 2).astype(F32)
    return s + jnp.concatenate([got[n:], got[:n]], 0)


def sum_own(partial_rows):
    s = core_sum(partial_rows)
    n = s.shape[0] // 2
    return s[:n] + xor_swap(s[n:].astype(BF), "ctx", 2).astype(F32)


def turn_pairs(n, k):
    return [(a * n + b, b * n + (a ^ k)) for a in range(n) for b in range(n)]


def unturn_pairs(n, k):
    return [(b * n + (a ^ k), a * n + b) for a in range(n) for b in range(n)]


def gather_weight(shard, z):
    n = lax.axis_size("tp")
    out = jnp.zeros((n,) + shard.shape, shard.dtype)
    for k in range(n):
        got = lax.ppermute(shard, ("ctx", "tp"), turn_pairs(n, k))
        out = lax.dynamic_update_index_in_dim(out, got, z ^ k, 0)
    out = out.reshape((-1,) + shard.shape[1:])
    if lax.axis_size("fsdp") == 2:
        return jnp.concatenate([out, xor_swap(out, "fsdp", 1)], 0)
    return lax.all_gather(out, "fsdp", axis=0, tiled=True)


def scatter_weight(grad, z):
    n = lax.axis_size("tp")
    if lax.axis_size("fsdp") == 2:
        half = grad.shape[0] // 2
        got = xor_swap(grad[half:].astype(BF), "fsdp", 1)
        s = grad[:half].astype(F32) + got.astype(F32)
    else:
        s = lax.psum_scatter(grad.astype(F32), "fsdp", scatter_dimension=0, tiled=True)
    s = s.astype(BF).reshape((n, -1) + grad.shape[1:])
    total = 0.0
    for k in range(n):
        piece = lax.dynamic_index_in_dim(s, z ^ k, 0, keepdims=False)
        got = lax.ppermute(piece, ("ctx", "tp"), unturn_pairs(n, k))
        total = total + got.astype(F32)
    return total


def butterfly_sum(x):
    for axis in ("ctx", "fsdp", "tp"):
        n = lax.axis_size(axis)
        if n & (n - 1):
            x = lax.psum(x, axis)
            continue
        k = 1
        while k < n:
            x = x + xor_swap(x, axis, k)
            k *= 2
    return x


def head_mask(h, width):
    lane = lax.broadcasted_iota(jnp.int32, (1, width), 1)
    return (lane >= h * DH) & (lane < (h + 1) * DH)


def only_head(x, h):
    return jnp.where(head_mask(h, x.shape[1]), x, jnp.zeros_like(x))


def nt(a, b):
    return lax.dot_general(a, b, (((1,), (1,)), ((), ())), preferred_element_type=F32)


def nn(a, b):
    return lax.dot_general(a, b, (((1,), (0,)), ((), ())), preferred_element_type=F32)


def tn(a, b):
    return lax.dot_general(a, b, (((0,), (0,)), ((), ())), preferred_element_type=F32)


def meets(lo_ref, hi_ref, i, j):
    return (hi_ref[i] >= lo_ref[j]) & (lo_ref[i] <= hi_ref[j])


def attend_kernel(
    heads, lo_ref, hi_ref, q_ref, k_ref, v_ref, segr_ref, segc_ref, o_ref, lse_ref, qm, vm, st, mx
):
    rows = q_ref.shape[0]
    blocks = rows // BQ
    for h in range(heads):
        qm[h] = only_head(q_ref[...] * jnp.asarray(0.125, BF), h)
        vm[h] = only_head(v_ref[...], h)

    def per_query(i, carry):
        qs = pl.ds(pl.multiple_of(i * BQ, BQ), BQ)
        seg_q = segr_ref[:, qs]
        mx[...] = jnp.full(mx.shape, 2 * NEG, F32)

        def score(j, c):
            @pl.when(meets(lo_ref, hi_ref, i, j))
            def _():
                ks = pl.ds(pl.multiple_of(j * BQ, BQ), BQ)
                kb = k_ref[ks, :]
                same = segc_ref[ks, :] == seg_q
                for h in range(heads):
                    s = jnp.where(same, nt(kb, qm[h, qs, :]), NEG)
                    st[h, ks, :] = s
                    mx[h : h + 1, :] = jnp.maximum(
                        mx[h : h + 1, :], jnp.max(s, 0, keepdims=True)
                    )

            return c

        lax.fori_loop(0, blocks, score, 0)
        o_ref[qs, :] = jnp.zeros((BQ, q_ref.shape[1]), F32)
        lse_ref[:, qs] = jnp.zeros((lse_ref.shape[0], BQ), F32)

        def mix(j, c):
            @pl.when(meets(lo_ref, hi_ref, i, j))
            def _():
                ks = pl.ds(pl.multiple_of(j * BQ, BQ), BQ)
                acc = None
                for h in range(heads):
                    p = jnp.exp(st[h, ks, :] - mx[h : h + 1, :])
                    lse_ref[h : h + 1, qs] += jnp.sum(p, 0, keepdims=True)
                    part = tn(p.astype(BF), vm[h, ks, :])
                    acc = part if acc is None else acc + part
                o_ref[qs, :] += acc

            return c

        lax.fori_loop(0, blocks, mix, 0)
        total = lse_ref[:, qs]
        scale = jnp.zeros((BQ, q_ref.shape[1]), F32)
        inverse = jnp.transpose(jnp.where(total > 0, 1.0 / total, 0.0))
        for h in range(heads):
            scale = jnp.where(head_mask(h, q_ref.shape[1]), inverse[:, h : h + 1], scale)
        o_ref[qs, :] = o_ref[qs, :] * scale
        lse_ref[0:heads, qs] = mx[0:heads, :] + jnp.log(total[0:heads, :])
        return carry

    lax.fori_loop(0, blocks, per_query, 0)


def attend_back_kernel(
    heads,
    lo_ref,
    hi_ref,
    q_ref,
    k_ref,
    v_ref,
    do_ref,
    o_ref,
    lse_ref,
    segr_ref,
    segc_ref,
    dq_ref,
    dk_ref,
    dv_ref,
    qm,
    km,
    dm,
    delta,
    aq,
    ak,
    av,
):
    rows = q_ref.shape[0]
    blocks = rows // BQ
    for h in range(heads):
        qm[h] = only_head(q_ref[...] * jnp.asarray(0.125, BF), h)
        km[h] = only_head(k_ref[...], h)
        dm[h] = only_head(do_ref[...], h)
    ak[...] = jnp.zeros_like(ak)
    av[...] = jnp.zeros_like(av)

    def per_query(i, carry):
        qs = pl.ds(pl.multiple_of(i * BQ, BQ), BQ)
        seg_q = segr_ref[:, qs]
        prod = jnp.transpose(do_ref[qs, :].astype(F32) * o_ref[qs, :])
        for h in range(heads):
            delta[h : h + 1, :] = jnp.sum(prod[h * DH : (h + 1) * DH, :], 0, keepdims=True)
        aq[...] = jnp.zeros_like(aq)

        def per_key(j, c):
            @pl.when(meets(lo_ref, hi_ref, i, j))
            def _():
                ks = pl.ds(pl.multiple_of(j * BQ, BQ), BQ)
                kb = k_ref[ks, :]
                vb = v_ref[ks, :]
                same = segc_ref[ks, :] == seg_q
                dq = dk = dv = None
                for h in range(heads):
                    qh = qm[h, qs, :]
                    dh = dm[h, qs, :]
                    s = jnp.where(same, nt(kb, qh), NEG)
                    p = jnp.exp(s - lse_ref[h : h + 1, qs])
                    ds = (p * (nt(vb, dh) - delta[h : h + 1, :])).astype(BF)
                    pv = nn(p.astype(BF), dh)
                    pk = nn(ds, qh)
                    pq = tn(ds, km[h, ks, :])
                    dq = pq if dq is None else dq + pq
                    dk = pk if dk is None else dk + pk
                    dv = pv if dv is None else dv + pv
                aq[...] += dq
                ak[ks, :] += dk
                av[ks, :] += dv

            return c

        lax.fori_loop(0, blocks, per_key, 0)
        dq_ref[qs, :] = (aq[...] * 0.125).astype(BF)
        return carry

    lax.fori_loop(0, blocks, per_query, 0)
    dk_ref[...] = ak[...].astype(BF)
    dv_ref[...] = av[...].astype(BF)


def attend(lo, hi, q, k, v, seg):
    rows, cols = q.shape
    heads = cols // DH
    vmem = pl.BlockSpec(memory_space=pltpu.VMEM)
    smem = pl.BlockSpec(memory_space=pltpu.SMEM)
    return pl.pallas_call(
        partial(attend_kernel, heads),
        out_shape=(
            jax.ShapeDtypeStruct((rows, cols), F32),
            jax.ShapeDtypeStruct((8, rows), F32),
        ),
        in_specs=[smem, smem] + [vmem] * 5,
        out_specs=(vmem, vmem),
        scratch_shapes=[
            pltpu.VMEM((heads, rows, cols), BF),
            pltpu.VMEM((heads, rows, cols), BF),
            pltpu.VMEM((heads, rows, BQ), F32),
            pltpu.VMEM((8, BQ), F32),
        ],
        compiler_params=pltpu.CompilerParams(vmem_limit_bytes=40 << 20),
        cost_estimate=pl.CostEstimate(
            flops=2 * rows * rows * cols, transcendentals=rows * rows, bytes_accessed=4 << 20
        ),
        name="attend",
    )(lo, hi, q, k, v, seg.reshape(1, rows), seg.reshape(rows, 1))


def attend_back(lo, hi, q, k, v, do, o, lse, seg):
    rows, cols = q.shape
    heads = cols // DH
    vmem = pl.BlockSpec(memory_space=pltpu.VMEM)
    smem = pl.BlockSpec(memory_space=pltpu.SMEM)
    out = jax.ShapeDtypeStruct((rows, cols), BF)
    return pl.pallas_call(
        partial(attend_back_kernel, heads),
        out_shape=(out, out, out),
        in_specs=[smem, smem] + [vmem] * 8,
        out_specs=(vmem, vmem, vmem),
        scratch_shapes=[
            pltpu.VMEM((heads, rows, cols), BF),
            pltpu.VMEM((heads, rows, cols), BF),
            pltpu.VMEM((heads, rows, cols), BF),
            pltpu.VMEM((8, BQ), F32),
            pltpu.VMEM((BQ, cols), F32),
            pltpu.VMEM((rows, cols), F32),
            pltpu.VMEM((rows, cols), F32),
        ],
        compiler_params=pltpu.CompilerParams(vmem_limit_bytes=40 << 20),
        cost_estimate=pl.CostEstimate(
            flops=5 * rows * rows * cols, transcendentals=rows * rows, bytes_accessed=6 << 20
        ),
        name="attend_back",
    )(lo, hi, q, k, v, do, o, lse, seg.reshape(1, rows), seg.reshape(rows, 1))


def norm(values):
    mean = jnp.mean(values, -1, keepdims=True)
    centred = values - mean
    variance = jnp.mean(centred * centred, -1, keepdims=True)
    rstd = lax.rsqrt(variance + EPS)
    return centred * rstd, rstd


def norm_back(grad, normal, rstd, gain):
    scaled = grad * gain
    return rstd * (
        scaled
        - jnp.mean(scaled, -1, keepdims=True)
        - normal * jnp.mean(scaled * normal, -1, keepdims=True)
    )


def per_device(
    inputs,
    segments,
    ln1_gain,
    ln1_bias,
    query_key_value_weight,
    b_qv,
    output_weight,
    output_bias,
    ln2_gain,
    ln2_bias,
    up_weight,
    up_bias,
    down_weight,
    down_bias,
    out_grad,
):
    z = lax.axis_index("tp")
    ctx = lax.axis_index("ctx")
    planes = lax.axis_size("tp")
    thin = inputs.shape[1]
    width = inputs.shape[2]
    ds = query_key_value_weight.shape[0]
    cols = query_key_value_weight.shape[2]
    hidden_cols = up_weight.shape[1]

    two = lax.axis_size("fsdp") == 2
    flip = (lax.axis_index("fsdp") == 1) if two else None

    def turn(a):
        if not two:
            return a
        half = a.shape[-1] // 2
        return jnp.where(flip, jnp.concatenate([a[..., half:], a[..., :half]], -1), a)

    vectors = turn(jnp.stack([ln1_gain, ln1_bias, output_bias, ln2_gain, ln2_bias, down_bias]))
    ln1_gain, ln1_bias, output_bias, ln2_gain, ln2_bias, down_bias = (
        vectors[i : i + 1] for i in range(6)
    )

    x_own = rows_over_z(turn(inputs), z)
    x_full = gather_ctx(x_own)
    w_attn = gather_weight(
        jnp.concatenate(
            [query_key_value_weight.reshape(ds, 3 * cols), jnp.transpose(output_weight)], 1
        ),
        z,
    )
    w_qkv, w_out_t = w_attn[:, : 3 * cols], w_attn[:, 3 * cols :]
    biases = lax.ppermute(
        jnp.concatenate([b_qv[0], b_qv[1], up_bias]), ("ctx", "tp"), turn_pairs(planes, 0)
    )
    b_q, b_v, b_up = biases[:cols], biases[cols : 2 * cols], biases[2 * cols :]
    g_own = rows_over_z(turn(out_grad), z)
    g_full = gather_ctx(g_own)
    w_mlp = gather_weight(jnp.concatenate([up_weight, jnp.transpose(down_weight)], 1), z)
    w_up, w_down_t = w_mlp[:, :hidden_cols], w_mlp[:, hidden_cols:]

    every = lax.all_gather(segments, ("ctx", "tp"), axis=1, tiled=True)
    labels = lax.dynamic_index_in_dim(every, z, 0, keepdims=False).reshape(-1, thin)
    order = jnp.stack(
        [(ctx ^ c) * planes + (z ^ k) for c in (0, 2, 1, 3) for k in range(planes)]
    )
    seg = jnp.take(labels, order, axis=0).reshape(-1)
    rows = seg.shape[0]
    grouped = seg.reshape(-1, BQ)
    lo, hi = jnp.min(grouped, 1), jnp.max(grouped, 1)
    keep = (seg > 0).reshape(rows, 1)

    x32 = x_full.astype(F32)
    normal_one, rstd_one = norm(x32)
    xa = (normal_one * ln1_gain + ln1_bias).astype(BF)
    mixed = jnp.dot(xa, w_qkv, preferred_element_type=F32)
    query = (mixed[:, :cols] + b_q).astype(BF)
    keyset = mixed[:, cols : 2 * cols].astype(BF)
    values = (mixed[:, 2 * cols :] + b_v).astype(BF)
    mixed_out, lse = attend(lo, hi, query, keyset, values, seg)
    attended = jnp.where(keep, mixed_out, 0.0).astype(BF)
    branch = sum_pair(nt(attended, w_out_t))
    n_own = x_own.shape[0]
    x_pair = x32[: 2 * n_own]
    middle = x_pair + branch + output_bias
    normal_two, rstd_two = norm(middle)
    xb_pair = (normal_two * ln2_gain + ln2_bias).astype(BF)
    xb = jnp.concatenate([xb_pair, xor_swap(xb_pair, "ctx", 1)], 0)
    pre = jnp.dot(xb, w_up, preferred_element_type=F32) + b_up
    hidden, gelu_pull = jax.vjp(partial(jax.nn.gelu, approximate=False), pre)
    hidden_low = hidden.astype(BF)

    dhidden = jnp.dot(g_full, w_down_t, preferred_element_type=F32)
    dpre = gelu_pull(dhidden)[0].astype(BF)
    dxb = sum_pair(nt(dpre, w_up))
    g_pair = g_full[: 2 * n_own].astype(F32)
    dmid = g_pair + norm_back(dxb, normal_two, rstd_two, ln2_gain)
    db_pair = dmid.astype(BF)
    dbranch = jnp.concatenate([db_pair, xor_swap(db_pair, "ctx", 1)], 0)

    mlp = sum_own(nt(hidden_low, w_down_t))
    output = rows_back_over_z((middle[:n_own] + mlp + down_bias).astype(BF), z)
    g_mlp = scatter_weight(
        jnp.concatenate([tn(xb, dpre), tn(g_full, hidden_low)], 1), z
    )
    grad_up = g_mlp[:, :hidden_cols]
    grad_down = jnp.transpose(g_mlp[:, hidden_cols:])

    dattended = jnp.where(keep, nn(dbranch, w_out_t), 0.0).astype(BF)
    dquery, dkey, dvalue = attend_back(
        lo, hi, query, keyset, values, dattended, mixed_out, lse, seg
    )
    dmixed = jnp.concatenate([dquery, dkey, dvalue], 1)
    dxa_part = nt(dmixed, w_qkv)
    dxa = sum_own(dxa_part)
    back_one = norm_back(dxa, normal_one[:n_own], rstd_one[:n_own], ln1_gain)
    input_grad = rows_back_over_z((dmid[:n_own] + back_one).astype(BF), z).astype(F32)
    g_attn = scatter_weight(jnp.concatenate([tn(xa, dmixed), tn(dbranch, attended)], 1), z)
    grad_qkv = g_attn[:, : 3 * cols].reshape(ds, 3, cols)
    grad_out = jnp.transpose(g_attn[:, 3 * cols :])

    def over_rows(a):
        return jnp.sum(a, 0)

    shared = turn(
        jnp.stack(
            [
                over_rows(dxa_part * normal_one),
                over_rows(dxa_part),
                over_rows(db_pair.astype(F32)) * 0.5,
                over_rows(dxb * normal_two) * 0.5,
                over_rows(dxb) * 0.5,
                over_rows(g_own.astype(F32)),
            ]
        )
    ).reshape(-1)
    local = jnp.concatenate(
        [
            over_rows(dquery.astype(F32)),
            over_rows(dvalue.astype(F32)),
            over_rows(dpre.astype(F32)),
        ]
    )
    placed = lax.dynamic_update_slice(
        jnp.zeros((planes, local.shape[0]), F32), local[None], (ctx, 0)
    )
    sums = butterfly_sum(jnp.concatenate([shared, placed.reshape(-1)]).reshape(-1, width))
    sums = sums.reshape(-1)
    head = sums[: 6 * width].reshape(6, width)
    mine = lax.dynamic_index_in_dim(sums[6 * width :].reshape(planes, -1), z, 0, keepdims=False)
    grad_b_qv = mine[: 2 * cols].reshape(2, cols)
    grad_b_up = mine[2 * cols :]

    output, input_grad = turn(output), turn(input_grad)
    return (
        output,
        input_grad,
        head[0],
        head[1],
        grad_qkv,
        grad_b_qv,
        grad_out,
        head[2],
        head[3],
        head[4],
        grad_up,
        grad_b_up,
        grad_down,
        head[5],
    )


def solution(mesh):
    in_specs = (
        P("fsdp", ("ctx", "tp"), None),
        P("fsdp", ("ctx", "tp")),
        P(),
        P(),
        P(("fsdp", "ctx"), None, "tp"),
        P(None, "tp"),
        P("tp", ("fsdp", "ctx")),
        P(),
        P(),
        P(),
        P(("fsdp", "ctx"), "tp"),
        P("tp"),
        P("tp", ("fsdp", "ctx")),
        P(),
        P("fsdp", ("ctx", "tp"), None),
    )
    out_specs = (
        P("fsdp", ("ctx", "tp"), None),
        P("fsdp", ("ctx", "tp"), None),
        P(),
        P(),
        P(("fsdp", "ctx"), None, "tp"),
        P(None, "tp"),
        P("tp", ("fsdp", "ctx")),
        P(),
        P(),
        P(),
        P(("fsdp", "ctx"), "tp"),
        P("tp"),
        P("tp", ("fsdp", "ctx")),
        P(),
    )
    return jax.shard_map(
        per_device, mesh=mesh, in_specs=in_specs, out_specs=out_specs, check_vma=False
    )
```

```python
from functools import partial

import jax
import jax.numpy as jnp
from jax import lax
from jax.experimental import pallas as pl
from jax.experimental.pallas import tpu as pltpu
from jax.sharding import PartitionSpec as P

DH = 64
EPS = 1e-06
BF = jnp.bfloat16
F32 = jnp.float32
NEG = -1e30
SPARE = 8
VMEM = pl.BlockSpec(memory_space=pltpu.VMEM)
SMEM = pl.BlockSpec(memory_space=pltpu.SMEM)


def after(x, *deps):
    return lax.optimization_barrier((x,) + deps)[0]


def xor_swap(x, axis, k):
    n = lax.axis_size(axis)
    return lax.ppermute(x, axis, [(i, i ^ k) for i in range(n)])


def turn_pairs(n, k):
    return [(a * n + b, b * n + (a ^ k)) for a in range(n) for b in range(n)]


def send_turned(x, k):
    return lax.ppermute(x, ("ctx", "tp"), turn_pairs(lax.axis_size("tp"), k))


def send_back(x, k):
    pairs = turn_pairs(lax.axis_size("tp"), k)
    return lax.ppermute(x, ("ctx", "tp"), [(d, s) for s, d in pairs])


def hop_pairs(n, k):
    pairs = []
    for a in range(n):
        for q in range(n):
            f, low = (q ^ k) // 2, (q ^ k) % 2
            pairs.append((a * n + q, ((a // 2) * 2 + low) * n + (a ^ (2 * f))))
    return pairs


def scatter_blocks(pieces):
    n = lax.axis_size("tp")
    y, q = lax.axis_index("ctx") // 2, lax.axis_index("tp")
    split = pieces.reshape((2, 2) + pieces.shape[1:])
    got = xor_swap(pick(split, y ^ 1), "ctx", 2)
    four = jnp.concatenate([pick(split, y), got], 0)
    return [lax.ppermute(pick(four, q ^ k), ("ctx", "tp"), hop_pairs(n, k)) for k in range(n)]


def rows_over_z(arr):
    return lax.all_to_all(arr, "tp", 0, 0, tiled=True)


def place(pieces, first):
    out = jnp.zeros((len(pieces),) + pieces[0].shape, pieces[0].dtype)
    for k, piece in enumerate(pieces):
        out = lax.dynamic_update_index_in_dim(out, piece, first ^ k, 0)
    return out


def pick(arr, index):
    return lax.dynamic_index_in_dim(arr, index, 0, keepdims=False)


def gather_ctx(own):
    half = jnp.concatenate([own, xor_swap(own, "ctx", 2)], 0)
    return half, xor_swap(half, "ctx", 1)


def weight_over_x(rows):
    if lax.axis_size("fsdp") == 2:
        got = xor_swap(rows, "fsdp", 1)
        first = lax.axis_index("fsdp") == 0
        return jnp.where(first, rows, got), jnp.where(first, got, rows)
    every = lax.all_gather(rows, "fsdp", axis=0, tiled=True)
    n = every.shape[0] // 2
    return every[:n], every[n:]


def nt(a, b):
    return lax.dot_general(a, b, (((1,), (1,)), ((), ())), preferred_element_type=F32)


def nn(a, b):
    return lax.dot_general(a, b, (((1,), (0,)), ((), ())), preferred_element_type=F32)


def tn(a, b):
    return lax.dot_general(a, b, (((0,), (0,)), ((), ())), preferred_element_type=F32)


def params(limit, steps=None):
    return pltpu.CompilerParams(vmem_limit_bytes=limit << 20)


def cost(micros, nbytes):
    return pl.CostEstimate(
        flops=micros * 1000 * 1000 * 1000, transcendentals=0, bytes_accessed=nbytes
    )


def normed(x):
    n = x.shape[-1]
    centred = x - jnp.sum(x, -1, keepdims=True) * (1.0 / n)
    rstd = lax.rsqrt(jnp.sum(centred * centred, -1, keepdims=True) * (1.0 / n) + EPS)
    return centred * rstd, rstd


def normed_back(grad, normal, rstd, gain):
    n = grad.shape[-1]
    scaled = grad * gain
    one = jnp.sum(scaled, -1, keepdims=True) * (1.0 / n)
    two = jnp.sum(scaled * normal, -1, keepdims=True) * (1.0 / n)
    return rstd * (scaled - one - normal * two)


def bias_row(ref, row):
    parts = ref[row : row + 3, :].astype(F32)
    return parts[0:1] + parts[1:2] + parts[2:3]


def qkv_kernel(
    cols,
    xo_ref,
    xp_ref,
    vec_ref,
    b_ref,
    wo_ref,
    wp_ref,
    xa_ref,
    q_ref,
    k_ref,
    v_ref,
    seg_ref,
    lo_ref,
    hi_ref,
):
    first, pieces = xo_ref.shape[0], xo_ref.shape[1]
    thin, width = xa_ref.shape[2], xa_ref.shape[3]
    half = width // 2
    b = bias_row(b_ref, 0)
    for i in range(2 * first):
        x_ref = xo_ref if i < first else xp_ref
        normal, _ = normed(x_rows(x_ref, i % first, thin).astype(F32))
        xa = (normal * vec_ref[0:1, :] + vec_ref[1:2, :]).astype(BF)
        put_rows(xa_ref, i, xa)
        mixed = nn(xa[:, :half], wo_ref[:, : 3 * cols]) + nn(xa[:, half:], wp_ref[:, : 3 * cols])
        put_rows(q_ref, i, mixed[:, :cols] + b[:, :cols])
        put_rows(k_ref, i, mixed[:, cols : 2 * cols])
        put_rows(v_ref, i, mixed[:, 2 * cols :] + b[:, cols : 2 * cols])
        labels = [
            x_ref[i % first, k, thin : thin + SPARE, :thin].astype(F32)[0:1, :]
            for k in range(pieces)
        ]
        labels = jnp.concatenate(labels, 1)
        seg_ref[:, i * pieces * thin : (i + 1) * pieces * thin] = jnp.broadcast_to(
            labels, (8, pieces * thin)
        )
        lo_ref[i] = jnp.min(labels).astype(jnp.int32)
        hi_ref[i] = jnp.max(labels).astype(jnp.int32)


def qkv(xo, xp, vec, b, wo, wp, cols, thin):
    first, pieces, _, width = xo.shape
    shape = lambda c: jax.ShapeDtypeStruct((2 * first, pieces, thin, c), BF)
    bound = jax.ShapeDtypeStruct((2 * first,), jnp.int32)
    return pl.pallas_call(
        partial(qkv_kernel, cols),
        out_shape=(
            shape(width),
            shape(cols),
            shape(cols),
            shape(cols),
            jax.ShapeDtypeStruct((8, 2 * first * pieces * thin), F32),
            bound,
            bound,
        ),
        in_specs=[VMEM] * 6,
        out_specs=(VMEM,) * 5 + (SMEM,) * 2,
        compiler_params=params(12),
        cost_estimate=cost(4, 6 << 20),
        name="qkv",
    )(xo, xp, vec, b, wo, wp)


def head_mask(h, width):
    lane = lax.broadcasted_iota(jnp.int32, (1, width), 1)
    return (lane >= h * DH) & (lane < (h + 1) * DH)


def only_head(x, h):
    return jnp.where(head_mask(h, x.shape[1]), x, jnp.zeros_like(x))


def x_rows(ref, i, thin):
    return ref[i, :, :thin, :].reshape(-1, ref.shape[3])


def g_rows(ref, i, thin):
    return ref[i, :, thin + SPARE :, :].reshape(-1, ref.shape[3])


def meets(lo_ref, hi_ref, i, j):
    return (hi_ref[i] >= lo_ref[j]) & (lo_ref[i] <= hi_ref[j])


def group(ref, i):
    return ref[i].reshape(ref.shape[1] * ref.shape[2], ref.shape[3])


def put_rows(ref, i, value):
    ref[i] = value.astype(ref.dtype).reshape(ref.shape[1:])


def put_half(kept_ref, sent_ref, i, lanes, value):
    n = kept_ref.shape[0]

    @pl.when(i < n)
    def _():
        kept_ref[jnp.minimum(i, n - 1), :, :, lanes] = value.reshape(kept_ref.shape[1:3] + (-1,))

    @pl.when(i >= n)
    def _():
        sent_ref[jnp.maximum(i - n, 0), :, :, lanes] = value.astype(sent_ref.dtype).reshape(
            sent_ref.shape[1:3] + (-1,)
        )


def attend_kernel(
    heads,
    lo_ref,
    hi_ref,
    q_ref,
    k_ref,
    v_ref,
    segr_ref,
    wo_ref,
    wp_ref,
    att_ref,
    lse_ref,
    kept_ref,
    sent_ref,
    qm,
    kk,
    vm,
    st,
    mx,
    acc_ref,
    ow,
    segc_ref,
):
    groups = q_ref.shape[0]
    n = q_ref.shape[1] * q_ref.shape[2]
    cols = q_ref.shape[3]
    half = wo_ref.shape[0]
    segc_ref[...] = jnp.transpose(segr_ref[...])
    ow[0] = wo_ref[:, 3 * cols :]
    ow[1] = wp_ref[:, 3 * cols :]
    for i in range(groups):
        rows = slice(i * n, (i + 1) * n)
        kk[rows, :] = group(k_ref, i)
        for h in range(heads):
            qm[h, rows, :] = only_head(group(q_ref, i) * jnp.asarray(0.125, BF), h)
            vm[h, rows, :] = only_head(group(v_ref, i), h)

    def per_query(i, carry):
        qs = pl.ds(pl.multiple_of(i * n, n), n)
        seg_q = segr_ref[0:1, qs]
        mx[...] = jnp.full(mx.shape, 2 * NEG, F32)

        def score(j, c):
            @pl.when(meets(lo_ref, hi_ref, i, j))
            def _():
                ks = pl.ds(pl.multiple_of(j * n, n), n)
                kb = kk[ks, :]
                same = segc_ref[ks, 0:1] == seg_q
                for h in range(heads):
                    s = jnp.where(same, nt(kb, qm[h, qs, :]), NEG)
                    st[h, ks, :] = s
                    mx[h : h + 1, :] = jnp.maximum(
                        mx[h : h + 1, :], jnp.max(s, 0, keepdims=True)
                    )

            return c

        lax.fori_loop(0, groups, score, 0)
        acc_ref[...] = jnp.zeros_like(acc_ref)
        lse_ref[:, qs] = jnp.zeros((lse_ref.shape[0], n), F32)

        def mix(j, c):
            @pl.when(meets(lo_ref, hi_ref, i, j))
            def _():
                ks = pl.ds(pl.multiple_of(j * n, n), n)
                acc = None
                for h in range(heads):
                    p = jnp.exp(st[h, ks, :] - mx[h : h + 1, :])
                    lse_ref[h : h + 1, qs] += jnp.sum(p, 0, keepdims=True)
                    part = tn(p.astype(BF), vm[h, ks, :])
                    acc = part if acc is None else acc + part
                acc_ref[...] += acc

            return c

        lax.fori_loop(0, groups, mix, 0)
        total = lse_ref[:, qs]
        scale = jnp.zeros((n, cols), F32)
        inverse = jnp.transpose(jnp.where(total > 0, 1.0 / total, 0.0))
        for h in range(heads):
            scale = jnp.where(head_mask(h, cols), inverse[:, h : h + 1], scale)
        keep = segc_ref[qs, 0:1] > 0
        att = jnp.where(keep, acc_ref[...] * scale, 0.0).astype(BF)
        lse_ref[0:heads, qs] = mx[0:heads, :] + jnp.log(total[0:heads, :])
        put_rows(att_ref, i, att)
        for part in range(2):
            lanes = slice(part * half, (part + 1) * half)
            put_half(kept_ref, sent_ref, i, lanes, nt(att, ow[part]))
        return carry

    lax.fori_loop(0, groups, per_query, 0)


def attend(lo, hi, q, k, v, segr, wo, wp):
    groups, pieces, thin, cols = q.shape
    heads = cols // DH
    n, rows = pieces * thin, groups * pieces * thin
    width = 2 * wo.shape[0]
    return pl.pallas_call(
        partial(attend_kernel, heads),
        out_shape=(
            jax.ShapeDtypeStruct(q.shape, BF),
            jax.ShapeDtypeStruct((8, rows), F32),
            jax.ShapeDtypeStruct((groups // 2, pieces, thin, width), F32),
            jax.ShapeDtypeStruct((groups // 2, pieces, thin, width), BF),
        ),
        in_specs=[SMEM, SMEM] + [VMEM] * 6,
        out_specs=(VMEM,) * 4,
        scratch_shapes=[
            pltpu.VMEM((heads, rows, cols), BF),
            pltpu.VMEM((rows, cols), BF),
            pltpu.VMEM((heads, rows, cols), BF),
            pltpu.VMEM((heads, rows, n), F32),
            pltpu.VMEM((8, n), F32),
            pltpu.VMEM((n, cols), F32),
            pltpu.VMEM((2, width // 2, cols), BF),
            pltpu.VMEM((rows, 8), F32),
        ],
        compiler_params=params(20),
        cost_estimate=cost(11, 8 << 20),
        name="attend",
    )(lo, hi, q, k, v, segr, wo, wp)


def attend_back_kernel(
    heads,
    lo_ref,
    hi_ref,
    q_ref,
    k_ref,
    v_ref,
    att_ref,
    lse_ref,
    db_ref,
    dp_ref,
    segr_ref,
    wo_ref,
    wp_ref,
    dq_ref,
    dk_ref,
    dv_ref,
    kept_ref,
    sent_ref,
    qm,
    km,
    kk,
    vv,
    dm,
    delta,
    aq,
    ak,
    av,
    ow,
    kw,
    segc_ref,
):
    groups = q_ref.shape[0]
    n = q_ref.shape[1] * q_ref.shape[2]
    cols = q_ref.shape[3]
    half = wo_ref.shape[0]
    segc_ref[...] = jnp.transpose(segr_ref[...])
    ow[0] = wo_ref[:, 3 * cols :]
    ow[1] = wp_ref[:, 3 * cols :]
    kw[0] = wo_ref[:, cols : 2 * cols]
    kw[1] = wp_ref[:, cols : 2 * cols]
    ak[...] = jnp.zeros_like(ak)
    av[...] = jnp.zeros_like(av)
    for i in range(groups):
        rows = slice(i * n, (i + 1) * n)
        kk[rows, :] = group(k_ref, i)
        vv[rows, :] = group(v_ref, i)
        grad = group(db_ref, i) if i < groups // 2 else group(dp_ref, i - groups // 2)
        out_back = nn(grad[:, :half], ow[0]) + nn(grad[:, half:], ow[1])
        do = jnp.where(segc_ref[rows, 0:1] > 0, out_back, 0.0).astype(BF)
        prod = jnp.transpose(do.astype(F32) * group(att_ref, i).astype(F32))
        for h in range(heads):
            delta[h : h + 1, rows] = jnp.sum(prod[h * DH : (h + 1) * DH, :], 0, keepdims=True)
            qm[h, rows, :] = only_head(group(q_ref, i) * jnp.asarray(0.125, BF), h)
            km[h, rows, :] = only_head(group(k_ref, i), h)
            dm[h, rows, :] = only_head(do, h)

    def per_query(i, carry):
        qs = pl.ds(pl.multiple_of(i * n, n), n)
        seg_q = segr_ref[0:1, qs]
        aq[...] = jnp.zeros_like(aq)

        def per_key(j, c):
            @pl.when(meets(lo_ref, hi_ref, i, j))
            def _():
                ks = pl.ds(pl.multiple_of(j * n, n), n)
                kb = kk[ks, :]
                vb = vv[ks, :]
                same = segc_ref[ks, 0:1] == seg_q
                dq = dk = dv = None
                for h in range(heads):
                    qh = qm[h, qs, :]
                    dh = dm[h, qs, :]
                    s = jnp.where(same, nt(kb, qh), NEG)
                    p = jnp.exp(s - lse_ref[h : h + 1, qs])
                    ds = (p * (nt(vb, dh) - delta[h : h + 1, qs])).astype(BF)
                    pv = nn(p.astype(BF), dh)
                    pk = nn(ds, qh)
                    pq = tn(ds, km[h, ks, :])
                    dq = pq if dq is None else dq + pq
                    dk = pk if dk is None else dk + pk
                    dv = pv if dv is None else dv + pv
                aq[...] += dq
                ak[ks, :] += dk
                av[ks, :] += dv

            return c

        lax.fori_loop(0, groups, per_key, 0)
        put_rows(dq_ref, i, aq[...] * 0.125)
        return carry

    lax.fori_loop(0, groups, per_query, 0)

    def finish(i, carry):
        qs = pl.ds(pl.multiple_of(i * n, n), n)
        dq = group(dq_ref, i)
        dk = ak[qs, :].astype(BF)
        dv = av[qs, :].astype(BF)
        put_rows(dk_ref, i, dk)
        put_rows(dv_ref, i, dv)
        for part, w in enumerate((wo_ref, wp_ref)):
            lanes = slice(part * half, (part + 1) * half)
            dx = nt(dq, w[:, :cols]) + nt(dk, kw[part]) + nt(dv, w[:, 2 * cols : 3 * cols])
            put_half(kept_ref, sent_ref, i, lanes, dx)
        return carry

    lax.fori_loop(0, groups, finish, 0)


def attend_back(lo, hi, q, k, v, att, lse, db, dp, segr, wo, wp):
    groups, pieces, thin, cols = q.shape
    heads = cols // DH
    n, rows = pieces * thin, groups * pieces * thin
    width = 2 * wo.shape[0]
    out = jax.ShapeDtypeStruct(q.shape, BF)
    per_head = pltpu.VMEM((heads, rows, cols), BF)
    return pl.pallas_call(
        partial(attend_back_kernel, heads),
        out_shape=(
            out,
            out,
            out,
            jax.ShapeDtypeStruct((groups // 2, pieces, thin, width), F32),
            jax.ShapeDtypeStruct((groups // 2, pieces, thin, width), BF),
        ),
        in_specs=[SMEM, SMEM] + [VMEM] * 10,
        out_specs=(VMEM,) * 5,
        scratch_shapes=[
            per_head,
            per_head,
            pltpu.VMEM((rows, cols), BF),
            pltpu.VMEM((rows, cols), BF),
            per_head,
            pltpu.VMEM((8, rows), F32),
            pltpu.VMEM((n, cols), F32),
            pltpu.VMEM((rows, cols), F32),
            pltpu.VMEM((rows, cols), F32),
            pltpu.VMEM((2, width // 2, cols), BF),
            pltpu.VMEM((2, width // 2, cols), BF),
            pltpu.VMEM((rows, 8), F32),
        ],
        compiler_params=params(28),
        cost_estimate=cost(18, 12 << 20),
        name="attend_back",
    )(lo, hi, q, k, v, att, lse, db, dp, segr, wo, wp)


def middle_kernel(s_ref, got_ref, x_ref, vec_ref, mid_ref, xb_ref):
    n, _, thin, width = s_ref.shape
    for i in range(n):
        x = x_rows(x_ref, i, thin).astype(F32)
        mid = group(s_ref, i) + group(got_ref, n - 1 - i).astype(F32) + x + vec_ref[0:1, :]
        put_rows(mid_ref, i, mid)
        normal, _ = normed(mid)
        put_rows(xb_ref, i, normal * vec_ref[1:2, :] + vec_ref[2:3, :])


def middle_rows(s, got, x, vec):
    return pl.pallas_call(
        middle_kernel,
        out_shape=(jax.ShapeDtypeStruct(s.shape, F32), jax.ShapeDtypeStruct(s.shape, BF)),
        in_specs=[VMEM] * 4,
        out_specs=(VMEM,) * 2,
        compiler_params=params(8),
        cost_estimate=cost(2, 4 << 20),
        name="middle_rows",
    )(s, got, x, vec)


def middle_back_kernel(s_ref, got_ref, mid_ref, g_ref, vec_ref, dmid_ref, db_ref, sum_ref):
    n, thin = s_ref.shape[0], s_ref.shape[2]
    for i in range(n):
        dxb = group(s_ref, i) + group(got_ref, n - 1 - i).astype(F32)
        normal, rstd = normed(group(mid_ref, i))
        grad = g_rows(g_ref, i, thin).astype(F32)
        dmid = grad + normed_back(dxb, normal, rstd, vec_ref[...])
        low = dmid.astype(BF)
        put_rows(dmid_ref, i, dmid)
        put_rows(db_ref, i, low)
        if i == 0:
            sum_ref[0:1, :] = jnp.sum(low.astype(F32), 0, keepdims=True)
            sum_ref[1:2, :] = jnp.sum(dxb * normal, 0, keepdims=True)
            sum_ref[2:3, :] = jnp.sum(dxb, 0, keepdims=True)
            sum_ref[3:4, :] = jnp.sum(grad, 0, keepdims=True)


def middle_back(s, got, mid, g, vec):
    return pl.pallas_call(
        middle_back_kernel,
        out_shape=(
            jax.ShapeDtypeStruct(s.shape, F32),
            jax.ShapeDtypeStruct(s.shape, BF),
            jax.ShapeDtypeStruct((4, s.shape[-1]), F32),
        ),
        in_specs=[VMEM] * 5,
        out_specs=(VMEM,) * 3,
        compiler_params=params(8),
        cost_estimate=cost(2, 5 << 20),
        name="middle_back",
    )(s, got, mid, g, vec)


def add_kernel(kept_ref, got_ref, sum_ref, low_ref):
    for i in range(kept_ref.shape[0]):
        total = group(kept_ref, i) + group(got_ref, i).astype(F32)
        put_rows(sum_ref, i, total)
        if i >= kept_ref.shape[0] - low_ref.shape[0]:
            put_rows(low_ref, i - (kept_ref.shape[0] - low_ref.shape[0]), total)


def core_sum(kept, sent, low_blocks):
    got = xor_swap(sent, "ctx", 1)
    return pl.pallas_call(
        add_kernel,
        out_shape=(
            jax.ShapeDtypeStruct(kept.shape, F32),
            jax.ShapeDtypeStruct((low_blocks,) + kept.shape[1:], BF),
        ),
        in_specs=[VMEM] * 2,
        out_specs=(VMEM,) * 2,
        compiler_params=params(6),
        cost_estimate=cost(1, 4 << 20),
        name="add_rows",
    )(kept, got)


def first_back_kernel(
    s_ref, got_ref, x_ref, dmid_ref, mid_ref, mlp_ref, mlpgot_ref, vec_ref, out_ref
):
    thin = s_ref.shape[2]
    pieces = out_ref.shape[0]
    result = group(mid_ref, 0) + group(mlp_ref, 0) + group(mlpgot_ref, 0).astype(F32)
    result = result + vec_ref[1:2, :]
    out_ref[:, :thin, :] = result.astype(BF).reshape(pieces, thin, -1)
    dxa = group(s_ref, 0) + group(got_ref, 0).astype(F32)
    normal, rstd = normed(x_rows(x_ref, 0, thin).astype(F32))
    grad = group(dmid_ref, 0) + normed_back(dxa, normal, rstd, vec_ref[0:1, :])
    out_ref[:, thin:, :] = grad.astype(BF).reshape(pieces, thin, -1)


def first_back(s, got, x, dmid, mid, mlp, mlpgot, vec):
    _, pieces, thin, width = s.shape
    return pl.pallas_call(
        first_back_kernel,
        out_shape=jax.ShapeDtypeStruct((pieces, 2 * thin, width), BF),
        in_specs=[VMEM] * 8,
        out_specs=VMEM,
        compiler_params=params(8),
        cost_estimate=cost(1, 6 << 20),
        name="first_back",
    )(s, got, x, dmid, mid, mlp, mlpgot, vec)


def pieces_kernel(own_ref, got_ref, vec_ref, out_ref):
    blocks, r = out_ref.shape[0], out_ref.shape[1] - SPARE
    for b in range(blocks):
        part = slice(b * r, (b + 1) * r)
        out_ref[b, :r, :] = (own_ref[part, :].astype(F32) + got_ref[part, :].astype(F32)).astype(BF)
        last = slice(blocks * r, blocks * r + 2)
        out_ref[b, r : r + 2, :] = (
            own_ref[last, :].astype(F32) + got_ref[last, :].astype(F32)
        ).astype(BF)
        out_ref[b, r + 2 :, :] = vec_ref[...].astype(BF)


def grad_pieces(grad, vec, blocks):
    rows = grad.shape[1] - SPARE
    if lax.axis_size("fsdp") == 2 and rows // blocks % 16 == 0:
        return pl.pallas_call(
            pieces_kernel,
            out_shape=jax.ShapeDtypeStruct((blocks, rows // blocks + SPARE, grad.shape[2]), BF),
            in_specs=[VMEM] * 3,
            out_specs=VMEM,
            compiler_params=params(6),
            cost_estimate=cost(1, 2 << 20),
            name="grad_pieces",
        )(grad[0], xor_swap(grad[1], "fsdp", 1), vec)
    last = lax.psum(grad[0, rows : rows + 2].astype(F32), "fsdp")
    split = grad[:, :rows].reshape(lax.axis_size("fsdp"), -1, grad.shape[2]).astype(F32)
    own = lax.psum_scatter(split, "fsdp", scatter_dimension=0, tiled=False)
    own = own.reshape(blocks, -1, own.shape[-1])
    small = jnp.concatenate([last, vec], 0)
    small = jnp.broadcast_to(small, (blocks,) + small.shape)
    return jnp.concatenate([own, small], 1).astype(BF)


def part_rows(ref, part):
    w = ref[:, part]
    return w.reshape(w.shape[0] * w.shape[1], w.shape[2])


def mlp_kernel(xo_ref, xp_ref, go_ref, gp_ref, m_ref, b_ref, hidden_ref, dpre_ref, kept_ref, sent_ref):
    first, thin = xo_ref.shape[0], xo_ref.shape[2]
    b = bias_row(b_ref, 3)
    for i in range(2 * first):
        own = i < first
        pre = nn(group(xo_ref if own else xp_ref, i % first), part_rows(m_ref, 0)) + b
        dhidden = nn(g_rows(go_ref if own else gp_ref, i % first, thin), part_rows(m_ref, 1))
        share = 0.5 * (1.0 + lax.erf(pre * (0.5**0.5)))
        density = jnp.exp(pre * pre * -0.5) * ((0.5 / 3.141592653589793) ** 0.5)
        n = pre.shape[0]
        hidden_ref[i * n : (i + 1) * n, :] = (pre * share).astype(BF)
        dpre = (dhidden * (share + pre * density)).astype(BF)
        dpre_ref[i * n : (i + 1) * n, :] = dpre
        put_rows(kept_ref if own else sent_ref, i % first, nt(dpre, part_rows(m_ref, 0)))


def mlp_block(xo, xp, go, gp, m, b):
    blocks, pieces, thin, width = xo.shape
    low = jax.ShapeDtypeStruct((2 * blocks * pieces * thin, m.shape[-1]), BF)
    return pl.pallas_call(
        mlp_kernel,
        out_shape=(low, low, jax.ShapeDtypeStruct(xo.shape, F32), jax.ShapeDtypeStruct(xo.shape, BF)),
        in_specs=[VMEM] * 6,
        out_specs=(VMEM,) * 4,
        compiler_params=params(12),
        cost_estimate=cost(7, 12 << 20),
        name="mlp_block",
    )(xo, xp, go, gp, m, b)


def mlp_grads_kernel(
    xo_ref,
    xp_ref,
    dpre_ref,
    go_ref,
    gp_ref,
    hidden_ref,
    m_ref,
    grad_ref,
    kept_ref,
    sent_ref,
    sum_ref,
):
    first, _, thin, width = xo_ref.shape
    half, blocks = width // 2, grad_ref.shape[0] // 2
    rows = dpre_ref.shape[0]
    n = rows // 2
    for i in range(2):
        lanes = slice(i * half, (i + 1) * half)
        where = slice(i * blocks, (i + 1) * blocks)
        xo, xp = (ref[:, :, :, lanes].reshape(n, half) for ref in (xo_ref, xp_ref))
        up = tn(xo, dpre_ref[:n, :]) + tn(xp, dpre_ref[n:, :])
        grad_ref[where, 0] = up.astype(BF).reshape((-1,) + grad_ref.shape[2:])
        go, gp = (ref[:, :, thin + SPARE :, lanes].reshape(n, half) for ref in (go_ref, gp_ref))
        down = tn(go, hidden_ref[:n, :]) + tn(gp, hidden_ref[n:, :])
        grad_ref[where, 1] = down.astype(BF).reshape((-1,) + grad_ref.shape[2:])
    size = n // first
    for i in range(2 * first):
        result = nt(hidden_ref[i * size : (i + 1) * size, :], part_rows(m_ref, 1))
        put_rows(kept_ref if i < first else sent_ref, i % first, result)
    sum_ref[...] = jnp.sum(dpre_ref[...].astype(F32), 0, keepdims=True)


def mlp_grads(xo, xp, dpre, go, gp, hidden, m):
    return pl.pallas_call(
        mlp_grads_kernel,
        out_shape=(
            jax.ShapeDtypeStruct(m.shape, BF),
            jax.ShapeDtypeStruct(xo.shape, F32),
            jax.ShapeDtypeStruct(xo.shape, BF),
            jax.ShapeDtypeStruct((1, dpre.shape[1]), F32),
        ),
        in_specs=[VMEM] * 7,
        out_specs=(VMEM,) * 4,
        compiler_params=params(14),
        cost_estimate=cost(6, 12 << 20),
        name="mlp_grads",
    )(xo, xp, dpre, go, gp, hidden, m)


def attend_grads_kernel(
    flip_ref,
    xa_ref,
    dq_ref,
    dk_ref,
    dv_ref,
    do_ref,
    dp_ref,
    att_ref,
    sum_ref,
    kept_ref,
    sent_ref,
    xo_ref,
    xp_ref,
    out_ref,
    vec_ref,
):
    rows, cols = dq_ref.shape
    half = xa_ref.shape[1] // 2
    n = do_ref.shape[0]
    for i in range(2):
        at = flip_ref[0] ^ i
        lanes = slice(i * half, (i + 1) * half)
        for c, ref in enumerate((dq_ref, dk_ref, dv_ref)):
            out_ref[at, :half, c * cols : (c + 1) * cols] = tn(xa_ref[:, lanes], ref[...]).astype(BF)
        out = tn(do_ref[:, lanes], att_ref[:n, :]) + tn(dp_ref[:, lanes], att_ref[n:, :])
        out_ref[at, :half, 3 * cols : 4 * cols] = out.astype(BF)
        out_ref[at, half : half + SPARE, :] = jnp.zeros((SPARE, out_ref.shape[2]), BF)
        for c, ref in enumerate((dq_ref, dv_ref)):
            total = jnp.sum(ref[...].astype(F32), 0, keepdims=True)
            out_ref[at, half : half + 1, c * cols : (c + 1) * cols] = total.astype(BF)
        out_ref[at, half + 1 : half + 2, : sum_ref.shape[1]] = sum_ref[...].astype(BF)
    first, _, thin, width = kept_ref.shape
    gain = bias = jnp.zeros((1, width), F32)
    for i in range(2 * first):
        x_ref, g_ref = (xo_ref, kept_ref) if i < first else (xp_ref, sent_ref)
        normal, _ = normed(x_rows(x_ref, i % first, thin).astype(F32))
        dx = group(g_ref, i % first).astype(F32)
        gain = gain + jnp.sum(dx * normal, 0, keepdims=True)
        bias = bias + jnp.sum(dx, 0, keepdims=True)
    vec_ref[0:1, :] = gain
    vec_ref[1:2, :] = bias


def attend_grads(flip, xa, dq, dk, dv, do, dp, att, sums, kept, sent, xo, xp):
    width = xa.shape[1]
    shape = (2, width // 2 + SPARE, 4 * dq.shape[1])
    return pl.pallas_call(
        attend_grads_kernel,
        out_shape=(jax.ShapeDtypeStruct(shape, BF), jax.ShapeDtypeStruct((2, width), F32)),
        in_specs=[SMEM] + [VMEM] * 12,
        out_specs=(VMEM, VMEM),
        compiler_params=params(14),
        cost_estimate=cost(6, 12 << 20),
        name="attend_grads",
    )(flip, xa, dq, dk, dv, do, dp, att, sums, kept, sent, xo, xp)


def exact_low(x):
    one = lax.reduce_precision(x, 8, 7)
    two = lax.reduce_precision(x - one, 8, 7)
    return jnp.concatenate([one, two, x - one - two], 0).astype(BF)


def per_device(
    inputs,
    segments,
    ln1_gain,
    ln1_bias,
    query_key_value_weight,
    b_qv,
    output_weight,
    output_bias,
    ln2_gain,
    ln2_bias,
    up_weight,
    up_bias,
    down_weight,
    down_bias,
    out_grad,
):
    z = lax.axis_index("tp")
    ctx = lax.axis_index("ctx")
    planes = lax.axis_size("tp")
    thin, width = inputs.shape[1], inputs.shape[2]
    ds, _, cols = query_key_value_weight.shape
    hidden_cols = up_weight.shape[1]

    vectors = jnp.stack([ln1_gain, ln1_bias, output_bias, ln2_gain, ln2_bias, down_bias])
    rows_of = lambda a: a.reshape(-1, a.shape[-1])

    labels = jnp.pad(segments.astype(BF)[:, None, :], ((0, 0), (0, SPARE - 1), (0, width - thin)))
    own = rows_over_z(jnp.concatenate([inputs, labels, out_grad], 1))
    biases = jnp.pad(b_qv.reshape(1, -1), ((0, 0), (0, width - 2 * cols)))
    biases = [exact_low(biases), exact_low(up_bias.reshape(1, -1)), jnp.zeros((SPARE - 6, width), BF)]
    a_shard = jnp.concatenate(
        [query_key_value_weight.reshape(ds, 3 * cols), jnp.transpose(output_weight)], 1
    )
    a_shard = after(jnp.concatenate([a_shard] + biases, 0), own)
    got = [send_turned(a_shard, k) for k in range(planes)]
    a_rows = place([g[:ds] for g in got], z).reshape(-1, width)
    biases = got[0][ds:]
    a_own, a_peer = weight_over_x(a_rows)
    x_pair, x_far = gather_ctx(own[None])

    m_shard = jnp.concatenate([up_weight, jnp.transpose(down_weight)], 0)
    m_shard = send_turned(after(m_shard, own), 0)
    m_all = lax.all_gather(m_shard, ("fsdp", "tp"), axis=0, tiled=True)
    m_all = m_all.reshape(-1, 2, ds, hidden_cols)
    aligned = ds % 16 == 0 and m_all.shape[0] % 2 == 0
    if not aligned:
        m_all = m_all.reshape(2, -1, 2, ds, hidden_cols).transpose(0, 2, 1, 3, 4)
        m_all = m_all.reshape(2, 2, width // 2, hidden_cols)

    xa, query, keyset, values, segr, lo, hi = qkv(
        x_pair, x_far, vectors, biases, a_own, a_peer, cols, thin
    )
    attended, lse, kept, sent = attend(lo, hi, query, keyset, values, segr, a_own, a_peer)
    s, low = core_sum(kept, sent, kept.shape[0])
    middle, xb_pair = middle_rows(s, xor_swap(low, "ctx", 2), x_pair, vectors[2:5])
    xb_far = xor_swap(xb_pair, "ctx", 1)

    hidden, dpre, kept, sent = mlp_block(xb_pair, xb_far, x_pair, x_far, m_all, biases)
    s, low = core_sum(kept, sent, kept.shape[0])
    m_grad, mlp_kept, mlp_sent, dpre_sum = mlp_grads(
        xb_pair, xb_far, after(dpre, s), x_pair, x_far, hidden, m_all
    )
    dmid, db_pair, sums_two = middle_back(
        s, after(xor_swap(low, "ctx", 2), dpre_sum), middle, x_pair, vectors[3:4]
    )
    db_far = xor_swap(db_pair, "ctx", 1)
    if not aligned:
        m_grad = m_grad.reshape(2, 2, -1, ds, hidden_cols).transpose(0, 2, 1, 3, 4)
    m_grad = m_grad.reshape(-1, hidden_cols)
    m_sums = lax.psum_scatter(m_grad, ("fsdp", "tp"), scatter_dimension=0, tiled=True)
    mlp_s, mlp_low = core_sum(mlp_kept, after(mlp_sent, s), 1)
    mlp_got = xor_swap(after(mlp_low, db_far), "ctx", 2)

    dquery, dkey, dvalue, kept, sent = attend_back(
        lo, hi, query, keyset, values, attended, lse, db_pair, db_far, segr, a_own, a_peer
    )
    s, low = core_sum(kept, sent, 1)
    got = xor_swap(low, "ctx", 2)
    flip = lax.axis_index("fsdp") if lax.axis_size("fsdp") == 2 else 0
    g_attn, sums_one = attend_grads(
        jnp.full((1,), flip, jnp.int32),
        rows_of(xa),
        after(rows_of(dquery), s),
        rows_of(dkey),
        rows_of(dvalue),
        rows_of(db_pair),
        rows_of(db_far),
        rows_of(attended),
        dpre_sum,
        kept,
        sent,
        x_pair,
        x_far,
    )
    shared = jnp.concatenate([sums_one, sums_two], 0)
    shared = shared + xor_swap(shared, "ctx", 1)
    shared = shared + xor_swap(shared, "ctx", 2)
    if lax.axis_size("fsdp") == 2:
        shared = shared + xor_swap(shared, "fsdp", 1)
    else:
        shared = lax.psum(shared, "fsdp")
    a_low = grad_pieces(g_attn, shared, planes)

    vec = jnp.concatenate([vectors[0:1], vectors[5:6]], 0)
    both = first_back(s, got, x_pair, dmid, middle, mlp_s, mlp_got, vec)
    both = rows_over_z(both)
    output, input_grad = both[:, :thin], both[:, thin:].astype(F32)
    got = scatter_blocks(after(a_low, m_sums))

    g_attn = sum(g.astype(F32) for g in got)
    grad_qkv = g_attn[:ds, : 3 * cols].reshape(ds, 3, cols)
    grad_out = jnp.transpose(g_attn[:ds, 3 * cols :])
    mine, shared = g_attn[ds : ds + 2], g_attn[ds + 2 :]
    g_mlp = send_back(after(m_sums, both), 0).astype(F32)
    grad_up, grad_down = g_mlp[:ds], jnp.transpose(g_mlp[ds:])
    return (
        output,
        input_grad,
        shared[0],
        shared[1],
        grad_qkv,
        mine[0, : 2 * cols].reshape(2, cols),
        grad_out,
        shared[2],
        shared[3],
        shared[4],
        grad_up,
        mine[1, :hidden_cols],
        grad_down,
        shared[5],
    )


def solution(mesh):
    in_specs = (
        P("fsdp", ("ctx", "tp"), None),
        P("fsdp", ("ctx", "tp")),
        P(),
        P(),
        P(("fsdp", "ctx"), None, "tp"),
        P(None, "tp"),
        P("tp", ("fsdp", "ctx")),
        P(),
        P(),
        P(),
        P(("fsdp", "ctx"), "tp"),
        P("tp"),
        P("tp", ("fsdp", "ctx")),
        P(),
        P("fsdp", ("ctx", "tp"), None),
    )
    out_specs = (
        P("fsdp", ("ctx", "tp"), None),
        P("fsdp", ("ctx", "tp"), None),
        P(),
        P(),
        P(("fsdp", "ctx"), None, "tp"),
        P(None, "tp"),
        P("tp", ("fsdp", "ctx")),
        P(),
        P(),
        P(),
        P(("fsdp", "ctx"), "tp"),
        P("tp"),
        P("tp", ("fsdp", "ctx")),
        P(),
    )
    return jax.shard_map(
        per_device, mesh=mesh, in_specs=in_specs, out_specs=out_specs, check_vma=False
    )
```

```python
from functools import partial

import jax
import jax.numpy as jnp
from jax import lax
from jax.experimental import pallas as pl
from jax.experimental.pallas import tpu as pltpu
from jax.sharding import PartitionSpec as P

DH = 64
EPS = 1e-06
BF = jnp.bfloat16
F32 = jnp.float32
NEG = -1e30
SPARE = 8
VMEM = pl.BlockSpec(memory_space=pltpu.VMEM)
SMEM = pl.BlockSpec(memory_space=pltpu.SMEM)


def after(x, *deps):
    return lax.optimization_barrier((x,) + deps)[0]


def xor_swap(x, axis, k):
    n = lax.axis_size(axis)
    return lax.ppermute(x, axis, [(i, i ^ k) for i in range(n)])


def turn_pairs(n, k):
    return [(a * n + b, b * n + (a ^ k)) for a in range(n) for b in range(n)]


def send_turned(x, k):
    return lax.ppermute(x, ("ctx", "tp"), turn_pairs(lax.axis_size("tp"), k))


def send_back(x, k):
    pairs = turn_pairs(lax.axis_size("tp"), k)
    return lax.ppermute(x, ("ctx", "tp"), [(d, s) for s, d in pairs])


def hop_pairs(n, k):
    pairs = []
    for a in range(n):
        for q in range(n):
            f, low = (q ^ k) // 2, (q ^ k) % 2
            pairs.append((a * n + q, ((a // 2) * 2 + low) * n + (a ^ (2 * f))))
    return pairs


def scatter_blocks(pieces, *late):
    n = lax.axis_size("tp")
    y, q = lax.axis_index("ctx") // 2, lax.axis_index("tp")
    split = pieces.reshape((2, 2) + pieces.shape[1:])
    got = xor_swap(pick(split, y ^ 1), "ctx", 2)
    four = after(jnp.concatenate([pick(split, y), got], 0), *late)
    return [lax.ppermute(pick(four, q ^ k), ("ctx", "tp"), hop_pairs(n, k)) for k in range(n)]


def rows_over_z(arr):
    return lax.all_to_all(arr, "tp", 0, 0, tiled=True)


def place(pieces, first):
    out = jnp.zeros((len(pieces),) + pieces[0].shape, pieces[0].dtype)
    for k, piece in enumerate(pieces):
        out = lax.dynamic_update_index_in_dim(out, piece, first ^ k, 0)
    return out


def pick(arr, index):
    return lax.dynamic_index_in_dim(arr, index, 0, keepdims=False)


def gather_ctx(own):
    half = jnp.concatenate([own, xor_swap(own, "ctx", 2)], 0)
    return half, xor_swap(half, "ctx", 1)


def weight_over_x(rows):
    if lax.axis_size("fsdp") == 2:
        got = xor_swap(rows, "fsdp", 1)
        first = lax.axis_index("fsdp") == 0
        return jnp.stack([jnp.where(first, rows, got), jnp.where(first, got, rows)])
    every = lax.all_gather(rows, "fsdp", axis=0, tiled=True)
    return every.reshape(2, -1, every.shape[1])


def nt(a, b):
    return lax.dot_general(a, b, (((1,), (1,)), ((), ())), preferred_element_type=F32)


def nn(a, b):
    return lax.dot_general(a, b, (((1,), (0,)), ((), ())), preferred_element_type=F32)


def tn(a, b):
    return lax.dot_general(a, b, (((0,), (0,)), ((), ())), preferred_element_type=F32)


def params(limit, steps=None):
    return pltpu.CompilerParams(vmem_limit_bytes=limit << 20)


def cost(micros, nbytes):
    return pl.CostEstimate(
        flops=int(micros * 0.2 * 10**9), transcendentals=0, bytes_accessed=1024
    )


def normed(x):
    n = x.shape[-1]
    centred = x - jnp.sum(x, -1, keepdims=True) * (1.0 / n)
    rstd = lax.rsqrt(jnp.sum(centred * centred, -1, keepdims=True) * (1.0 / n) + EPS)
    return centred * rstd, rstd


def normed_back(grad, normal, rstd, gain):
    n = grad.shape[-1]
    scaled = grad * gain
    one = jnp.sum(scaled, -1, keepdims=True) * (1.0 / n)
    two = jnp.sum(scaled * normal, -1, keepdims=True) * (1.0 / n)
    return rstd * (scaled - one - normal * two)


def bias_row(ref, row):
    parts = ref[row : row + 3, :].astype(F32)
    return parts[0:1] + parts[1:2] + parts[2:3]


def qkv_kernel(
    cols,
    xo_ref,
    xp_ref,
    vec_ref,
    b_ref,
    w_ref,
    qkv_ref,
    seg_ref,
    lo_ref,
    hi_ref,
):
    first, pieces = xo_ref.shape[0], xo_ref.shape[1]
    thin, width = qkv_ref.shape[2], xo_ref.shape[3]
    half = width // 2
    b = bias_row(b_ref, 0)
    for i in range(2 * first):
        x_ref = xo_ref if i < first else xp_ref
        normal, _ = normed(x_rows(x_ref, i % first, thin).astype(F32))
        xa = (normal * vec_ref[0:1, :] + vec_ref[1:2, :]).astype(BF)
        mixed = nn(xa[:, :half], w_ref[0, :, : 3 * cols]) + nn(xa[:, half:], w_ref[1, :, : 3 * cols])
        parts = (
            mixed[:, :cols] + b[:, :cols],
            mixed[:, cols : 2 * cols],
            mixed[:, 2 * cols :] + b[:, cols : 2 * cols],
        )
        for c, part in enumerate(parts):
            put_lanes(qkv_ref, i, c, part)
        labels = [
            x_ref[i % first, k, thin : thin + SPARE, :thin].astype(F32)[0:1, :]
            for k in range(pieces)
        ]
        labels = jnp.concatenate(labels, 1)
        seg_ref[:, i * pieces * thin : (i + 1) * pieces * thin] = jnp.broadcast_to(
            labels, (8, pieces * thin)
        )
        lo_ref[i] = jnp.min(labels).astype(jnp.int32)
        hi_ref[i] = jnp.max(labels).astype(jnp.int32)


def qkv(xo, xp, vec, b, w, cols, thin):
    first, pieces, _, _ = xo.shape
    bound = jax.ShapeDtypeStruct((2 * first,), jnp.int32)
    return pl.pallas_call(
        partial(qkv_kernel, cols),
        out_shape=(
            jax.ShapeDtypeStruct((2 * first, pieces, thin, 4 * cols), BF),
            jax.ShapeDtypeStruct((8, 2 * first * pieces * thin), F32),
            bound,
            bound,
        ),
        in_specs=[VMEM] * 5,
        out_specs=(VMEM,) * 2 + (SMEM,) * 2,
        compiler_params=params(12),
        cost_estimate=cost(4, 6 << 20),
        name="qkv",
    )(xo, xp, vec, b, w)


def head_mask(h, width):
    lane = lax.broadcasted_iota(jnp.int32, (1, width), 1)
    return (lane >= h * DH) & (lane < (h + 1) * DH)


def only_head(x, h):
    return jnp.where(head_mask(h, x.shape[1]), x, jnp.zeros_like(x))


def x_rows(ref, i, thin):
    return ref[i, :, :thin, :].reshape(-1, ref.shape[3])


def group(ref, i):
    return ref[i].reshape(ref.shape[1] * ref.shape[2], ref.shape[3])


def put_rows(ref, i, value):
    ref[i] = value.astype(ref.dtype).reshape(ref.shape[1:])


def lanes_of(ref, part):
    cols = ref.shape[-1] // 4
    wide = ref.shape[-1] // 3
    return slice(part * wide, part * wide + cols)


def part_rows(ref, i, part):
    value = ref[i, :, :, lanes_of(ref, part)]
    return value.reshape(-1, value.shape[-1])


def put_lanes(ref, i, part, value):
    ref[i, :, :, lanes_of(ref, part)] = value.astype(ref.dtype).reshape(
        ref.shape[1:3] + value.shape[1:]
    )


def turned(x):
    return jnp.transpose(x.astype(F32)).astype(x.dtype)


def with_blocks(lo_ref, hi_ref, list_ref, i, groups, work):
    count = jnp.int32(0)
    for j in range(groups):
        on = (hi_ref[i] >= lo_ref[j]) & (lo_ref[i] <= hi_ref[j])

        @pl.when(on)
        def _():
            list_ref[count] = j

        count = count + on.astype(jnp.int32)
    for number in range(1, groups + 1):

        @pl.when(count == number)
        def _():
            work([list_ref[t] for t in range(number)])


def put_projected(kept_ref, sent_ref, i, project):
    first = kept_ref.shape[0]
    out = kept_ref if i < first else sent_ref
    half = out.shape[3] // 2
    for part in range(2):
        out[i % first, :, :, part * half : (part + 1) * half] = (
            project(part).astype(out.dtype).reshape(out.shape[1:3] + (half,))
        )


def attend_kernel(
    heads,
    lo_ref,
    hi_ref,
    qkv_ref,
    segr_ref,
    w_ref,
    att_ref,
    lse_ref,
    kept_ref,
    sent_ref,
    kk,
    vt,
    ow,
    segc_ref,
    list_ref,
):
    groups = qkv_ref.shape[0]
    n = qkv_ref.shape[1] * qkv_ref.shape[2]
    cols = qkv_ref.shape[3] // 4
    segc_ref[...] = jnp.transpose(segr_ref[...])
    ow[...] = w_ref[:, :, 3 * cols :]
    for i in range(groups):
        kk[i * n : (i + 1) * n, :] = part_rows(qkv_ref, i, 1)
        vt[i] = turned(part_rows(qkv_ref, i, 2))

    def per_query(i, carry):
        qs = pl.ds(pl.multiple_of(i * n, n), n)

        def work(js):
            seg_q = segr_ref[0:1, qs]
            q = part_rows(qkv_ref, i, 0) * jnp.asarray(0.125, BF)
            places = [pl.ds(pl.multiple_of(j * n, n), n) for j in js]
            same = [segc_ref[ks, 0:1] == seg_q for ks in places]
            outs = []
            for h in range(heads):
                qh = only_head(q, h)
                scores = [
                    jnp.where(mask, nt(kk[ks, :], qh), NEG) for ks, mask in zip(places, same)
                ]
                top = [jnp.max(s, 0, keepdims=True) for s in scores]
                top = sum_of(top, jnp.maximum)
                total, out = [], []
                for s, j in zip(scores, js):
                    p = jnp.exp(s - top)
                    total.append(jnp.sum(p, 0, keepdims=True))
                    out.append(nn(vt[j, h * DH : (h + 1) * DH, :], p.astype(BF)))
                total = sum_of(total, jnp.add)
                outs.append(sum_of(out, jnp.add) * (1.0 / total))
                lse_ref[h : h + 1, qs] = top + jnp.log(total)
            out = jnp.transpose(jnp.concatenate(outs, 0))
            put_rows(att_ref, i, jnp.where(segc_ref[qs, 0:1] > 0, out, 0.0))

        with_blocks(lo_ref, hi_ref, list_ref, i, groups, work)
        return carry

    lax.fori_loop(0, groups, per_query, 0)
    for i in range(groups):
        att = group(att_ref, i)
        put_projected(kept_ref, sent_ref, i, lambda part: nt(att, ow[part]))


def sum_of(values, join):
    total = values[0]
    for value in values[1:]:
        total = join(total, value)
    return total


def attend(lo, hi, mixed, segr, w):
    groups, pieces, thin, _ = mixed.shape
    cols = mixed.shape[3] // 4
    heads = cols // DH
    n, rows = pieces * thin, groups * pieces * thin
    width = 2 * w.shape[1]
    return pl.pallas_call(
        partial(attend_kernel, heads),
        out_shape=(
            jax.ShapeDtypeStruct((groups, pieces, thin, cols), BF),
            jax.ShapeDtypeStruct((8, rows), F32),
            jax.ShapeDtypeStruct((groups // 2, pieces, thin, width), F32),
            jax.ShapeDtypeStruct((groups // 2, pieces, thin, width), BF),
        ),
        in_specs=[SMEM, SMEM] + [VMEM] * 3,
        out_specs=(VMEM,) * 4,
        scratch_shapes=[
            pltpu.VMEM((rows, cols), BF),
            pltpu.VMEM((groups, cols, n), BF),
            pltpu.VMEM((2, width // 2, cols), BF),
            pltpu.VMEM((rows, 8), F32),
            pltpu.SMEM((groups,), jnp.int32),
        ],
        compiler_params=params(16),
        cost_estimate=cost(11, 8 << 20),
        name="attend",
    )(lo, hi, mixed, segr, w)


def attend_back_kernel(
    heads,
    lo_ref,
    hi_ref,
    qkv_ref,
    att_ref,
    lse_ref,
    db_ref,
    dp_ref,
    segr_ref,
    w_ref,
    dmix_ref,
    kept_ref,
    sent_ref,
    kt,
    kk,
    vv,
    do_ref,
    delta,
    ak,
    av,
    ow,
    kw,
    segc_ref,
    list_ref,
):
    groups = qkv_ref.shape[0]
    n = qkv_ref.shape[1] * qkv_ref.shape[2]
    cols = qkv_ref.shape[3] // 4
    half = w_ref.shape[1]
    segc_ref[...] = jnp.transpose(segr_ref[...])
    ow[...] = w_ref[:, :, 3 * cols :]
    kw[...] = w_ref[:, :, cols : 2 * cols]
    ak[...] = jnp.zeros_like(ak)
    av[...] = jnp.zeros_like(av)
    for i in range(groups):
        rows = slice(i * n, (i + 1) * n)
        kk[rows, :] = part_rows(qkv_ref, i, 1)
        vv[rows, :] = part_rows(qkv_ref, i, 2)
        kt[i] = turned(part_rows(qkv_ref, i, 1))
        grad = group(db_ref, i) if i < groups // 2 else group(dp_ref, i - groups // 2)
        out_back = nn(grad[:, :half], ow[0]) + nn(grad[:, half:], ow[1])
        do = jnp.where(segc_ref[rows, 0:1] > 0, out_back, 0.0).astype(BF)
        do_ref[rows, :] = do
        prod = jnp.transpose(do.astype(F32) * group(att_ref, i).astype(F32))
        for h in range(heads):
            delta[h : h + 1, rows] = jnp.sum(prod[h * DH : (h + 1) * DH, :], 0, keepdims=True)

    def per_query(i, carry):
        qs = pl.ds(pl.multiple_of(i * n, n), n)

        def work(js):
            seg_q = segr_ref[0:1, qs]
            q = part_rows(qkv_ref, i, 0) * jnp.asarray(0.125, BF)
            do = do_ref[qs, :]
            qh = [only_head(q, h) for h in range(heads)]
            dh = [only_head(do, h) for h in range(heads)]
            dq = [[] for _ in range(heads)]
            for j in js:
                ks = pl.ds(pl.multiple_of(j * n, n), n)
                same = segc_ref[ks, 0:1] == seg_q
                dk, dv = [], []
                for h in range(heads):
                    s = jnp.where(same, nt(kk[ks, :], qh[h]), NEG)
                    p = jnp.exp(s - lse_ref[h : h + 1, qs])
                    ds = (p * (nt(vv[ks, :], dh[h]) - delta[h : h + 1, qs])).astype(BF)
                    dv.append(nn(p.astype(BF), dh[h]))
                    dk.append(nn(ds, qh[h]))
                    dq[h].append(nn(kt[j, h * DH : (h + 1) * DH, :], ds))
                ak[ks, :] += sum_of(dk, jnp.add)
                av[ks, :] += sum_of(dv, jnp.add)
            dq = jnp.concatenate([sum_of(parts, jnp.add) for parts in dq], 0)
            put_lanes(dmix_ref, i, 0, jnp.transpose(dq) * 0.125)

        with_blocks(lo_ref, hi_ref, list_ref, i, groups, work)
        return carry

    lax.fori_loop(0, groups, per_query, 0)
    for i in range(groups):
        rows = slice(i * n, (i + 1) * n)
        dq = part_rows(dmix_ref, i, 0)
        dk = ak[rows, :].astype(BF)
        dv = av[rows, :].astype(BF)
        put_lanes(dmix_ref, i, 1, dk)
        put_lanes(dmix_ref, i, 2, dv)

        def project(part):
            dx = nt(dq, w_ref[part, :, :cols]) + nt(dk, kw[part])
            return dx + nt(dv, w_ref[part, :, 2 * cols : 3 * cols])

        put_projected(kept_ref, sent_ref, i, project)


def attend_back(lo, hi, mixed, att, lse, db, dp, segr, w):
    groups, pieces, thin, cols = att.shape
    heads = cols // DH
    n, rows = pieces * thin, groups * pieces * thin
    width = 2 * w.shape[1]
    return pl.pallas_call(
        partial(attend_back_kernel, heads),
        out_shape=(
            jax.ShapeDtypeStruct(mixed.shape, BF),
            jax.ShapeDtypeStruct((groups // 2, pieces, thin, width), F32),
            jax.ShapeDtypeStruct((groups // 2, pieces, thin, width), BF),
        ),
        in_specs=[SMEM, SMEM] + [VMEM] * 7,
        out_specs=(VMEM,) * 3,
        scratch_shapes=[
            pltpu.VMEM((groups, cols, n), BF),
            pltpu.VMEM((rows, cols), BF),
            pltpu.VMEM((rows, cols), BF),
            pltpu.VMEM((rows, cols), BF),
            pltpu.VMEM((8, rows), F32),
            pltpu.VMEM((rows, cols), F32),
            pltpu.VMEM((rows, cols), F32),
            pltpu.VMEM((2, width // 2, cols), BF),
            pltpu.VMEM((2, width // 2, cols), BF),
            pltpu.VMEM((rows, 8), F32),
            pltpu.SMEM((groups,), jnp.int32),
        ],
        compiler_params=params(18),
        cost_estimate=cost(70, 12 << 20),
        name="attend_back",
    )(lo, hi, mixed, att, lse, db, dp, segr, w)


def middle_kernel(s_ref, got_ref, x_ref, vec_ref, mid_ref, xb_ref):
    n, _, thin, width = s_ref.shape
    for i in range(n):
        x = x_rows(x_ref, i, thin).astype(F32)
        mid = group(s_ref, i) + group(got_ref, n - 1 - i).astype(F32) + x + vec_ref[0:1, :]
        put_rows(mid_ref, i, mid)
        normal, _ = normed(mid)
        put_rows(xb_ref, i, normal * vec_ref[1:2, :] + vec_ref[2:3, :])


def middle_rows(s, got, x, vec):
    return pl.pallas_call(
        middle_kernel,
        out_shape=(jax.ShapeDtypeStruct(s.shape, F32), jax.ShapeDtypeStruct(s.shape, BF)),
        in_specs=[VMEM] * 4,
        out_specs=(VMEM,) * 2,
        compiler_params=params(8),
        cost_estimate=cost(2, 4 << 20),
        name="middle_rows",
    )(s, got, x, vec)


def middle_back_kernel(s_ref, got_ref, mid_ref, g_ref, vec_ref, dmid_ref, db_ref, sum_ref):
    n = s_ref.shape[0]
    for i in range(n):
        dxb = group(s_ref, i) + group(got_ref, n - 1 - i).astype(F32)
        normal, rstd = normed(group(mid_ref, i))
        grad = group(g_ref, i).astype(F32)
        dmid = grad + normed_back(dxb, normal, rstd, vec_ref[...])
        low = dmid.astype(BF)
        put_rows(dmid_ref, i, dmid)
        put_rows(db_ref, i, low)
        if i == 0:
            sum_ref[0:1, :] = jnp.sum(low.astype(F32), 0, keepdims=True)
            sum_ref[1:2, :] = jnp.sum(dxb * normal, 0, keepdims=True)
            sum_ref[2:3, :] = jnp.sum(dxb, 0, keepdims=True)
            sum_ref[3:4, :] = jnp.sum(grad, 0, keepdims=True)


def middle_back(s, got, mid, g, vec):
    return pl.pallas_call(
        middle_back_kernel,
        out_shape=(
            jax.ShapeDtypeStruct(s.shape, F32),
            jax.ShapeDtypeStruct(s.shape, BF),
            jax.ShapeDtypeStruct((4, s.shape[-1]), F32),
        ),
        in_specs=[VMEM] * 5,
        out_specs=(VMEM,) * 3,
        compiler_params=params(8),
        cost_estimate=cost(2, 5 << 20),
        name="middle_back",
    )(s, got, mid, g, vec)


def add_kernel(kept_ref, got_ref, sum_ref, low_ref):
    for i in range(kept_ref.shape[0]):
        total = group(kept_ref, i) + group(got_ref, i).astype(F32)
        put_rows(sum_ref, i, total)
        if i >= kept_ref.shape[0] - low_ref.shape[0]:
            put_rows(low_ref, i - (kept_ref.shape[0] - low_ref.shape[0]), total)


def core_sum(kept, sent, low_blocks):
    got = xor_swap(sent, "ctx", 1)
    return pl.pallas_call(
        add_kernel,
        out_shape=(
            jax.ShapeDtypeStruct(kept.shape, F32),
            jax.ShapeDtypeStruct((low_blocks,) + kept.shape[1:], BF),
        ),
        in_specs=[VMEM] * 2,
        out_specs=(VMEM,) * 2,
        compiler_params=params(6),
        cost_estimate=cost(1, 4 << 20),
        name="add_rows",
    )(kept, got)


def first_back_kernel(
    s_ref, got_ref, x_ref, dmid_ref, mid_ref, mlp_ref, mlpgot_ref, vec_ref, out_ref
):
    thin = s_ref.shape[2]
    pieces = out_ref.shape[0]
    result = group(mid_ref, 0) + group(mlp_ref, 0) + group(mlpgot_ref, 0).astype(F32)
    result = result + vec_ref[1:2, :]
    out_ref[:, :thin, :] = result.astype(BF).reshape(pieces, thin, -1)
    dxa = group(s_ref, 0) + group(got_ref, 0).astype(F32)
    normal, rstd = normed(x_rows(x_ref, 0, thin).astype(F32))
    grad = group(dmid_ref, 0) + normed_back(dxa, normal, rstd, vec_ref[0:1, :])
    out_ref[:, thin:, :] = grad.astype(BF).reshape(pieces, thin, -1)


def first_back(s, got, x, dmid, mid, mlp, mlpgot, vec):
    _, pieces, thin, width = s.shape
    return pl.pallas_call(
        first_back_kernel,
        out_shape=jax.ShapeDtypeStruct((pieces, 2 * thin, width), BF),
        in_specs=[VMEM] * 8,
        out_specs=VMEM,
        compiler_params=params(8),
        cost_estimate=cost(20, 6 << 20),
        name="first_back",
    )(s, got, x, dmid, mid, mlp, mlpgot, vec)


def pieces_kernel(own_ref, got_ref, vec_ref, out_ref):
    blocks, r = out_ref.shape[0], out_ref.shape[1] - SPARE
    for b in range(blocks):
        part = slice(b * r, (b + 1) * r)
        out_ref[b, :r, :] = (own_ref[part, :].astype(F32) + got_ref[part, :].astype(F32)).astype(BF)
        last = slice(blocks * r, blocks * r + 2)
        out_ref[b, r : r + 2, :] = (
            own_ref[last, :].astype(F32) + got_ref[last, :].astype(F32)
        ).astype(BF)
        out_ref[b, r + 2 :, :] = vec_ref[...].astype(BF)


def grad_pieces(stay, go, vec, blocks):
    rows = stay.shape[0] - SPARE
    if lax.axis_size("fsdp") == 2 and rows // blocks % 16 == 0:
        return pl.pallas_call(
            pieces_kernel,
            out_shape=jax.ShapeDtypeStruct((blocks, rows // blocks + SPARE, stay.shape[1]), BF),
            in_specs=[VMEM] * 3,
            out_specs=VMEM,
            compiler_params=params(6),
            cost_estimate=cost(1, 2 << 20),
            name="grad_pieces",
        )(stay, xor_swap(go, "fsdp", 1), vec)
    last = lax.psum(stay[rows : rows + 2].astype(F32), "fsdp")
    split = jnp.concatenate([stay[:rows], go[:rows]], 0).reshape(
        lax.axis_size("fsdp"), -1, stay.shape[1]
    )
    own = lax.psum_scatter(split.astype(F32), "fsdp", scatter_dimension=0, tiled=False)
    own = own.reshape(blocks, -1, own.shape[-1])
    small = jnp.concatenate([last, vec], 0)
    small = jnp.broadcast_to(small, (blocks,) + small.shape)
    return jnp.concatenate([own, small], 1).astype(BF)


def weight_part(ref, part):
    w = ref[:, part]
    return w.reshape(w.shape[0] * w.shape[1], w.shape[2])


def mlp_kernel(
    xo_ref,
    xp_ref,
    go_ref,
    gp_ref,
    m_ref,
    b_ref,
    hidden_ref,
    dpre_ref,
    kept_ref,
    sent_ref,
):
    first = xo_ref.shape[0]
    b = bias_row(b_ref, 3)
    for i in range(2 * first):
        own = i < first
        pre = nn(group(xo_ref if own else xp_ref, i % first), weight_part(m_ref, 0)) + b
        dhidden = nn(group(go_ref if own else gp_ref, i % first), weight_part(m_ref, 1))
        share = 0.5 * (1.0 + lax.erf(pre * (0.5**0.5)))
        density = jnp.exp(pre * pre * -0.5) * ((0.5 / 3.141592653589793) ** 0.5)
        n = pre.shape[0]
        hidden_ref[i * n : (i + 1) * n, :] = (pre * share).astype(BF)
        dpre = (dhidden * (share + pre * density)).astype(BF)
        dpre_ref[i * n : (i + 1) * n, :] = dpre
        put_rows(kept_ref if own else sent_ref, i % first, nt(dpre, weight_part(m_ref, 0)))


def mlp_block(xo, xp, go, gp, m, b):
    blocks, pieces, thin, width = xo.shape
    low = jax.ShapeDtypeStruct((2 * blocks * pieces * thin, m.shape[-1]), BF)
    return pl.pallas_call(
        mlp_kernel,
        out_shape=(low, low, jax.ShapeDtypeStruct(xo.shape, F32), jax.ShapeDtypeStruct(xo.shape, BF)),
        in_specs=[VMEM] * 6,
        out_specs=(VMEM,) * 4,
        compiler_params=params(12),
        cost_estimate=cost(7, 12 << 20),
        name="mlp_block",
    )(xo, xp, go, gp, m, b)


def mlp_grads_kernel(
    xo_ref,
    xp_ref,
    dpre_ref,
    go_ref,
    gp_ref,
    hidden_ref,
    m_ref,
    grad_ref,
    kept_ref,
    sent_ref,
    sum_ref,
):
    first, width = xo_ref.shape[0], xo_ref.shape[3]
    half = width // 2
    rows = dpre_ref.shape[0]
    n = rows // 2
    for i in range(2):
        lanes = slice(i * half, (i + 1) * half)
        xo, xp = (ref[:, :, :, lanes].reshape(n, half) for ref in (xo_ref, xp_ref))
        up = tn(xo, dpre_ref[:n, :]) + tn(xp, dpre_ref[n:, :])
        grad_ref[:, i, 0] = up.astype(BF).reshape((-1,) + grad_ref.shape[3:])
        go, gp = (ref[:, :, :, lanes].reshape(n, half) for ref in (go_ref, gp_ref))
        down = tn(go, hidden_ref[:n, :]) + tn(gp, hidden_ref[n:, :])
        grad_ref[:, i, 1] = down.astype(BF).reshape((-1,) + grad_ref.shape[3:])
    size = n // first
    for i in range(2 * first):
        result = nt(hidden_ref[i * size : (i + 1) * size, :], weight_part(m_ref, 1))
        put_rows(kept_ref if i < first else sent_ref, i % first, result)
    sum_ref[...] = jnp.sum(dpre_ref[...].astype(F32), 0, keepdims=True)


def mlp_grads(xo, xp, dpre, go, gp, hidden, m):
    return pl.pallas_call(
        mlp_grads_kernel,
        out_shape=(
            jax.ShapeDtypeStruct((m.shape[0] // 2, 2) + m.shape[1:], BF),
            jax.ShapeDtypeStruct(xo.shape, F32),
            jax.ShapeDtypeStruct(xo.shape, BF),
            jax.ShapeDtypeStruct((1, dpre.shape[1]), F32),
        ),
        in_specs=[VMEM] * 7,
        out_specs=(VMEM,) * 4,
        compiler_params=params(14),
        cost_estimate=cost(6, 12 << 20),
        name="mlp_grads",
    )(xo, xp, dpre, go, gp, hidden, m)


def attend_grads_kernel(
    flip_ref,
    sum_ref,
    norm_ref,
    dmix_ref,
    do_ref,
    dp_ref,
    att_ref,
    kept_ref,
    sent_ref,
    xo_ref,
    xp_ref,
    stay_ref,
    go_ref,
    vec_ref,
    xa,
):
    first, _, thin, width = kept_ref.shape
    rows, cols = att_ref.shape
    half = width // 2
    n = do_ref.shape[0]
    block = rows // (2 * first)
    gain = bias = jnp.zeros((1, width), F32)
    for i in range(2 * first):
        x_ref, g_ref = (xo_ref, kept_ref) if i < first else (xp_ref, sent_ref)
        normal, _ = normed(x_rows(x_ref, i % first, thin).astype(F32))
        xa[i * block : (i + 1) * block, :] = (
            normal * norm_ref[0:1, :] + norm_ref[1:2, :]
        ).astype(BF)
        dx = group(g_ref, i % first).astype(F32)
        gain = gain + jnp.sum(dx * normal, 0, keepdims=True)
        bias = bias + jnp.sum(dx, 0, keepdims=True)
    vec_ref[0:1, :] = gain
    vec_ref[1:2, :] = bias
    totals = [
        jnp.sum(dmix_ref[:, lanes_of(dmix_ref, c)].astype(F32), 0, keepdims=True).astype(BF)
        for c in (0, 2)
    ]

    def half_grads(i, out_ref):
        lanes = slice(i * half, (i + 1) * half)
        for c in range(3):
            out_ref[:half, c * cols : (c + 1) * cols] = tn(
                xa[:, lanes], dmix_ref[:, lanes_of(dmix_ref, c)]
            ).astype(BF)
        out = tn(do_ref[:, lanes], att_ref[:n, :]) + tn(dp_ref[:, lanes], att_ref[n:, :])
        out_ref[:half, 3 * cols : 4 * cols] = out.astype(BF)
        out_ref[half : half + SPARE, :] = jnp.zeros((SPARE, out_ref.shape[1]), BF)
        for place, total in enumerate(totals):
            out_ref[half : half + 1, place * cols : (place + 1) * cols] = total
        out_ref[half + 1 : half + 2, : sum_ref.shape[1]] = sum_ref[...].astype(BF)

    for flip in range(2):

        @pl.when(flip_ref[0] == flip)
        def _():
            half_grads(flip, stay_ref)
            half_grads(1 - flip, go_ref)


def attend_grads(flip, sums, norms, dmix, do, dp, att, kept, sent, xo, xp):
    width = do.shape[1]
    shape = jax.ShapeDtypeStruct((width // 2 + SPARE, 4 * att.shape[1]), BF)
    return pl.pallas_call(
        attend_grads_kernel,
        out_shape=(shape, shape, jax.ShapeDtypeStruct((2, width), F32)),
        in_specs=[SMEM] + [VMEM] * 10,
        out_specs=(VMEM,) * 3,
        scratch_shapes=[pltpu.VMEM((att.shape[0], width), BF)],
        compiler_params=params(14),
        cost_estimate=cost(6, 12 << 20),
        name="attend_grads",
    )(flip, sums, norms, dmix, do, dp, att, kept, sent, xo, xp)


def exact_low(x):
    one = lax.reduce_precision(x, 8, 7)
    two = lax.reduce_precision(x - one, 8, 7)
    return jnp.concatenate([one, two, x - one - two], 0).astype(BF)


def per_device(
    inputs,
    segments,
    ln1_gain,
    ln1_bias,
    query_key_value_weight,
    b_qv,
    output_weight,
    output_bias,
    ln2_gain,
    ln2_bias,
    up_weight,
    up_bias,
    down_weight,
    down_bias,
    out_grad,
):
    z = lax.axis_index("tp")
    ctx = lax.axis_index("ctx")
    planes = lax.axis_size("tp")
    thin, width = inputs.shape[1], inputs.shape[2]
    ds, _, cols = query_key_value_weight.shape
    hidden_cols = up_weight.shape[1]

    vectors = jnp.stack([ln1_gain, ln1_bias, output_bias, ln2_gain, ln2_bias, down_bias])
    rows_of = lambda a: a.reshape(-1, a.shape[-1])

    biases = jnp.pad(b_qv.reshape(1, -1), ((0, 0), (0, width - 2 * cols)))
    biases = [exact_low(biases), exact_low(up_bias.reshape(1, -1)), jnp.zeros((SPARE - 6, width), BF)]
    a_shard = jnp.concatenate(
        [query_key_value_weight.reshape(ds, 3 * cols), jnp.transpose(output_weight)], 1
    )
    a_shard = jnp.concatenate([a_shard] + biases, 0)
    labels = jnp.pad(segments.astype(BF)[:, None, :], ((0, 0), (0, SPARE - 1), (0, width - thin)))
    own = rows_over_z(jnp.concatenate([after(inputs, a_shard), labels, out_grad], 1))
    x_own, g_own = own[:, : thin + SPARE], own[:, thin + SPARE :]
    got = [send_turned(a_shard, k) for k in range(planes)]
    a_rows = place([g[:ds] for g in got], z).reshape(-1, width)
    biases = got[0][ds:]
    w_attn = weight_over_x(a_rows)
    x_pair, x_far = gather_ctx(after(x_own, w_attn)[None])
    g_own = after(g_own, x_pair)[None]

    m_shard = jnp.concatenate([up_weight, jnp.transpose(down_weight)], 0)
    m_shard = send_turned(after(m_shard, a_rows), 0)
    m_all = lax.all_gather(m_shard, ("fsdp", "tp"), axis=0, tiled=True)
    m_all = m_all.reshape(-1, 2, ds, hidden_cols)
    aligned = ds % 16 == 0 and m_all.shape[0] % 2 == 0
    if not aligned:
        m_all = m_all.reshape(2, -1, 2, ds, hidden_cols).transpose(0, 2, 1, 3, 4)
        m_all = m_all.reshape(2, 2, width // 2, hidden_cols)

    mixed, segr, lo, hi = qkv(x_pair, x_far, vectors, biases, w_attn, cols, thin)
    g_got = xor_swap(g_own, "ctx", 2)
    attended, lse, kept, sent = attend(lo, hi, mixed, segr, w_attn)
    g_got, kept, sent = lax.optimization_barrier((g_got, kept, sent))
    g_pair = jnp.concatenate([g_own, g_got], 0)
    g_far = xor_swap(g_pair, "ctx", 1)
    s, low = core_sum(kept, sent, kept.shape[0])
    got = after(xor_swap(low, "ctx", 2), m_all)
    middle, xb_pair = middle_rows(s, got, x_pair, vectors[2:5])
    xb_far = xor_swap(xb_pair, "ctx", 1)

    hidden, dpre, kept, sent = mlp_block(xb_pair, xb_far, g_pair, g_far, m_all, biases)
    s, low = core_sum(kept, sent, kept.shape[0])
    m_grad, mlp_kept, mlp_sent, dpre_sum = mlp_grads(
        xb_pair, xb_far, after(dpre, s), g_pair, g_far, hidden, m_all
    )
    got = xor_swap(low, "ctx", 2)
    mlp_s, mlp_low = core_sum(mlp_kept, after(mlp_sent, got), 1)
    dmid, db_pair, sums_two = middle_back(
        s, after(got, dpre_sum), middle, g_pair, vectors[3:4]
    )
    db_far = xor_swap(db_pair, "ctx", 1)
    if not aligned:
        m_grad = m_grad[0].transpose(1, 0, 2, 3).reshape(2, -1, planes, ds, hidden_cols)
        m_grad = m_grad.transpose(2, 1, 0, 3, 4)
    m_sums = lax.psum_scatter(m_grad, "tp", scatter_dimension=0, tiled=False)
    mlp_got = xor_swap(after(mlp_low, db_far), "ctx", 2)

    dmix, kept, sent = attend_back(
        lo, hi, mixed, attended, lse, db_pair, db_far, segr, w_attn
    )
    s, low = core_sum(kept, after(sent, mlp_got), 1)
    flip = lax.axis_index("fsdp") if lax.axis_size("fsdp") == 2 else 0
    got = xor_swap(low, "ctx", 2)
    g_stay, g_go, sums_one = attend_grads(
        jnp.full((1,), flip, jnp.int32),
        dpre_sum,
        vectors[0:2],
        after(rows_of(dmix), s),
        rows_of(db_pair),
        rows_of(db_far),
        rows_of(attended),
        kept,
        sent,
        x_pair,
        x_far,
    )
    vec = jnp.concatenate([vectors[0:1], vectors[5:6]], 0)
    both = first_back(s, after(got, sums_one), x_pair, dmid, middle, mlp_s, mlp_got, vec)
    shared = after(jnp.concatenate([sums_one, sums_two], 0), both)
    shared = shared + xor_swap(shared, "ctx", 1)
    shared = shared + xor_swap(shared, "ctx", 2)
    if lax.axis_size("fsdp") == 2:
        shared = shared + xor_swap(shared, "fsdp", 1)
    else:
        shared = lax.psum(shared, "fsdp")
    a_low = grad_pieces(g_stay, g_go, shared, planes)

    both = rows_over_z(both)
    output, input_grad = both[:, :thin], both[:, thin:].astype(F32)
    got = scatter_blocks(a_low, m_sums, both)
    if lax.axis_size("fsdp") == 2:
        x = lax.axis_index("fsdp")
        m_got = xor_swap(pick(m_sums, x ^ 1), "fsdp", 1)
        m_sums = (pick(m_sums, x).astype(F32) + m_got.astype(F32)).astype(BF)
    else:
        m_sums = lax.psum_scatter(m_sums.astype(F32), "fsdp", scatter_dimension=0, tiled=False)
        m_sums = m_sums.astype(BF)
    m_back = send_back(m_sums.reshape(2 * ds, hidden_cols), 0)
    *got, m_back = lax.optimization_barrier((*got, m_back))

    g_attn = sum(g.astype(F32) for g in got)
    grad_qkv = g_attn[:ds, : 3 * cols].reshape(ds, 3, cols)
    grad_out = jnp.transpose(g_attn[:ds, 3 * cols :])
    mine, shared = g_attn[ds : ds + 2], g_attn[ds + 2 :]
    g_mlp = m_back.astype(F32)
    grad_up, grad_down = g_mlp[:ds], jnp.transpose(g_mlp[ds:])
    return (
        output,
        input_grad,
        shared[0],
        shared[1],
        grad_qkv,
        mine[0, : 2 * cols].reshape(2, cols),
        grad_out,
        shared[2],
        shared[3],
        shared[4],
        grad_up,
        mine[1, :hidden_cols],
        grad_down,
        shared[5],
    )


def solution(mesh):
    in_specs = (
        P("fsdp", ("ctx", "tp"), None),
        P("fsdp", ("ctx", "tp")),
        P(),
        P(),
        P(("fsdp", "ctx"), None, "tp"),
        P(None, "tp"),
        P("tp", ("fsdp", "ctx")),
        P(),
        P(),
        P(),
        P(("fsdp", "ctx"), "tp"),
        P("tp"),
        P("tp", ("fsdp", "ctx")),
        P(),
        P("fsdp", ("ctx", "tp"), None),
    )
    out_specs = (
        P("fsdp", ("ctx", "tp"), None),
        P("fsdp", ("ctx", "tp"), None),
        P(),
        P(),
        P(("fsdp", "ctx"), None, "tp"),
        P(None, "tp"),
        P("tp", ("fsdp", "ctx")),
        P(),
        P(),
        P(),
        P(("fsdp", "ctx"), "tp"),
        P("tp"),
        P("tp", ("fsdp", "ctx")),
        P(),
    )
    return jax.shard_map(
        per_device, mesh=mesh, in_specs=in_specs, out_specs=out_specs, check_vma=False
    )
```

```python
from functools import partial

import jax
import jax.numpy as jnp
from jax import lax
from jax.experimental import pallas as pl
from jax.experimental.pallas import tpu as pltpu
from jax.sharding import PartitionSpec as P

DH = 64
EPS = 1e-06
BF = jnp.bfloat16
F32 = jnp.float32
NEG = -1e30
SPARE = 8
VMEM = pl.BlockSpec(memory_space=pltpu.VMEM)
SMEM = pl.BlockSpec(memory_space=pltpu.SMEM)


def after(x, *deps):
    return lax.optimization_barrier((x,) + deps)[0]


def xor_swap(x, axis, k):
    n = lax.axis_size(axis)
    return lax.ppermute(x, axis, [(i, i ^ k) for i in range(n)])


def turn_pairs(n, k):
    return [(a * n + b, b * n + (a ^ k)) for a in range(n) for b in range(n)]


def send_turned(x, k):
    return lax.ppermute(x, ("ctx", "tp"), turn_pairs(lax.axis_size("tp"), k))


def send_back(x, k):
    pairs = turn_pairs(lax.axis_size("tp"), k)
    return lax.ppermute(x, ("ctx", "tp"), [(d, s) for s, d in pairs])


def hop_pairs(n, k):
    pairs = []
    for a in range(n):
        for q in range(n):
            f, low = (q ^ k) // 2, (q ^ k) % 2
            pairs.append((a * n + q, ((a // 2) * 2 + low) * n + (a ^ (2 * f))))
    return pairs


def scatter_blocks(pieces, *late):
    n = lax.axis_size("tp")
    y, q = lax.axis_index("ctx") // 2, lax.axis_index("tp")
    split = pieces.reshape((2, 2) + pieces.shape[1:])
    got = xor_swap(pick(split, y ^ 1), "ctx", 2)
    four = after(jnp.concatenate([pick(split, y), got], 0), *late)
    return [lax.ppermute(pick(four, q ^ k), ("ctx", "tp"), hop_pairs(n, k)) for k in range(n)]


def rows_over_z(arr):
    return lax.all_to_all(arr, "tp", 0, 0, tiled=True)


def place(pieces, first):
    out = jnp.zeros((len(pieces),) + pieces[0].shape, pieces[0].dtype)
    for k, piece in enumerate(pieces):
        out = lax.dynamic_update_index_in_dim(out, piece, first ^ k, 0)
    return out


def pick(arr, index):
    return lax.dynamic_index_in_dim(arr, index, 0, keepdims=False)


def gather_ctx(own):
    half = jnp.concatenate([own, xor_swap(own, "ctx", 2)], 0)
    return half, xor_swap(half, "ctx", 1)


def weight_over_x(rows):
    if lax.axis_size("fsdp") == 2:
        got = xor_swap(rows, "fsdp", 1)
        first = lax.axis_index("fsdp") == 0
        return jnp.stack([jnp.where(first, rows, got), jnp.where(first, got, rows)])
    every = lax.all_gather(rows, "fsdp", axis=0, tiled=True)
    return every.reshape(2, -1, every.shape[1])


def nt(a, b):
    return lax.dot_general(a, b, (((1,), (1,)), ((), ())), preferred_element_type=F32)


def nn(a, b):
    return lax.dot_general(a, b, (((1,), (0,)), ((), ())), preferred_element_type=F32)


def tn(a, b):
    return lax.dot_general(a, b, (((0,), (0,)), ((), ())), preferred_element_type=F32)


def params(limit, steps=None):
    return pltpu.CompilerParams(vmem_limit_bytes=limit << 20)


def cost(micros, nbytes):
    return pl.CostEstimate(
        flops=int(micros * 0.2 * 10**9), transcendentals=0, bytes_accessed=1024
    )


def normed(x):
    n = x.shape[-1]
    centred = x - jnp.sum(x, -1, keepdims=True) * (1.0 / n)
    rstd = lax.rsqrt(jnp.sum(centred * centred, -1, keepdims=True) * (1.0 / n) + EPS)
    return centred * rstd, rstd


def normed_back(grad, normal, rstd, gain):
    n = grad.shape[-1]
    scaled = grad * gain
    one = jnp.sum(scaled, -1, keepdims=True) * (1.0 / n)
    two = jnp.sum(scaled * normal, -1, keepdims=True) * (1.0 / n)
    return rstd * (scaled - one - normal * two)


def bias_row(ref, row):
    parts = ref[row : row + 3, :].astype(F32)
    return parts[0:1] + parts[1:2] + parts[2:3]


def qkv_kernel(
    cols,
    xo_ref,
    xp_ref,
    vec_ref,
    b_ref,
    w_ref,
    qkv_ref,
    seg_ref,
    lo_ref,
    hi_ref,
):
    first, pieces = xo_ref.shape[0], xo_ref.shape[1]
    thin, width = qkv_ref.shape[2], xo_ref.shape[3]
    half = width // 2
    b = bias_row(b_ref, 0)
    for i in range(2 * first):
        x_ref = xo_ref if i < first else xp_ref
        normal, _ = normed(x_rows(x_ref, i % first, thin).astype(F32))
        xa = (normal * vec_ref[0:1, :] + vec_ref[1:2, :]).astype(BF)
        mixed = nn(xa[:, :half], w_ref[0, :, : 3 * cols]) + nn(xa[:, half:], w_ref[1, :, : 3 * cols])
        parts = (
            mixed[:, :cols] + b[:, :cols],
            mixed[:, cols : 2 * cols],
            mixed[:, 2 * cols :] + b[:, cols : 2 * cols],
        )
        for c, part in enumerate(parts):
            put_lanes(qkv_ref, i, c, part)
        labels = [
            x_ref[i % first, k, thin : thin + SPARE, :thin].astype(F32)[0:1, :]
            for k in range(pieces)
        ]
        labels = jnp.concatenate(labels, 1)
        seg_ref[:, i * pieces * thin : (i + 1) * pieces * thin] = jnp.broadcast_to(
            labels, (8, pieces * thin)
        )
        lo_ref[i] = jnp.min(labels).astype(jnp.int32)
        hi_ref[i] = jnp.max(labels).astype(jnp.int32)


def qkv(xo, xp, vec, b, w, cols, thin):
    first, pieces, _, _ = xo.shape
    bound = jax.ShapeDtypeStruct((2 * first,), jnp.int32)
    return pl.pallas_call(
        partial(qkv_kernel, cols),
        out_shape=(
            jax.ShapeDtypeStruct((2 * first, pieces, thin, 4 * cols), BF),
            jax.ShapeDtypeStruct((8, 2 * first * pieces * thin), F32),
            bound,
            bound,
        ),
        in_specs=[VMEM] * 5,
        out_specs=(VMEM,) * 2 + (SMEM,) * 2,
        compiler_params=params(12),
        cost_estimate=cost(4, 6 << 20),
        name="qkv",
    )(xo, xp, vec, b, w)


def head_mask(h, width):
    lane = lax.broadcasted_iota(jnp.int32, (1, width), 1)
    return (lane >= h * DH) & (lane < (h + 1) * DH)


def only_head(x, h):
    return jnp.where(head_mask(h, x.shape[1]), x, jnp.zeros_like(x))


def x_rows(ref, i, thin):
    return ref[i, :, :thin, :].reshape(-1, ref.shape[3])


def group(ref, i):
    return ref[i].reshape(ref.shape[1] * ref.shape[2], ref.shape[3])


def put_rows(ref, i, value):
    ref[i] = value.astype(ref.dtype).reshape(ref.shape[1:])


def lanes_of(ref, part):
    cols = ref.shape[-1] // 4
    wide = ref.shape[-1] // 3
    return slice(part * wide, part * wide + cols)


def part_rows(ref, i, part):
    value = ref[i, :, :, lanes_of(ref, part)]
    return value.reshape(-1, value.shape[-1])


def put_lanes(ref, i, part, value):
    ref[i, :, :, lanes_of(ref, part)] = value.astype(ref.dtype).reshape(
        ref.shape[1:3] + value.shape[1:]
    )


def turned(x):
    return jnp.transpose(x.astype(F32)).astype(x.dtype)


def with_blocks(lo_ref, hi_ref, list_ref, i, groups, work):
    count = jnp.int32(0)
    for j in range(groups):
        on = (hi_ref[i] >= lo_ref[j]) & (lo_ref[i] <= hi_ref[j])

        @pl.when(on)
        def _():
            list_ref[count] = j

        count = count + on.astype(jnp.int32)
    for number in range(1, groups + 1):

        @pl.when(count == number)
        def _():
            work([list_ref[t] for t in range(number)])


def put_projected(kept_ref, sent_ref, i, project):
    first = kept_ref.shape[0]
    out = kept_ref if i < first else sent_ref
    half = out.shape[3] // 2
    for part in range(2):
        out[i % first, :, :, part * half : (part + 1) * half] = (
            project(part).astype(out.dtype).reshape(out.shape[1:3] + (half,))
        )


def attend_kernel(
    heads,
    lo_ref,
    hi_ref,
    qkv_ref,
    segr_ref,
    w_ref,
    att_ref,
    lse_ref,
    kept_ref,
    sent_ref,
    kk,
    vt,
    ow,
    segc_ref,
    list_ref,
):
    groups = qkv_ref.shape[0]
    n = qkv_ref.shape[1] * qkv_ref.shape[2]
    cols = qkv_ref.shape[3] // 4
    segc_ref[...] = jnp.transpose(segr_ref[...])
    ow[...] = w_ref[:, :, 3 * cols :]
    for i in range(groups):
        kk[i * n : (i + 1) * n, :] = part_rows(qkv_ref, i, 1)
        vt[i] = turned(part_rows(qkv_ref, i, 2))

    def per_query(i, carry):
        qs = pl.ds(pl.multiple_of(i * n, n), n)

        def work(js):
            seg_q = segr_ref[0:1, qs]
            q = part_rows(qkv_ref, i, 0) * jnp.asarray(0.125, BF)
            places = [pl.ds(pl.multiple_of(j * n, n), n) for j in js]
            same = [segc_ref[ks, 0:1] == seg_q for ks in places]
            outs = []
            for h in range(heads):
                qh = only_head(q, h)
                scores = [
                    jnp.where(mask, nt(kk[ks, :], qh), NEG) for ks, mask in zip(places, same)
                ]
                top = [jnp.max(s, 0, keepdims=True) for s in scores]
                top = sum_of(top, jnp.maximum)
                total, out = [], []
                for s, j in zip(scores, js):
                    p = jnp.exp(s - top)
                    total.append(jnp.sum(p, 0, keepdims=True))
                    out.append(nn(vt[j, h * DH : (h + 1) * DH, :], p.astype(BF)))
                total = sum_of(total, jnp.add)
                outs.append(sum_of(out, jnp.add) * (1.0 / total))
                lse_ref[h : h + 1, qs] = top + jnp.log(total)
            out = jnp.transpose(jnp.concatenate(outs, 0))
            put_rows(att_ref, i, jnp.where(segc_ref[qs, 0:1] > 0, out, 0.0))

        with_blocks(lo_ref, hi_ref, list_ref, i, groups, work)
        return carry

    lax.fori_loop(0, groups, per_query, 0)
    for i in range(groups):
        att = group(att_ref, i)
        put_projected(kept_ref, sent_ref, i, lambda part: nt(att, ow[part]))


def sum_of(values, join):
    total = values[0]
    for value in values[1:]:
        total = join(total, value)
    return total


def attend(lo, hi, mixed, segr, w):
    groups, pieces, thin, _ = mixed.shape
    cols = mixed.shape[3] // 4
    heads = cols // DH
    n, rows = pieces * thin, groups * pieces * thin
    width = 2 * w.shape[1]
    return pl.pallas_call(
        partial(attend_kernel, heads),
        out_shape=(
            jax.ShapeDtypeStruct((groups, pieces, thin, cols), BF),
            jax.ShapeDtypeStruct((8, rows), F32),
            jax.ShapeDtypeStruct((groups // 2, pieces, thin, width), F32),
            jax.ShapeDtypeStruct((groups // 2, pieces, thin, width), BF),
        ),
        in_specs=[SMEM, SMEM] + [VMEM] * 3,
        out_specs=(VMEM,) * 4,
        scratch_shapes=[
            pltpu.VMEM((rows, cols), BF),
            pltpu.VMEM((groups, cols, n), BF),
            pltpu.VMEM((2, width // 2, cols), BF),
            pltpu.VMEM((rows, 8), F32),
            pltpu.SMEM((groups,), jnp.int32),
        ],
        compiler_params=params(16),
        cost_estimate=cost(11, 8 << 20),
        name="attend",
    )(lo, hi, mixed, segr, w)


def attend_back_kernel(
    heads,
    lo_ref,
    hi_ref,
    qkv_ref,
    att_ref,
    lse_ref,
    db_ref,
    dp_ref,
    segr_ref,
    w_ref,
    dmix_ref,
    kept_ref,
    sent_ref,
    kt,
    kk,
    vv,
    do_ref,
    delta,
    ak,
    av,
    ow,
    kw,
    segc_ref,
    list_ref,
):
    groups = qkv_ref.shape[0]
    n = qkv_ref.shape[1] * qkv_ref.shape[2]
    cols = qkv_ref.shape[3] // 4
    half = w_ref.shape[1]
    segc_ref[...] = jnp.transpose(segr_ref[...])
    ow[...] = w_ref[:, :, 3 * cols :]
    kw[...] = w_ref[:, :, cols : 2 * cols]
    ak[...] = jnp.zeros_like(ak)
    av[...] = jnp.zeros_like(av)
    for i in range(groups):
        rows = slice(i * n, (i + 1) * n)
        kk[rows, :] = part_rows(qkv_ref, i, 1)
        vv[rows, :] = part_rows(qkv_ref, i, 2)
        kt[i] = turned(part_rows(qkv_ref, i, 1))
        grad = group(db_ref, i) if i < groups // 2 else group(dp_ref, i - groups // 2)
        out_back = nn(grad[:, :half], ow[0]) + nn(grad[:, half:], ow[1])
        do = jnp.where(segc_ref[rows, 0:1] > 0, out_back, 0.0).astype(BF)
        do_ref[rows, :] = do
        prod = jnp.transpose(do.astype(F32) * group(att_ref, i).astype(F32))
        for h in range(heads):
            delta[h : h + 1, rows] = jnp.sum(prod[h * DH : (h + 1) * DH, :], 0, keepdims=True)

    def per_query(i, carry):
        qs = pl.ds(pl.multiple_of(i * n, n), n)

        def work(js):
            seg_q = segr_ref[0:1, qs]
            q = part_rows(qkv_ref, i, 0) * jnp.asarray(0.125, BF)
            do = do_ref[qs, :]
            qh = [only_head(q, h) for h in range(heads)]
            dh = [only_head(do, h) for h in range(heads)]
            dq = [[] for _ in range(heads)]
            for j in js:
                ks = pl.ds(pl.multiple_of(j * n, n), n)
                same = segc_ref[ks, 0:1] == seg_q
                dk, dv = [], []
                for h in range(heads):
                    s = jnp.where(same, nt(kk[ks, :], qh[h]), NEG)
                    p = jnp.exp(s - lse_ref[h : h + 1, qs])
                    ds = (p * (nt(vv[ks, :], dh[h]) - delta[h : h + 1, qs])).astype(BF)
                    dv.append(nn(p.astype(BF), dh[h]))
                    dk.append(nn(ds, qh[h]))
                    dq[h].append(nn(kt[j, h * DH : (h + 1) * DH, :], ds))
                ak[ks, :] += sum_of(dk, jnp.add)
                av[ks, :] += sum_of(dv, jnp.add)
            dq = jnp.concatenate([sum_of(parts, jnp.add) for parts in dq], 0)
            put_lanes(dmix_ref, i, 0, jnp.transpose(dq) * 0.125)

        with_blocks(lo_ref, hi_ref, list_ref, i, groups, work)
        return carry

    lax.fori_loop(0, groups, per_query, 0)
    for i in range(groups):
        rows = slice(i * n, (i + 1) * n)
        dq = part_rows(dmix_ref, i, 0)
        dk = ak[rows, :].astype(BF)
        dv = av[rows, :].astype(BF)
        put_lanes(dmix_ref, i, 1, dk)
        put_lanes(dmix_ref, i, 2, dv)

        def project(part):
            dx = nt(dq, w_ref[part, :, :cols]) + nt(dk, kw[part])
            return dx + nt(dv, w_ref[part, :, 2 * cols : 3 * cols])

        put_projected(kept_ref, sent_ref, i, project)


def attend_back(lo, hi, mixed, att, lse, db, dp, segr, w):
    groups, pieces, thin, cols = att.shape
    heads = cols // DH
    n, rows = pieces * thin, groups * pieces * thin
    width = 2 * w.shape[1]
    return pl.pallas_call(
        partial(attend_back_kernel, heads),
        out_shape=(
            jax.ShapeDtypeStruct(mixed.shape, BF),
            jax.ShapeDtypeStruct((groups // 2, pieces, thin, width), F32),
            jax.ShapeDtypeStruct((groups // 2, pieces, thin, width), BF),
        ),
        in_specs=[SMEM, SMEM] + [VMEM] * 7,
        out_specs=(VMEM,) * 3,
        scratch_shapes=[
            pltpu.VMEM((groups, cols, n), BF),
            pltpu.VMEM((rows, cols), BF),
            pltpu.VMEM((rows, cols), BF),
            pltpu.VMEM((rows, cols), BF),
            pltpu.VMEM((8, rows), F32),
            pltpu.VMEM((rows, cols), F32),
            pltpu.VMEM((rows, cols), F32),
            pltpu.VMEM((2, width // 2, cols), BF),
            pltpu.VMEM((2, width // 2, cols), BF),
            pltpu.VMEM((rows, 8), F32),
            pltpu.SMEM((groups,), jnp.int32),
        ],
        compiler_params=params(18),
        cost_estimate=cost(70, 12 << 20),
        name="attend_back",
    )(lo, hi, mixed, att, lse, db, dp, segr, w)


def middle_kernel(s_ref, got_ref, x_ref, vec_ref, mid_ref, xb_ref):
    n, _, thin, width = s_ref.shape
    for i in range(n):
        x = x_rows(x_ref, i, thin).astype(F32)
        mid = group(s_ref, i).astype(F32) + group(got_ref, n - 1 - i).astype(F32) + x + vec_ref[0:1, :]
        put_rows(mid_ref, i, mid)
        normal, _ = normed(mid)
        put_rows(xb_ref, i, normal * vec_ref[1:2, :] + vec_ref[2:3, :])


def middle_rows(s, got, x, vec):
    return pl.pallas_call(
        middle_kernel,
        out_shape=(jax.ShapeDtypeStruct(s.shape, F32), jax.ShapeDtypeStruct(s.shape, BF)),
        in_specs=[VMEM] * 4,
        out_specs=(VMEM,) * 2,
        compiler_params=params(8),
        cost_estimate=cost(2, 4 << 20),
        name="middle_rows",
    )(s, got, x, vec)


def middle_back_kernel(s_ref, got_ref, mid_ref, g_ref, vec_ref, dmid_ref, db_ref, sum_ref):
    n = s_ref.shape[0]
    for i in range(n):
        dxb = group(s_ref, i).astype(F32) + group(got_ref, n - 1 - i).astype(F32)
        normal, rstd = normed(group(mid_ref, i))
        grad = group(g_ref, i).astype(F32)
        dmid = grad + normed_back(dxb, normal, rstd, vec_ref[...])
        low = dmid.astype(BF)
        put_rows(dmid_ref, i, dmid)
        put_rows(db_ref, i, low)
        if i == 0:
            sum_ref[0:1, :] = jnp.sum(low.astype(F32), 0, keepdims=True)
            sum_ref[1:2, :] = jnp.sum(dxb * normal, 0, keepdims=True)
            sum_ref[2:3, :] = jnp.sum(dxb, 0, keepdims=True)
            sum_ref[3:4, :] = jnp.sum(grad, 0, keepdims=True)


def middle_back(s, got, mid, g, vec):
    return pl.pallas_call(
        middle_back_kernel,
        out_shape=(
            jax.ShapeDtypeStruct(s.shape, F32),
            jax.ShapeDtypeStruct(s.shape, BF),
            jax.ShapeDtypeStruct((4, s.shape[-1]), F32),
        ),
        in_specs=[VMEM] * 5,
        out_specs=(VMEM,) * 3,
        compiler_params=params(8),
        cost_estimate=cost(2, 5 << 20),
        name="middle_back",
    )(s, got, mid, g, vec)


def add_kernel(kept_ref, got_ref, *out_refs):
    at = 0
    for ref in out_refs:
        for i in range(ref.shape[0]):
            put_rows(ref, i, group(kept_ref, at) + group(got_ref, at).astype(F32))
            at += 1


def core_sum(kept, sent, split):
    got = xor_swap(sent, "ctx", 1)
    return pl.pallas_call(
        add_kernel,
        out_shape=[jax.ShapeDtypeStruct((n,) + kept.shape[1:], BF) for n in split],
        in_specs=[VMEM] * 2,
        out_specs=[VMEM] * len(split),
        compiler_params=params(6),
        cost_estimate=cost(1, 4 << 20),
        name="add_rows",
    )(kept, got)


def first_back_kernel(
    s_ref, got_ref, x_ref, dmid_ref, mid_ref, mlp_ref, mlpgot_ref, vec_ref, out_ref
):
    thin = s_ref.shape[2]
    pieces = out_ref.shape[0]
    result = group(mid_ref, 0) + group(mlp_ref, 0).astype(F32) + group(mlpgot_ref, 0).astype(F32)
    result = result + vec_ref[1:2, :]
    out_ref[:, :thin, :] = result.astype(BF).reshape(pieces, thin, -1)
    dxa = group(s_ref, 0).astype(F32) + group(got_ref, 0).astype(F32)
    normal, rstd = normed(x_rows(x_ref, 0, thin).astype(F32))
    grad = group(dmid_ref, 0) + normed_back(dxa, normal, rstd, vec_ref[0:1, :])
    out_ref[:, thin:, :] = grad.astype(BF).reshape(pieces, thin, -1)


def first_back(s, got, x, dmid, mid, mlp, mlpgot, vec):
    _, pieces, thin, width = s.shape
    return pl.pallas_call(
        first_back_kernel,
        out_shape=jax.ShapeDtypeStruct((pieces, 2 * thin, width), BF),
        in_specs=[VMEM] * 8,
        out_specs=VMEM,
        compiler_params=params(8),
        cost_estimate=cost(20, 6 << 20),
        name="first_back",
    )(s, got, x, dmid, mid, mlp, mlpgot, vec)


def pieces_kernel(own_ref, got_ref, vec_ref, out_ref):
    blocks, r = out_ref.shape[0], out_ref.shape[1] - SPARE
    for b in range(blocks):
        part = slice(b * r, (b + 1) * r)
        out_ref[b, :r, :] = (own_ref[part, :].astype(F32) + got_ref[part, :].astype(F32)).astype(BF)
        last = slice(blocks * r, blocks * r + 2)
        out_ref[b, r : r + 2, :] = (
            own_ref[last, :].astype(F32) + got_ref[last, :].astype(F32)
        ).astype(BF)
        out_ref[b, r + 2 :, :] = vec_ref[...].astype(BF)


def grad_pieces(stay, go, vec, blocks):
    rows = stay.shape[0] - SPARE
    if lax.axis_size("fsdp") == 2 and rows // blocks % 16 == 0:
        return pl.pallas_call(
            pieces_kernel,
            out_shape=jax.ShapeDtypeStruct((blocks, rows // blocks + SPARE, stay.shape[1]), BF),
            in_specs=[VMEM] * 3,
            out_specs=VMEM,
            compiler_params=params(6),
            cost_estimate=cost(1, 2 << 20),
            name="grad_pieces",
        )(stay, xor_swap(go, "fsdp", 1), vec)
    last = lax.psum(stay[rows : rows + 2].astype(F32), "fsdp")
    split = jnp.concatenate([stay[:rows], go[:rows]], 0).reshape(
        lax.axis_size("fsdp"), -1, stay.shape[1]
    )
    own = lax.psum_scatter(split.astype(F32), "fsdp", scatter_dimension=0, tiled=False)
    own = own.reshape(blocks, -1, own.shape[-1])
    small = jnp.concatenate([last, vec], 0)
    small = jnp.broadcast_to(small, (blocks,) + small.shape)
    return jnp.concatenate([own, small], 1).astype(BF)


def weight_part(ref, part):
    w = ref[:, part]
    return w.reshape(w.shape[0] * w.shape[1], w.shape[2])


def mlp_kernel(
    xo_ref,
    xp_ref,
    go_ref,
    gp_ref,
    m_ref,
    b_ref,
    hidden_ref,
    dpre_ref,
    kept_ref,
    sent_ref,
):
    first = xo_ref.shape[0]
    b = bias_row(b_ref, 3)
    for i in range(2 * first):
        own = i < first
        pre = nn(group(xo_ref if own else xp_ref, i % first), weight_part(m_ref, 0)) + b
        dhidden = nn(group(go_ref if own else gp_ref, i % first), weight_part(m_ref, 1))
        share = 0.5 * (1.0 + lax.erf(pre * (0.5**0.5)))
        density = jnp.exp(pre * pre * -0.5) * ((0.5 / 3.141592653589793) ** 0.5)
        n = pre.shape[0]
        hidden_ref[i * n : (i + 1) * n, :] = (pre * share).astype(BF)
        dpre = (dhidden * (share + pre * density)).astype(BF)
        dpre_ref[i * n : (i + 1) * n, :] = dpre
        put_rows(kept_ref if own else sent_ref, i % first, nt(dpre, weight_part(m_ref, 0)))


def mlp_block(xo, xp, go, gp, m, b):
    blocks, pieces, thin, width = xo.shape
    low = jax.ShapeDtypeStruct((2 * blocks * pieces * thin, m.shape[-1]), BF)
    return pl.pallas_call(
        mlp_kernel,
        out_shape=(low, low, jax.ShapeDtypeStruct(xo.shape, F32), jax.ShapeDtypeStruct(xo.shape, BF)),
        in_specs=[VMEM] * 6,
        out_specs=(VMEM,) * 4,
        compiler_params=params(12),
        cost_estimate=cost(7, 12 << 20),
        name="mlp_block",
    )(xo, xp, go, gp, m, b)


def mlp_grads_kernel(
    xo_ref,
    xp_ref,
    dpre_ref,
    go_ref,
    gp_ref,
    hidden_ref,
    m_ref,
    grad_ref,
    kept_ref,
    sent_ref,
    sum_ref,
):
    first, width = xo_ref.shape[0], xo_ref.shape[3]
    half = width // 2
    rows = dpre_ref.shape[0]
    n = rows // 2

    def half_grads(i, carry):
        lanes = pl.ds(pl.multiple_of(i * half, 128), half)
        xo, xp = (ref[:, :, :, lanes].reshape(n, half) for ref in (xo_ref, xp_ref))
        up = tn(xo, dpre_ref[:n, :]) + tn(xp, dpre_ref[n:, :])
        grad_ref[:, i, 0] = up.astype(BF).reshape((-1,) + grad_ref.shape[3:])
        go, gp = (ref[:, :, :, lanes].reshape(n, half) for ref in (go_ref, gp_ref))
        down = tn(go, hidden_ref[:n, :]) + tn(gp, hidden_ref[n:, :])
        grad_ref[:, i, 1] = down.astype(BF).reshape((-1,) + grad_ref.shape[3:])
        return carry

    lax.fori_loop(0, 2, half_grads, 0)
    size = n // first
    for i in range(2 * first):
        result = nt(hidden_ref[i * size : (i + 1) * size, :], weight_part(m_ref, 1))
        put_rows(kept_ref if i < first else sent_ref, i % first, result)
    sum_ref[...] = jnp.sum(dpre_ref[...].astype(F32), 0, keepdims=True)


def mlp_grads(xo, xp, dpre, go, gp, hidden, m):
    return pl.pallas_call(
        mlp_grads_kernel,
        out_shape=(
            jax.ShapeDtypeStruct((m.shape[0] // 2, 2) + m.shape[1:], BF),
            jax.ShapeDtypeStruct(xo.shape, F32),
            jax.ShapeDtypeStruct(xo.shape, BF),
            jax.ShapeDtypeStruct((1, dpre.shape[1]), F32),
        ),
        in_specs=[VMEM] * 7,
        out_specs=(VMEM,) * 4,
        compiler_params=params(14),
        cost_estimate=cost(6, 12 << 20),
        name="mlp_grads",
    )(xo, xp, dpre, go, gp, hidden, m)


def attend_grads_kernel(
    flip_ref,
    sum_ref,
    norm_ref,
    dmix_ref,
    do_ref,
    dp_ref,
    att_ref,
    kept_ref,
    sent_ref,
    xo_ref,
    xp_ref,
    stay_ref,
    go_ref,
    vec_ref,
    xa,
):
    first, _, thin, width = kept_ref.shape
    rows, cols = att_ref.shape
    half = width // 2
    n = do_ref.shape[0]
    block = rows // (2 * first)
    gain = bias = jnp.zeros((1, width), F32)
    for i in range(2 * first):
        x_ref, g_ref = (xo_ref, kept_ref) if i < first else (xp_ref, sent_ref)
        normal, _ = normed(x_rows(x_ref, i % first, thin).astype(F32))
        xa[i * block : (i + 1) * block, :] = (
            normal * norm_ref[0:1, :] + norm_ref[1:2, :]
        ).astype(BF)
        dx = group(g_ref, i % first).astype(F32)
        gain = gain + jnp.sum(dx * normal, 0, keepdims=True)
        bias = bias + jnp.sum(dx, 0, keepdims=True)
    vec_ref[0:1, :] = gain
    vec_ref[1:2, :] = bias
    totals = [
        jnp.sum(dmix_ref[:, lanes_of(dmix_ref, c)].astype(F32), 0, keepdims=True).astype(BF)
        for c in (0, 2)
    ]

    def half_grads(i, out_ref):
        lanes = pl.ds(pl.multiple_of(i * half, 128), half)
        grads = tn(xa[:, lanes], dmix_ref[...]).astype(BF)
        for c in range(3):
            out_ref[:half, c * cols : (c + 1) * cols] = grads[:, lanes_of(dmix_ref, c)]
        out = tn(do_ref[:, lanes], att_ref[:n, :]) + tn(dp_ref[:, lanes], att_ref[n:, :])
        out_ref[:half, 3 * cols : 4 * cols] = out.astype(BF)
        out_ref[half : half + SPARE, :] = jnp.zeros((SPARE, out_ref.shape[1]), BF)
        for place, total in enumerate(totals):
            out_ref[half : half + 1, place * cols : (place + 1) * cols] = total
        out_ref[half + 1 : half + 2, : sum_ref.shape[1]] = sum_ref[...].astype(BF)

    half_grads(flip_ref[0], stay_ref)
    half_grads(1 - flip_ref[0], go_ref)


def attend_grads(flip, sums, norms, dmix, do, dp, att, kept, sent, xo, xp):
    width = do.shape[1]
    shape = jax.ShapeDtypeStruct((width // 2 + SPARE, 4 * att.shape[1]), BF)
    return pl.pallas_call(
        attend_grads_kernel,
        out_shape=(shape, shape, jax.ShapeDtypeStruct((2, width), F32)),
        in_specs=[SMEM] + [VMEM] * 10,
        out_specs=(VMEM,) * 3,
        scratch_shapes=[pltpu.VMEM((att.shape[0], width), BF)],
        compiler_params=params(14),
        cost_estimate=cost(6, 12 << 20),
        name="attend_grads",
    )(flip, sums, norms, dmix, do, dp, att, kept, sent, xo, xp)


def exact_low(x):
    one = lax.reduce_precision(x, 8, 7)
    two = lax.reduce_precision(x - one, 8, 7)
    return jnp.concatenate([one, two, x - one - two], 0).astype(BF)


def per_device(
    inputs,
    segments,
    ln1_gain,
    ln1_bias,
    query_key_value_weight,
    b_qv,
    output_weight,
    output_bias,
    ln2_gain,
    ln2_bias,
    up_weight,
    up_bias,
    down_weight,
    down_bias,
    out_grad,
):
    z = lax.axis_index("tp")
    ctx = lax.axis_index("ctx")
    planes = lax.axis_size("tp")
    thin, width = inputs.shape[1], inputs.shape[2]
    ds, _, cols = query_key_value_weight.shape
    hidden_cols = up_weight.shape[1]

    vectors = jnp.stack([ln1_gain, ln1_bias, output_bias, ln2_gain, ln2_bias, down_bias])
    rows_of = lambda a: a.reshape(-1, a.shape[-1])

    biases = jnp.pad(b_qv.reshape(1, -1), ((0, 0), (0, width - 2 * cols)))
    biases = [exact_low(biases), exact_low(up_bias.reshape(1, -1)), jnp.zeros((SPARE - 6, width), BF)]
    a_shard = jnp.concatenate(
        [query_key_value_weight.reshape(ds, 3 * cols), jnp.transpose(output_weight)], 1
    )
    a_shard = jnp.concatenate([a_shard] + biases, 0)
    labels = jnp.pad(segments.astype(BF)[:, None, :], ((0, 0), (0, SPARE - 1), (0, width - thin)))
    own = rows_over_z(jnp.concatenate([after(inputs, a_shard), labels, out_grad], 1))
    x_own, g_own = own[:, : thin + SPARE], own[:, thin + SPARE :]
    got = [send_turned(a_shard, k) for k in range(planes)]
    a_rows = place([g[:ds] for g in got], z).reshape(-1, width)
    biases = got[0][ds:]
    w_attn = weight_over_x(a_rows)
    x_pair, x_far = gather_ctx(after(x_own, w_attn)[None])
    g_own = after(g_own, x_pair)[None]

    m_shard = jnp.concatenate([up_weight, jnp.transpose(down_weight)], 0)
    m_shard = send_turned(after(m_shard, a_rows), 0)
    m_all = lax.all_gather(m_shard, ("fsdp", "tp"), axis=0, tiled=True)
    m_all = m_all.reshape(-1, 2, ds, hidden_cols)
    aligned = ds % 16 == 0 and m_all.shape[0] % 2 == 0
    if not aligned:
        m_all = m_all.reshape(2, -1, 2, ds, hidden_cols).transpose(0, 2, 1, 3, 4)
        m_all = m_all.reshape(2, 2, width // 2, hidden_cols)

    mixed, segr, lo, hi = qkv(x_pair, x_far, vectors, biases, w_attn, cols, thin)
    g_got = xor_swap(g_own, "ctx", 2)
    attended, lse, kept, sent = attend(lo, hi, mixed, segr, w_attn)
    g_got, kept, sent = lax.optimization_barrier((g_got, kept, sent))
    g_pair = jnp.concatenate([g_own, g_got], 0)
    g_far = xor_swap(g_pair, "ctx", 1)
    (s,) = core_sum(kept, sent, (2,))
    got = after(xor_swap(s, "ctx", 2), m_all)
    middle, xb_pair = middle_rows(s, got, x_pair, vectors[2:5])
    xb_far = xor_swap(xb_pair, "ctx", 1)

    hidden, dpre, kept, sent = mlp_block(xb_pair, xb_far, g_pair, g_far, m_all, biases)
    (s,) = core_sum(kept, sent, (2,))
    m_grad, mlp_kept, mlp_sent, dpre_sum = mlp_grads(
        xb_pair, xb_far, after(dpre, s), g_pair, g_far, hidden, m_all
    )
    got = xor_swap(s, "ctx", 2)
    mlp_s, mlp_low = core_sum(mlp_kept, after(mlp_sent, got), (1, 1))
    dmid, db_pair, sums_two = middle_back(
        s, after(got, dpre_sum), middle, g_pair, vectors[3:4]
    )
    db_far = xor_swap(db_pair, "ctx", 1)
    if not aligned:
        m_grad = m_grad[0].transpose(1, 0, 2, 3).reshape(2, -1, planes, ds, hidden_cols)
        m_grad = m_grad.transpose(2, 1, 0, 3, 4)
    m_sums = lax.psum_scatter(m_grad, "tp", scatter_dimension=0, tiled=False)
    mlp_got = xor_swap(after(mlp_low, db_far), "ctx", 2)

    dmix, kept, sent = attend_back(
        lo, hi, mixed, attended, lse, db_pair, db_far, segr, w_attn
    )
    s, low = core_sum(kept, after(sent, mlp_got), (1, 1))
    flip = lax.axis_index("fsdp") if lax.axis_size("fsdp") == 2 else 0
    got = xor_swap(low, "ctx", 2)
    g_stay, g_go, sums_one = attend_grads(
        jnp.full((1,), flip, jnp.int32),
        dpre_sum,
        vectors[0:2],
        after(rows_of(dmix), s),
        rows_of(db_pair),
        rows_of(db_far),
        rows_of(attended),
        kept,
        sent,
        x_pair,
        x_far,
    )
    vec = jnp.concatenate([vectors[0:1], vectors[5:6]], 0)
    shared = jnp.concatenate([sums_one, sums_two], 0)
    if lax.axis_size("fsdp") == 2:
        shared = shared + xor_swap(shared, "fsdp", 1)
    else:
        shared = lax.psum(shared, "fsdp")
    shared = shared + xor_swap(shared, "ctx", 1)
    both = first_back(s, after(got, shared), x_pair, dmid, middle, mlp_s, mlp_got, vec)
    shared = after(shared, both)
    shared = shared + xor_swap(shared, "ctx", 2)
    a_low = grad_pieces(g_stay, g_go, shared, planes)

    both = rows_over_z(both)
    output, input_grad = both[:, :thin], both[:, thin:].astype(F32)
    m_z = m_sums
    if lax.axis_size("fsdp") == 2:
        x = lax.axis_index("fsdp")
        m_got = xor_swap(pick(after(m_sums, a_low), x ^ 1), "fsdp", 1)
        m_sums = (pick(m_sums, x).astype(F32) + m_got.astype(F32)).astype(BF)
    else:
        m_sums = lax.psum_scatter(m_sums.astype(F32), "fsdp", scatter_dimension=0, tiled=False)
        m_sums = m_sums.astype(BF)
    m_back = send_back(m_sums.reshape(2 * ds, hidden_cols), 0)
    *got, m_back = lax.optimization_barrier((*scatter_blocks(a_low, m_z, both), m_back))

    g_attn = sum(g.astype(F32) for g in got)
    grad_qkv = g_attn[:ds, : 3 * cols].reshape(ds, 3, cols)
    grad_out = jnp.transpose(g_attn[:ds, 3 * cols :])
    mine, shared = g_attn[ds : ds + 2], g_attn[ds + 2 :]
    g_mlp = m_back.astype(F32)
    grad_up, grad_down = g_mlp[:ds], jnp.transpose(g_mlp[ds:])
    return (
        output,
        input_grad,
        shared[0],
        shared[1],
        grad_qkv,
        mine[0, : 2 * cols].reshape(2, cols),
        grad_out,
        shared[2],
        shared[3],
        shared[4],
        grad_up,
        mine[1, :hidden_cols],
        grad_down,
        shared[5],
    )


def solution(mesh):
    in_specs = (
        P("fsdp", ("ctx", "tp"), None),
        P("fsdp", ("ctx", "tp")),
        P(),
        P(),
        P(("fsdp", "ctx"), None, "tp"),
        P(None, "tp"),
        P("tp", ("fsdp", "ctx")),
        P(),
        P(),
        P(),
        P(("fsdp", "ctx"), "tp"),
        P("tp"),
        P("tp", ("fsdp", "ctx")),
        P(),
        P("fsdp", ("ctx", "tp"), None),
    )
    out_specs = (
        P("fsdp", ("ctx", "tp"), None),
        P("fsdp", ("ctx", "tp"), None),
        P(),
        P(),
        P(("fsdp", "ctx"), None, "tp"),
        P(None, "tp"),
        P("tp", ("fsdp", "ctx")),
        P(),
        P(),
        P(),
        P(("fsdp", "ctx"), "tp"),
        P("tp"),
        P("tp", ("fsdp", "ctx")),
        P(),
    )
    return jax.shard_map(
        per_device, mesh=mesh, in_specs=in_specs, out_specs=out_specs, check_vma=False
    )
```

```python
from functools import partial

import jax
import jax.numpy as jnp
from jax import lax
from jax.experimental import pallas as pl
from jax.experimental.pallas import tpu as pltpu
from jax.sharding import PartitionSpec as P

DH = 64
EPS = 1e-06
BF = jnp.bfloat16
F32 = jnp.float32
NEG = -1e30
SPARE = 8
VMEM = pl.BlockSpec(memory_space=pltpu.VMEM)
SMEM = pl.BlockSpec(memory_space=pltpu.SMEM)


def after(x, *deps):
    return lax.optimization_barrier((x,) + deps)[0]


def xor_swap(x, axis, k):
    n = lax.axis_size(axis)
    return lax.ppermute(x, axis, [(i, i ^ k) for i in range(n)])


def turn_pairs(n, k):
    return [(a * n + b, b * n + (a ^ k)) for a in range(n) for b in range(n)]


def send_turned(x, k):
    return lax.ppermute(x, ("ctx", "tp"), turn_pairs(lax.axis_size("tp"), k))


def send_back(x, k):
    pairs = turn_pairs(lax.axis_size("tp"), k)
    return lax.ppermute(x, ("ctx", "tp"), [(d, s) for s, d in pairs])


def hop_pairs(n, k):
    pairs = []
    for a in range(n):
        for q in range(n):
            f, low = (q ^ k) // 2, (q ^ k) % 2
            pairs.append((a * n + q, ((a // 2) * 2 + low) * n + (a ^ (2 * f))))
    return pairs


def scatter_blocks(pieces, *late):
    n = lax.axis_size("tp")
    y, q = lax.axis_index("ctx") // 2, lax.axis_index("tp")
    split = pieces.reshape((2, 2) + pieces.shape[1:])
    got = xor_swap(pick(split, y ^ 1), "ctx", 2)
    four = after(jnp.concatenate([pick(split, y), got], 0), *late)
    return [lax.ppermute(pick(four, q ^ k), ("ctx", "tp"), hop_pairs(n, k)) for k in range(n)]


def rows_over_z(arr):
    return lax.all_to_all(arr, "tp", 0, 0, tiled=True)


def place(pieces, first):
    out = jnp.zeros((len(pieces),) + pieces[0].shape, pieces[0].dtype)
    for k, piece in enumerate(pieces):
        out = lax.dynamic_update_index_in_dim(out, piece, first ^ k, 0)
    return out


def pick(arr, index):
    return lax.dynamic_index_in_dim(arr, index, 0, keepdims=False)


def gather_ctx(own):
    half = jnp.concatenate([own, xor_swap(own, "ctx", 2)], 0)
    return half, xor_swap(half, "ctx", 1)


def weight_over_x(rows):
    if lax.axis_size("fsdp") == 2:
        got = xor_swap(rows, "fsdp", 1)
        first = lax.axis_index("fsdp") == 0
        return jnp.stack([jnp.where(first, rows, got), jnp.where(first, got, rows)])
    every = lax.all_gather(rows, "fsdp", axis=0, tiled=True)
    return every.reshape(2, -1, every.shape[1])


def nt(a, b):
    return lax.dot_general(a, b, (((1,), (1,)), ((), ())), preferred_element_type=F32)


def nn(a, b):
    return lax.dot_general(a, b, (((1,), (0,)), ((), ())), preferred_element_type=F32)


def tn(a, b):
    return lax.dot_general(a, b, (((0,), (0,)), ((), ())), preferred_element_type=F32)


def params(limit, steps=None):
    return pltpu.CompilerParams(vmem_limit_bytes=limit << 20)


def cost(micros, nbytes):
    return pl.CostEstimate(
        flops=int(micros * 0.2 * 10**9), transcendentals=0, bytes_accessed=1024
    )


def normed(x):
    n = x.shape[-1]
    centred = x - jnp.sum(x, -1, keepdims=True) * (1.0 / n)
    rstd = lax.rsqrt(jnp.sum(centred * centred, -1, keepdims=True) * (1.0 / n) + EPS)
    return centred * rstd, rstd


def normed_back(grad, normal, rstd, gain):
    n = grad.shape[-1]
    scaled = grad * gain
    one = jnp.sum(scaled, -1, keepdims=True) * (1.0 / n)
    two = jnp.sum(scaled * normal, -1, keepdims=True) * (1.0 / n)
    return rstd * (scaled - one - normal * two)


def bias_row(ref, row):
    parts = ref[row : row + 3, :].astype(F32)
    return parts[0:1] + parts[1:2] + parts[2:3]


def qkv_kernel(
    cols,
    xo_ref,
    xp_ref,
    vec_ref,
    b_ref,
    w_ref,
    qkv_ref,
    seg_ref,
    lo_ref,
    hi_ref,
):
    first, pieces = xo_ref.shape[0], xo_ref.shape[1]
    thin, width = qkv_ref.shape[2], xo_ref.shape[3]
    half = width // 2
    b = bias_row(b_ref, 0)
    for i in range(2 * first):
        x_ref = xo_ref if i < first else xp_ref
        normal, _ = normed(x_rows(x_ref, i % first, thin).astype(F32))
        xa = (normal * vec_ref[0:1, :] + vec_ref[1:2, :]).astype(BF)
        mixed = nn(xa[:, :half], w_ref[0, :, : 3 * cols]) + nn(xa[:, half:], w_ref[1, :, : 3 * cols])
        parts = (
            mixed[:, :cols] + b[:, :cols],
            mixed[:, cols : 2 * cols],
            mixed[:, 2 * cols :] + b[:, cols : 2 * cols],
        )
        for c, part in enumerate(parts):
            put_lanes(qkv_ref, i, c, part)
        labels = [
            x_ref[i % first, k, thin : thin + SPARE, :thin].astype(F32)[0:1, :]
            for k in range(pieces)
        ]
        labels = jnp.concatenate(labels, 1)
        seg_ref[:, i * pieces * thin : (i + 1) * pieces * thin] = jnp.broadcast_to(
            labels, (8, pieces * thin)
        )
        lo_ref[i] = jnp.min(labels).astype(jnp.int32)
        hi_ref[i] = jnp.max(labels).astype(jnp.int32)


def qkv(xo, xp, vec, b, w, cols, thin):
    first, pieces, _, _ = xo.shape
    bound = jax.ShapeDtypeStruct((2 * first,), jnp.int32)
    return pl.pallas_call(
        partial(qkv_kernel, cols),
        out_shape=(
            jax.ShapeDtypeStruct((2 * first, pieces, thin, 4 * cols), BF),
            jax.ShapeDtypeStruct((8, 2 * first * pieces * thin), F32),
            bound,
            bound,
        ),
        in_specs=[VMEM] * 5,
        out_specs=(VMEM,) * 2 + (SMEM,) * 2,
        compiler_params=params(12),
        cost_estimate=cost(4, 6 << 20),
        name="qkv",
    )(xo, xp, vec, b, w)


def head_mask(h, width):
    lane = lax.broadcasted_iota(jnp.int32, (1, width), 1)
    return (lane >= h * DH) & (lane < (h + 1) * DH)


def only_head(x, h):
    return jnp.where(head_mask(h, x.shape[1]), x, jnp.zeros_like(x))


def x_rows(ref, i, thin):
    return ref[i, :, :thin, :].reshape(-1, ref.shape[3])


def group(ref, i):
    return ref[i].reshape(ref.shape[1] * ref.shape[2], ref.shape[3])


def put_rows(ref, i, value):
    ref[i] = value.astype(ref.dtype).reshape(ref.shape[1:])


def lanes_of(ref, part):
    cols = ref.shape[-1] // 4
    wide = ref.shape[-1] // 3
    return slice(part * wide, part * wide + cols)


def part_rows(ref, i, part):
    value = ref[i, :, :, lanes_of(ref, part)]
    return value.reshape(-1, value.shape[-1])


def put_lanes(ref, i, part, value):
    ref[i, :, :, lanes_of(ref, part)] = value.astype(ref.dtype).reshape(
        ref.shape[1:3] + value.shape[1:]
    )


def turned(x):
    return jnp.transpose(x.astype(F32)).astype(x.dtype)


def with_blocks(lo_ref, hi_ref, list_ref, i, groups, work):
    count = jnp.int32(0)
    for j in range(groups):
        on = (hi_ref[i] >= lo_ref[j]) & (lo_ref[i] <= hi_ref[j])

        @pl.when(on)
        def _():
            list_ref[count] = j

        count = count + on.astype(jnp.int32)
    for number, less in ((2, 0), (groups, 2)):

        @pl.when((count > less) & (count <= number))
        def _():
            js = [list_ref[jnp.minimum(t, count - 1)] for t in range(number)]
            work(js, count == number)


def put_projected(kept_ref, sent_ref, i, project):
    first = kept_ref.shape[0]
    out = kept_ref if i < first else sent_ref
    half = out.shape[3] // 2
    for part in range(2):
        out[i % first, :, :, part * half : (part + 1) * half] = (
            project(part).astype(out.dtype).reshape(out.shape[1:3] + (half,))
        )


def attend_kernel(
    heads,
    lo_ref,
    hi_ref,
    qkv_ref,
    segr_ref,
    w_ref,
    att_ref,
    lse_ref,
    kept_ref,
    sent_ref,
    kk,
    vt,
    ow,
    segc_ref,
    list_ref,
):
    groups = qkv_ref.shape[0]
    n = qkv_ref.shape[1] * qkv_ref.shape[2]
    cols = qkv_ref.shape[3] // 4
    segc_ref[...] = jnp.transpose(segr_ref[...])
    ow[...] = w_ref[:, :, 3 * cols :]
    for i in range(groups):
        kk[i * n : (i + 1) * n, :] = part_rows(qkv_ref, i, 1)
        vt[i] = turned(part_rows(qkv_ref, i, 2))

    def per_query(i, carry):
        qs = pl.ds(pl.multiple_of(i * n, n), n)

        def work(js, last):
            seg_q = segr_ref[0:1, qs]
            seg_last = jnp.where(last, seg_q, -1.0)
            q = part_rows(qkv_ref, i, 0) * jnp.asarray(0.125, BF)
            places = [pl.ds(pl.multiple_of(j * n, n), n) for j in js]
            same = [segc_ref[ks, 0:1] == seg_q for ks in places[:-1]]
            same.append(segc_ref[places[-1], 0:1] == seg_last)
            outs = []
            for h in range(heads):
                qh = only_head(q, h)
                scores = [
                    jnp.where(mask, nt(kk[ks, :], qh), NEG) for ks, mask in zip(places, same)
                ]
                top = [jnp.max(s, 0, keepdims=True) for s in scores]
                top = sum_of(top, jnp.maximum)
                total, out = [], []
                for s, j in zip(scores, js):
                    p = jnp.exp(s - top)
                    total.append(jnp.sum(p, 0, keepdims=True))
                    out.append(nn(vt[j, h * DH : (h + 1) * DH, :], p.astype(BF)))
                total = sum_of(total, jnp.add)
                outs.append(sum_of(out, jnp.add) * (1.0 / total))
                lse_ref[h : h + 1, qs] = top + jnp.log(total)
            out = jnp.transpose(jnp.concatenate(outs, 0))
            put_rows(att_ref, i, jnp.where(segc_ref[qs, 0:1] > 0, out, 0.0))

        with_blocks(lo_ref, hi_ref, list_ref, i, groups, work)
        return carry

    lax.fori_loop(0, groups, per_query, 0)
    for i in range(groups):
        att = group(att_ref, i)
        put_projected(kept_ref, sent_ref, i, lambda part: nt(att, ow[part]))


def sum_of(values, join):
    total = values[0]
    for value in values[1:]:
        total = join(total, value)
    return total


def attend(lo, hi, mixed, segr, w):
    groups, pieces, thin, _ = mixed.shape
    cols = mixed.shape[3] // 4
    heads = cols // DH
    n, rows = pieces * thin, groups * pieces * thin
    width = 2 * w.shape[1]
    return pl.pallas_call(
        partial(attend_kernel, heads),
        out_shape=(
            jax.ShapeDtypeStruct((groups, pieces, thin, cols), BF),
            jax.ShapeDtypeStruct((8, rows), F32),
            jax.ShapeDtypeStruct((groups // 2, pieces, thin, width), F32),
            jax.ShapeDtypeStruct((groups // 2, pieces, thin, width), BF),
        ),
        in_specs=[SMEM, SMEM] + [VMEM] * 3,
        out_specs=(VMEM,) * 4,
        scratch_shapes=[
            pltpu.VMEM((rows, cols), BF),
            pltpu.VMEM((groups, cols, n), BF),
            pltpu.VMEM((2, width // 2, cols), BF),
            pltpu.VMEM((rows, 8), F32),
            pltpu.SMEM((groups,), jnp.int32),
        ],
        compiler_params=params(16),
        cost_estimate=cost(11, 8 << 20),
        name="attend",
    )(lo, hi, mixed, segr, w)


def attend_back_kernel(
    heads,
    lo_ref,
    hi_ref,
    qkv_ref,
    att_ref,
    lse_ref,
    db_ref,
    dp_ref,
    segr_ref,
    w_ref,
    dmix_ref,
    kept_ref,
    sent_ref,
    kt,
    kk,
    vv,
    do_ref,
    delta,
    ak,
    av,
    ow,
    kw,
    segc_ref,
    list_ref,
):
    groups = qkv_ref.shape[0]
    n = qkv_ref.shape[1] * qkv_ref.shape[2]
    cols = qkv_ref.shape[3] // 4
    half = w_ref.shape[1]
    segc_ref[...] = jnp.transpose(segr_ref[...])
    ow[...] = w_ref[:, :, 3 * cols :]
    kw[...] = w_ref[:, :, cols : 2 * cols]
    ak[...] = jnp.zeros_like(ak)
    av[...] = jnp.zeros_like(av)
    for i in range(groups):
        rows = slice(i * n, (i + 1) * n)
        kk[rows, :] = part_rows(qkv_ref, i, 1)
        vv[rows, :] = part_rows(qkv_ref, i, 2)
        kt[i] = turned(part_rows(qkv_ref, i, 1))
        grad = group(db_ref, i) if i < groups // 2 else group(dp_ref, i - groups // 2)
        out_back = nn(grad[:, :half], ow[0]) + nn(grad[:, half:], ow[1])
        do = jnp.where(segc_ref[rows, 0:1] > 0, out_back, 0.0).astype(BF)
        do_ref[rows, :] = do
        prod = jnp.transpose(do.astype(F32) * group(att_ref, i).astype(F32))
        for h in range(heads):
            delta[h : h + 1, rows] = jnp.sum(prod[h * DH : (h + 1) * DH, :], 0, keepdims=True)

    def per_query(i, carry):
        qs = pl.ds(pl.multiple_of(i * n, n), n)

        def work(js, last):
            seg_q = segr_ref[0:1, qs]
            seg_last = jnp.where(last, seg_q, -1.0)
            q = part_rows(qkv_ref, i, 0) * jnp.asarray(0.125, BF)
            do = do_ref[qs, :]
            qh = [only_head(q, h) for h in range(heads)]
            dh = [only_head(do, h) for h in range(heads)]
            dq = [[] for _ in range(heads)]
            for t, j in enumerate(js):
                ks = pl.ds(pl.multiple_of(j * n, n), n)
                same = segc_ref[ks, 0:1] == (seg_q if t < len(js) - 1 else seg_last)
                dk, dv = [], []
                for h in range(heads):
                    s = jnp.where(same, nt(kk[ks, :], qh[h]), NEG)
                    p = jnp.exp(s - lse_ref[h : h + 1, qs])
                    ds = (p * (nt(vv[ks, :], dh[h]) - delta[h : h + 1, qs])).astype(BF)
                    dv.append(nn(p.astype(BF), dh[h]))
                    dk.append(nn(ds, qh[h]))
                    dq[h].append(nn(kt[j, h * DH : (h + 1) * DH, :], ds))
                ak[ks, :] += sum_of(dk, jnp.add)
                av[ks, :] += sum_of(dv, jnp.add)
            dq = jnp.concatenate([sum_of(parts, jnp.add) for parts in dq], 0)
            put_lanes(dmix_ref, i, 0, jnp.transpose(dq) * 0.125)

        with_blocks(lo_ref, hi_ref, list_ref, i, groups, work)
        return carry

    lax.fori_loop(0, groups, per_query, 0)
    for i in range(groups):
        rows = slice(i * n, (i + 1) * n)
        dq = part_rows(dmix_ref, i, 0)
        dk = ak[rows, :].astype(BF)
        dv = av[rows, :].astype(BF)
        put_lanes(dmix_ref, i, 1, dk)
        put_lanes(dmix_ref, i, 2, dv)

        def project(part):
            dx = nt(dq, w_ref[part, :, :cols]) + nt(dk, kw[part])
            return dx + nt(dv, w_ref[part, :, 2 * cols : 3 * cols])

        put_projected(kept_ref, sent_ref, i, project)


def attend_back(lo, hi, mixed, att, lse, db, dp, segr, w):
    groups, pieces, thin, cols = att.shape
    heads = cols // DH
    n, rows = pieces * thin, groups * pieces * thin
    width = 2 * w.shape[1]
    return pl.pallas_call(
        partial(attend_back_kernel, heads),
        out_shape=(
            jax.ShapeDtypeStruct(mixed.shape, BF),
            jax.ShapeDtypeStruct((groups // 2, pieces, thin, width), F32),
            jax.ShapeDtypeStruct((groups // 2, pieces, thin, width), BF),
        ),
        in_specs=[SMEM, SMEM] + [VMEM] * 7,
        out_specs=(VMEM,) * 3,
        scratch_shapes=[
            pltpu.VMEM((groups, cols, n), BF),
            pltpu.VMEM((rows, cols), BF),
            pltpu.VMEM((rows, cols), BF),
            pltpu.VMEM((rows, cols), BF),
            pltpu.VMEM((8, rows), F32),
            pltpu.VMEM((rows, cols), F32),
            pltpu.VMEM((rows, cols), F32),
            pltpu.VMEM((2, width // 2, cols), BF),
            pltpu.VMEM((2, width // 2, cols), BF),
            pltpu.VMEM((rows, 8), F32),
            pltpu.SMEM((groups,), jnp.int32),
        ],
        compiler_params=params(18),
        cost_estimate=cost(70, 12 << 20),
        name="attend_back",
    )(lo, hi, mixed, att, lse, db, dp, segr, w)


def middle_kernel(s_ref, got_ref, x_ref, vec_ref, mid_ref, xb_ref):
    n, _, thin, width = s_ref.shape
    for i in range(n):
        x = x_rows(x_ref, i, thin).astype(F32)
        mid = group(s_ref, i).astype(F32) + group(got_ref, n - 1 - i).astype(F32) + x + vec_ref[0:1, :]
        put_rows(mid_ref, i, mid)
        normal, _ = normed(mid)
        put_rows(xb_ref, i, normal * vec_ref[1:2, :] + vec_ref[2:3, :])


def middle_rows(s, got, x, vec):
    return pl.pallas_call(
        middle_kernel,
        out_shape=(jax.ShapeDtypeStruct(s.shape, F32), jax.ShapeDtypeStruct(s.shape, BF)),
        in_specs=[VMEM] * 4,
        out_specs=(VMEM,) * 2,
        compiler_params=params(8),
        cost_estimate=cost(2, 4 << 20),
        name="middle_rows",
    )(s, got, x, vec)


def middle_back_kernel(s_ref, got_ref, mid_ref, g_ref, vec_ref, dmid_ref, db_ref, sum_ref):
    n = s_ref.shape[0]

    def step(i, carry):
        dxb = group(s_ref, i).astype(F32) + group(got_ref, n - 1 - i).astype(F32)
        normal, rstd = normed(group(mid_ref, i))
        grad = group(g_ref, i).astype(F32)
        dmid = grad + normed_back(dxb, normal, rstd, vec_ref[...])
        low = dmid.astype(BF)
        put_rows(dmid_ref, i, dmid)
        put_rows(db_ref, i, low)

        @pl.when(i == 0)
        def _():
            sum_ref[0:1, :] = jnp.sum(low.astype(F32), 0, keepdims=True)
            sum_ref[1:2, :] = jnp.sum(dxb * normal, 0, keepdims=True)
            sum_ref[2:3, :] = jnp.sum(dxb, 0, keepdims=True)
            sum_ref[3:4, :] = jnp.sum(grad, 0, keepdims=True)

        return carry

    lax.fori_loop(0, n, step, 0)


def middle_back(s, got, mid, g, vec):
    return pl.pallas_call(
        middle_back_kernel,
        out_shape=(
            jax.ShapeDtypeStruct(s.shape, F32),
            jax.ShapeDtypeStruct(s.shape, BF),
            jax.ShapeDtypeStruct((4, s.shape[-1]), F32),
        ),
        in_specs=[VMEM] * 5,
        out_specs=(VMEM,) * 3,
        compiler_params=params(8),
        cost_estimate=cost(2, 5 << 20),
        name="middle_back",
    )(s, got, mid, g, vec)


def add_kernel(kept_ref, got_ref, *out_refs):
    at = 0
    for ref in out_refs:
        for i in range(ref.shape[0]):
            put_rows(ref, i, group(kept_ref, at) + group(got_ref, at).astype(F32))
            at += 1


def core_sum(kept, sent, split):
    got = xor_swap(sent, "ctx", 1)
    return pl.pallas_call(
        add_kernel,
        out_shape=[jax.ShapeDtypeStruct((n,) + kept.shape[1:], BF) for n in split],
        in_specs=[VMEM] * 2,
        out_specs=[VMEM] * len(split),
        compiler_params=params(6),
        cost_estimate=cost(1, 4 << 20),
        name="add_rows",
    )(kept, got)


def first_back_kernel(
    s_ref, got_ref, x_ref, dmid_ref, mid_ref, mlp_ref, mlpgot_ref, vec_ref, out_ref
):
    thin = s_ref.shape[2]
    pieces = out_ref.shape[0]
    result = group(mid_ref, 0) + group(mlp_ref, 0).astype(F32) + group(mlpgot_ref, 0).astype(F32)
    result = result + vec_ref[1:2, :]
    out_ref[:, :thin, :] = result.astype(BF).reshape(pieces, thin, -1)
    dxa = group(s_ref, 0).astype(F32) + group(got_ref, 0).astype(F32)
    normal, rstd = normed(x_rows(x_ref, 0, thin).astype(F32))
    grad = group(dmid_ref, 0) + normed_back(dxa, normal, rstd, vec_ref[0:1, :])
    out_ref[:, thin:, :] = grad.astype(BF).reshape(pieces, thin, -1)


def first_back(s, got, x, dmid, mid, mlp, mlpgot, vec):
    _, pieces, thin, width = s.shape
    return pl.pallas_call(
        first_back_kernel,
        out_shape=jax.ShapeDtypeStruct((pieces, 2 * thin, width), BF),
        in_specs=[VMEM] * 8,
        out_specs=VMEM,
        compiler_params=params(8),
        cost_estimate=cost(20, 6 << 20),
        name="first_back",
    )(s, got, x, dmid, mid, mlp, mlpgot, vec)


def pieces_kernel(own_ref, got_ref, vec_ref, out_ref):
    blocks, r = out_ref.shape[0], out_ref.shape[1] - SPARE
    for b in range(blocks):
        part = slice(b * r, (b + 1) * r)
        out_ref[b, :r, :] = (own_ref[part, :].astype(F32) + got_ref[part, :].astype(F32)).astype(BF)
        last = slice(blocks * r, blocks * r + 2)
        out_ref[b, r : r + 2, :] = (
            own_ref[last, :].astype(F32) + got_ref[last, :].astype(F32)
        ).astype(BF)
        out_ref[b, r + 2 :, :] = vec_ref[...].astype(BF)


def grad_pieces(stay, go, vec, blocks):
    rows = stay.shape[0] - SPARE
    if lax.axis_size("fsdp") == 2 and rows // blocks % 16 == 0:
        return pl.pallas_call(
            pieces_kernel,
            out_shape=jax.ShapeDtypeStruct((blocks, rows // blocks + SPARE, stay.shape[1]), BF),
            in_specs=[VMEM] * 3,
            out_specs=VMEM,
            compiler_params=params(6),
            cost_estimate=cost(1, 2 << 20),
            name="grad_pieces",
        )(stay, xor_swap(go, "fsdp", 1), vec)
    last = lax.psum(stay[rows : rows + 2].astype(F32), "fsdp")
    split = jnp.concatenate([stay[:rows], go[:rows]], 0).reshape(
        lax.axis_size("fsdp"), -1, stay.shape[1]
    )
    own = lax.psum_scatter(split.astype(F32), "fsdp", scatter_dimension=0, tiled=False)
    own = own.reshape(blocks, -1, own.shape[-1])
    small = jnp.concatenate([last, vec], 0)
    small = jnp.broadcast_to(small, (blocks,) + small.shape)
    return jnp.concatenate([own, small], 1).astype(BF)


def weight_part(ref, part):
    w = ref[:, part]
    return w.reshape(w.shape[0] * w.shape[1], w.shape[2])


def mlp_kernel(
    xo_ref,
    xp_ref,
    go_ref,
    gp_ref,
    m_ref,
    b_ref,
    hidden_ref,
    dpre_ref,
    kept_ref,
    sent_ref,
):
    first = xo_ref.shape[0]
    b = bias_row(b_ref, 3)
    for i in range(2 * first):
        own = i < first
        pre = nn(group(xo_ref if own else xp_ref, i % first), weight_part(m_ref, 0)) + b
        dhidden = nn(group(go_ref if own else gp_ref, i % first), weight_part(m_ref, 1))
        share = 0.5 * (1.0 + lax.erf(pre * (0.5**0.5)))
        density = jnp.exp(pre * pre * -0.5) * ((0.5 / 3.141592653589793) ** 0.5)
        n = pre.shape[0]
        hidden_ref[i * n : (i + 1) * n, :] = (pre * share).astype(BF)
        dpre = (dhidden * (share + pre * density)).astype(BF)
        dpre_ref[i * n : (i + 1) * n, :] = dpre
        put_rows(kept_ref if own else sent_ref, i % first, nt(dpre, weight_part(m_ref, 0)))


def mlp_block(xo, xp, go, gp, m, b):
    blocks, pieces, thin, width = xo.shape
    low = jax.ShapeDtypeStruct((2 * blocks * pieces * thin, m.shape[-1]), BF)
    return pl.pallas_call(
        mlp_kernel,
        out_shape=(low, low, jax.ShapeDtypeStruct(xo.shape, F32), jax.ShapeDtypeStruct(xo.shape, BF)),
        in_specs=[VMEM] * 6,
        out_specs=(VMEM,) * 4,
        compiler_params=params(12),
        cost_estimate=cost(7, 12 << 20),
        name="mlp_block",
    )(xo, xp, go, gp, m, b)


def mlp_grads_kernel(
    xo_ref,
    xp_ref,
    dpre_ref,
    go_ref,
    gp_ref,
    hidden_ref,
    m_ref,
    grad_ref,
    kept_ref,
    sent_ref,
    sum_ref,
):
    first, width = xo_ref.shape[0], xo_ref.shape[3]
    half = width // 2
    rows = dpre_ref.shape[0]
    n = rows // 2

    def half_grads(i, carry):
        lanes = pl.ds(pl.multiple_of(i * half, 128), half)
        xo, xp = (ref[:, :, :, lanes].reshape(n, half) for ref in (xo_ref, xp_ref))
        up = tn(xo, dpre_ref[:n, :]) + tn(xp, dpre_ref[n:, :])
        grad_ref[:, i, 0] = up.astype(BF).reshape((-1,) + grad_ref.shape[3:])
        go, gp = (ref[:, :, :, lanes].reshape(n, half) for ref in (go_ref, gp_ref))
        down = tn(go, hidden_ref[:n, :]) + tn(gp, hidden_ref[n:, :])
        grad_ref[:, i, 1] = down.astype(BF).reshape((-1,) + grad_ref.shape[3:])
        return carry

    lax.fori_loop(0, 2, half_grads, 0)
    size = n // first
    for base, out_ref in ((0, kept_ref), (first, sent_ref)):

        def step(i, carry, base=base, out_ref=out_ref):
            part = pl.ds(pl.multiple_of((base + i) * size, size), size)
            put_rows(out_ref, i, nt(hidden_ref[part, :], weight_part(m_ref, 1)))
            return carry

        lax.fori_loop(0, first, step, 0)
    sum_ref[...] = jnp.sum(dpre_ref[...].astype(F32), 0, keepdims=True)


def mlp_grads(xo, xp, dpre, go, gp, hidden, m):
    return pl.pallas_call(
        mlp_grads_kernel,
        out_shape=(
            jax.ShapeDtypeStruct((m.shape[0] // 2, 2) + m.shape[1:], BF),
            jax.ShapeDtypeStruct(xo.shape, F32),
            jax.ShapeDtypeStruct(xo.shape, BF),
            jax.ShapeDtypeStruct((1, dpre.shape[1]), F32),
        ),
        in_specs=[VMEM] * 7,
        out_specs=(VMEM,) * 4,
        compiler_params=params(14),
        cost_estimate=cost(6, 12 << 20),
        name="mlp_grads",
    )(xo, xp, dpre, go, gp, hidden, m)


def attend_grads_kernel(
    flip_ref,
    sum_ref,
    norm_ref,
    dmix_ref,
    do_ref,
    dp_ref,
    att_ref,
    kept_ref,
    sent_ref,
    xo_ref,
    xp_ref,
    stay_ref,
    go_ref,
    vec_ref,
    xa,
):
    first, _, thin, width = kept_ref.shape
    rows, cols = att_ref.shape
    half = width // 2
    n = do_ref.shape[0]
    block = rows // (2 * first)
    vec_ref[...] = jnp.zeros_like(vec_ref)
    for base, x_ref, g_ref in ((0, xo_ref, kept_ref), (first, xp_ref, sent_ref)):

        def step(i, carry, base=base, x_ref=x_ref, g_ref=g_ref):
            normal, _ = normed(x_rows(x_ref, i, thin).astype(F32))
            xa[pl.ds(pl.multiple_of((base + i) * block, block), block), :] = (
                normal * norm_ref[0:1, :] + norm_ref[1:2, :]
            ).astype(BF)
            dx = group(g_ref, i).astype(F32)
            vec_ref[0:1, :] += jnp.sum(dx * normal, 0, keepdims=True)
            vec_ref[1:2, :] += jnp.sum(dx, 0, keepdims=True)
            return carry

        lax.fori_loop(0, first, step, 0)
    totals = [
        jnp.sum(dmix_ref[:, lanes_of(dmix_ref, c)].astype(F32), 0, keepdims=True).astype(BF)
        for c in (0, 2)
    ]

    def half_grads(i, out_ref):
        lanes = pl.ds(pl.multiple_of(i * half, 128), half)
        grads = tn(xa[:, lanes], dmix_ref[...]).astype(BF)
        for c in range(3):
            out_ref[:half, c * cols : (c + 1) * cols] = grads[:, lanes_of(dmix_ref, c)]
        out = tn(do_ref[:, lanes], att_ref[:n, :]) + tn(dp_ref[:, lanes], att_ref[n:, :])
        out_ref[:half, 3 * cols : 4 * cols] = out.astype(BF)
        out_ref[half : half + SPARE, :] = jnp.zeros((SPARE, out_ref.shape[1]), BF)
        for place, total in enumerate(totals):
            out_ref[half : half + 1, place * cols : (place + 1) * cols] = total
        out_ref[half + 1 : half + 2, : sum_ref.shape[1]] = sum_ref[...].astype(BF)

    half_grads(flip_ref[0], stay_ref)
    half_grads(1 - flip_ref[0], go_ref)


def attend_grads(flip, sums, norms, dmix, do, dp, att, kept, sent, xo, xp):
    width = do.shape[1]
    shape = jax.ShapeDtypeStruct((width // 2 + SPARE, 4 * att.shape[1]), BF)
    return pl.pallas_call(
        attend_grads_kernel,
        out_shape=(shape, shape, jax.ShapeDtypeStruct((2, width), F32)),
        in_specs=[SMEM] + [VMEM] * 10,
        out_specs=(VMEM,) * 3,
        scratch_shapes=[pltpu.VMEM((att.shape[0], width), BF)],
        compiler_params=params(14),
        cost_estimate=cost(6, 12 << 20),
        name="attend_grads",
    )(flip, sums, norms, dmix, do, dp, att, kept, sent, xo, xp)


def exact_low(x):
    one = lax.reduce_precision(x, 8, 7)
    two = lax.reduce_precision(x - one, 8, 7)
    return jnp.concatenate([one, two, x - one - two], 0).astype(BF)


def per_device(
    inputs,
    segments,
    ln1_gain,
    ln1_bias,
    query_key_value_weight,
    b_qv,
    output_weight,
    output_bias,
    ln2_gain,
    ln2_bias,
    up_weight,
    up_bias,
    down_weight,
    down_bias,
    out_grad,
):
    z = lax.axis_index("tp")
    ctx = lax.axis_index("ctx")
    planes = lax.axis_size("tp")
    thin, width = inputs.shape[1], inputs.shape[2]
    ds, _, cols = query_key_value_weight.shape
    hidden_cols = up_weight.shape[1]

    vectors = jnp.stack([ln1_gain, ln1_bias, output_bias, ln2_gain, ln2_bias, down_bias])
    rows_of = lambda a: a.reshape(-1, a.shape[-1])

    biases = jnp.pad(b_qv.reshape(1, -1), ((0, 0), (0, width - 2 * cols)))
    biases = [exact_low(biases), exact_low(up_bias.reshape(1, -1)), jnp.zeros((SPARE - 6, width), BF)]
    a_shard = jnp.concatenate(
        [query_key_value_weight.reshape(ds, 3 * cols), jnp.transpose(output_weight)], 1
    )
    a_shard = jnp.concatenate([a_shard] + biases, 0)
    labels = jnp.pad(segments.astype(BF)[:, None, :], ((0, 0), (0, SPARE - 1), (0, width - thin)))
    own = rows_over_z(jnp.concatenate([after(inputs, a_shard), labels, out_grad], 1))
    x_own, g_own = own[:, : thin + SPARE], own[:, thin + SPARE :]
    got = [send_turned(a_shard, k) for k in range(planes)]
    a_rows = place([g[:ds] for g in got], z).reshape(-1, width)
    biases = got[0][ds:]
    w_attn = weight_over_x(a_rows)
    x_pair, x_far = gather_ctx(after(x_own, w_attn)[None])
    g_own = after(g_own, x_pair)[None]

    m_shard = jnp.concatenate([up_weight, jnp.transpose(down_weight)], 0)
    m_shard = send_turned(after(m_shard, a_rows), 0)
    m_all = lax.all_gather(m_shard, ("fsdp", "tp"), axis=0, tiled=True)
    m_all = m_all.reshape(-1, 2, ds, hidden_cols)
    aligned = ds % 16 == 0 and m_all.shape[0] % 2 == 0
    if not aligned:
        m_all = m_all.reshape(2, -1, 2, ds, hidden_cols).transpose(0, 2, 1, 3, 4)
        m_all = m_all.reshape(2, 2, width // 2, hidden_cols)

    mixed, segr, lo, hi = qkv(x_pair, x_far, vectors, biases, w_attn, cols, thin)
    g_got = xor_swap(g_own, "ctx", 2)
    attended, lse, kept, sent = attend(lo, hi, mixed, segr, w_attn)
    g_got, kept, sent = lax.optimization_barrier((g_got, kept, sent))
    g_pair = jnp.concatenate([g_own, g_got], 0)
    g_far = xor_swap(g_pair, "ctx", 1)
    (s,) = core_sum(kept, sent, (2,))
    got = after(xor_swap(s, "ctx", 2), m_all)
    middle, xb_pair = middle_rows(s, got, x_pair, vectors[2:5])
    xb_far = xor_swap(xb_pair, "ctx", 1)

    hidden, dpre, kept, sent = mlp_block(xb_pair, xb_far, g_pair, g_far, m_all, biases)
    (s,) = core_sum(kept, sent, (2,))
    m_grad, mlp_kept, mlp_sent, dpre_sum = mlp_grads(
        xb_pair, xb_far, after(dpre, s), g_pair, g_far, hidden, m_all
    )
    got = xor_swap(s, "ctx", 2)
    mlp_s, mlp_low = core_sum(mlp_kept, after(mlp_sent, got), (1, 1))
    dmid, db_pair, sums_two = middle_back(
        s, after(got, dpre_sum), middle, g_pair, vectors[3:4]
    )
    db_far = xor_swap(db_pair, "ctx", 1)
    if not aligned:
        m_grad = m_grad[0].transpose(1, 0, 2, 3).reshape(2, -1, planes, ds, hidden_cols)
        m_grad = m_grad.transpose(2, 1, 0, 3, 4)
    m_sums = lax.psum_scatter(m_grad, "tp", scatter_dimension=0, tiled=False)
    mlp_got = xor_swap(after(mlp_low, db_far), "ctx", 2)

    dmix, kept, sent = attend_back(
        lo, hi, mixed, attended, lse, db_pair, db_far, segr, w_attn
    )
    s, low = core_sum(kept, after(sent, mlp_got), (1, 1))
    flip = lax.axis_index("fsdp") if lax.axis_size("fsdp") == 2 else 0
    got = xor_swap(low, "ctx", 2)
    g_stay, g_go, sums_one = attend_grads(
        jnp.full((1,), flip, jnp.int32),
        dpre_sum,
        vectors[0:2],
        after(rows_of(dmix), s),
        rows_of(db_pair),
        rows_of(db_far),
        rows_of(attended),
        kept,
        sent,
        x_pair,
        x_far,
    )
    vec = jnp.concatenate([vectors[0:1], vectors[5:6]], 0)
    shared = jnp.concatenate([sums_one, sums_two], 0)
    if lax.axis_size("fsdp") == 2:
        shared = shared + xor_swap(shared, "fsdp", 1)
    else:
        shared = lax.psum(shared, "fsdp")
    shared = shared + xor_swap(shared, "ctx", 1)
    both = first_back(s, after(got, shared), x_pair, dmid, middle, mlp_s, mlp_got, vec)
    shared = after(shared, both)
    shared = shared + xor_swap(shared, "ctx", 2)
    a_low = grad_pieces(g_stay, g_go, shared, planes)

    both = rows_over_z(both)
    output, input_grad = both[:, :thin], both[:, thin:].astype(F32)
    m_z = m_sums
    if lax.axis_size("fsdp") == 2:
        x = lax.axis_index("fsdp")
        m_got = xor_swap(pick(after(m_sums, a_low), x ^ 1), "fsdp", 1)
        m_sums = (pick(m_sums, x).astype(F32) + m_got.astype(F32)).astype(BF)
    else:
        m_sums = lax.psum_scatter(m_sums.astype(F32), "fsdp", scatter_dimension=0, tiled=False)
        m_sums = m_sums.astype(BF)
    m_back = send_back(m_sums.reshape(2 * ds, hidden_cols), 0)
    *got, m_back = lax.optimization_barrier((*scatter_blocks(a_low, m_z, both), m_back))

    g_attn = sum(g.astype(F32) for g in got)
    grad_qkv = g_attn[:ds, : 3 * cols].reshape(ds, 3, cols)
    grad_out = jnp.transpose(g_attn[:ds, 3 * cols :])
    mine, shared = g_attn[ds : ds + 2], g_attn[ds + 2 :]
    g_mlp = m_back.astype(F32)
    grad_up, grad_down = g_mlp[:ds], jnp.transpose(g_mlp[ds:])
    return (
        output,
        input_grad,
        shared[0],
        shared[1],
        grad_qkv,
        mine[0, : 2 * cols].reshape(2, cols),
        grad_out,
        shared[2],
        shared[3],
        shared[4],
        grad_up,
        mine[1, :hidden_cols],
        grad_down,
        shared[5],
    )


def solution(mesh):
    in_specs = (
        P("fsdp", ("ctx", "tp"), None),
        P("fsdp", ("ctx", "tp")),
        P(),
        P(),
        P(("fsdp", "ctx"), None, "tp"),
        P(None, "tp"),
        P("tp", ("fsdp", "ctx")),
        P(),
        P(),
        P(),
        P(("fsdp", "ctx"), "tp"),
        P("tp"),
        P("tp", ("fsdp", "ctx")),
        P(),
        P("fsdp", ("ctx", "tp"), None),
    )
    out_specs = (
        P("fsdp", ("ctx", "tp"), None),
        P("fsdp", ("ctx", "tp"), None),
        P(),
        P(),
        P(("fsdp", "ctx"), None, "tp"),
        P(None, "tp"),
        P("tp", ("fsdp", "ctx")),
        P(),
        P(),
        P(),
        P(("fsdp", "ctx"), "tp"),
        P("tp"),
        P("tp", ("fsdp", "ctx")),
        P(),
    )
    return jax.shard_map(
        per_device, mesh=mesh, in_specs=in_specs, out_specs=out_specs, check_vma=False
    )
```

```python
from functools import partial

import jax
import jax.numpy as jnp
from jax import lax
from jax.experimental import pallas as pl
from jax.experimental.pallas import tpu as pltpu
from jax.sharding import PartitionSpec as P

DH = 64
EPS = 1e-06
BF = jnp.bfloat16
F32 = jnp.float32
NEG = -1e30
SPARE = 8
VMEM = pl.BlockSpec(memory_space=pltpu.VMEM)
SMEM = pl.BlockSpec(memory_space=pltpu.SMEM)


def after(x, *deps):
    return lax.optimization_barrier((x,) + deps)[0]


def xor_swap(x, axis, k):
    n = lax.axis_size(axis)
    return lax.ppermute(x, axis, [(i, i ^ k) for i in range(n)])


def turn_pairs(n, k):
    return [(a * n + b, b * n + (a ^ k)) for a in range(n) for b in range(n)]


def send_turned(x, k):
    return lax.ppermute(x, ("ctx", "tp"), turn_pairs(lax.axis_size("tp"), k))


def send_back(x, k):
    pairs = turn_pairs(lax.axis_size("tp"), k)
    return lax.ppermute(x, ("ctx", "tp"), [(d, s) for s, d in pairs])


def hop_pairs(n, k):
    pairs = []
    for a in range(n):
        for q in range(n):
            f, low = (q ^ k) // 2, (q ^ k) % 2
            pairs.append((a * n + q, ((a // 2) * 2 + low) * n + (a ^ (2 * f))))
    return pairs


def scatter_blocks(pieces, *late):
    n = lax.axis_size("tp")
    y, q = lax.axis_index("ctx") // 2, lax.axis_index("tp")
    split = pieces.reshape((2, 2) + pieces.shape[1:])
    got = xor_swap(pick(split, y ^ 1), "ctx", 2)
    four = after(jnp.concatenate([pick(split, y), got], 0), *late)
    return [lax.ppermute(pick(four, q ^ k), ("ctx", "tp"), hop_pairs(n, k)) for k in range(n)]


def rows_over_z(arr):
    return lax.all_to_all(arr, "tp", 0, 0, tiled=True)


def place(pieces, first):
    out = jnp.zeros((len(pieces),) + pieces[0].shape, pieces[0].dtype)
    for k, piece in enumerate(pieces):
        out = lax.dynamic_update_index_in_dim(out, piece, first ^ k, 0)
    return out


def pick(arr, index):
    return lax.dynamic_index_in_dim(arr, index, 0, keepdims=False)


def gather_ctx(own):
    half = jnp.concatenate([own, xor_swap(own, "ctx", 2)], 0)
    return half, xor_swap(half, "ctx", 1)


def weight_over_x(rows):
    if lax.axis_size("fsdp") == 2:
        got = xor_swap(rows, "fsdp", 1)
        first = lax.axis_index("fsdp") == 0
        return jnp.stack([jnp.where(first, rows, got), jnp.where(first, got, rows)])
    every = lax.all_gather(rows, "fsdp", axis=0, tiled=True)
    return every.reshape(2, -1, every.shape[1])


def nt(a, b):
    return lax.dot_general(a, b, (((1,), (1,)), ((), ())), preferred_element_type=F32)


def nn(a, b):
    return lax.dot_general(a, b, (((1,), (0,)), ((), ())), preferred_element_type=F32)


def tn(a, b):
    return lax.dot_general(a, b, (((0,), (0,)), ((), ())), preferred_element_type=F32)


def params(limit, steps=None):
    return pltpu.CompilerParams(vmem_limit_bytes=limit << 20)


def cost(micros, nbytes):
    return pl.CostEstimate(
        flops=int(micros * 0.27 * 10**9), transcendentals=0, bytes_accessed=1024
    )


def normed(x):
    n = x.shape[-1]
    centred = x - jnp.sum(x, -1, keepdims=True) * (1.0 / n)
    rstd = lax.rsqrt(jnp.sum(centred * centred, -1, keepdims=True) * (1.0 / n) + EPS)
    return centred * rstd, rstd


def normed_back(grad, normal, rstd, gain):
    n = grad.shape[-1]
    scaled = grad * gain
    one = jnp.sum(scaled, -1, keepdims=True) * (1.0 / n)
    two = jnp.sum(scaled * normal, -1, keepdims=True) * (1.0 / n)
    return rstd * (scaled - one - normal * two)


def bias_row(ref, row):
    parts = ref[row : row + 3, :].astype(F32)
    return parts[0:1] + parts[1:2] + parts[2:3]


def qkv_kernel(
    cols,
    xo_ref,
    xp_ref,
    vec_ref,
    b_ref,
    w_ref,
    qkv_ref,
    seg_ref,
    lo_ref,
    hi_ref,
):
    first, pieces = xo_ref.shape[0], xo_ref.shape[1]
    thin, width = qkv_ref.shape[2], xo_ref.shape[3]
    half = width // 2
    b = bias_row(b_ref, 0)
    for i in range(2 * first):
        x_ref = xo_ref if i < first else xp_ref
        normal, _ = normed(x_rows(x_ref, i % first, thin).astype(F32))
        xa = (normal * vec_ref[0:1, :] + vec_ref[1:2, :]).astype(BF)
        mixed = nn(xa[:, :half], w_ref[0, :, : 3 * cols]) + nn(xa[:, half:], w_ref[1, :, : 3 * cols])
        parts = (
            mixed[:, :cols] + b[:, :cols],
            mixed[:, cols : 2 * cols],
            mixed[:, 2 * cols :] + b[:, cols : 2 * cols],
        )
        for c, part in enumerate(parts):
            put_lanes(qkv_ref, i, c, part)
        labels = [
            x_ref[i % first, k, thin : thin + SPARE, :thin].astype(F32)[0:1, :]
            for k in range(pieces)
        ]
        labels = jnp.concatenate(labels, 1)
        seg_ref[:, i * pieces * thin : (i + 1) * pieces * thin] = jnp.broadcast_to(
            labels, (8, pieces * thin)
        )
        lo_ref[i] = jnp.min(labels).astype(jnp.int32)
        hi_ref[i] = jnp.max(labels).astype(jnp.int32)


def qkv(xo, xp, vec, b, w, cols, thin):
    first, pieces, _, _ = xo.shape
    bound = jax.ShapeDtypeStruct((2 * first,), jnp.int32)
    return pl.pallas_call(
        partial(qkv_kernel, cols),
        out_shape=(
            jax.ShapeDtypeStruct((2 * first, pieces, thin, 4 * cols), BF),
            jax.ShapeDtypeStruct((8, 2 * first * pieces * thin), F32),
            bound,
            bound,
        ),
        in_specs=[VMEM] * 5,
        out_specs=(VMEM,) * 2 + (SMEM,) * 2,
        compiler_params=params(12),
        cost_estimate=cost(4, 6 << 20),
        name="qkv",
    )(xo, xp, vec, b, w)


def head_mask(h, width):
    lane = lax.broadcasted_iota(jnp.int32, (1, width), 1)
    return (lane >= h * DH) & (lane < (h + 1) * DH)


def only_head(x, h):
    return jnp.where(head_mask(h, x.shape[1]), x, jnp.zeros_like(x))


def x_rows(ref, i, thin):
    return ref[i, :, :thin, :].reshape(-1, ref.shape[3])


def group(ref, i):
    return ref[i].reshape(ref.shape[1] * ref.shape[2], ref.shape[3])


def put_rows(ref, i, value):
    ref[i] = value.astype(ref.dtype).reshape(ref.shape[1:])


def lanes_of(ref, part):
    cols = ref.shape[-1] // 4
    wide = ref.shape[-1] // 3
    return slice(part * wide, part * wide + cols)


def part_rows(ref, i, part):
    value = ref[i, :, :, lanes_of(ref, part)]
    return value.reshape(-1, value.shape[-1])


def put_lanes(ref, i, part, value):
    ref[i, :, :, lanes_of(ref, part)] = value.astype(ref.dtype).reshape(
        ref.shape[1:3] + value.shape[1:]
    )


def turned(x):
    return jnp.transpose(x.astype(F32)).astype(x.dtype)


def with_blocks(lo_ref, hi_ref, list_ref, i, groups, work):
    count = jnp.int32(0)
    for j in range(groups):
        on = (hi_ref[i] >= lo_ref[j]) & (lo_ref[i] <= hi_ref[j])

        @pl.when(on)
        def _():
            list_ref[count] = j

        count = count + on.astype(jnp.int32)
    for number, less in ((2, 0), (groups, 2)):

        @pl.when((count > less) & (count <= number))
        def _():
            js = [list_ref[jnp.minimum(t, count - 1)] for t in range(number)]
            work(js, count == number)


def put_projected(kept_ref, sent_ref, i, project):
    first = kept_ref.shape[0]
    out = kept_ref if i < first else sent_ref
    half = out.shape[3] // 2
    for part in range(2):
        out[i % first, :, :, part * half : (part + 1) * half] = (
            project(part).astype(out.dtype).reshape(out.shape[1:3] + (half,))
        )


def attend_kernel(
    heads,
    lo_ref,
    hi_ref,
    qkv_ref,
    segr_ref,
    w_ref,
    att_ref,
    lse_ref,
    kept_ref,
    sent_ref,
    kk,
    vt,
    ow,
    segc_ref,
    list_ref,
):
    groups = qkv_ref.shape[0]
    n = qkv_ref.shape[1] * qkv_ref.shape[2]
    cols = qkv_ref.shape[3] // 4
    segc_ref[...] = jnp.transpose(segr_ref[...])
    ow[...] = w_ref[:, :, 3 * cols :]
    for i in range(groups):
        kk[i * n : (i + 1) * n, :] = part_rows(qkv_ref, i, 1)
        vt[i] = turned(part_rows(qkv_ref, i, 2))

    def per_query(i, carry):
        qs = pl.ds(pl.multiple_of(i * n, n), n)

        def work(js, last):
            seg_q = segr_ref[0:1, qs]
            seg_last = jnp.where(last, seg_q, -1.0)
            q = part_rows(qkv_ref, i, 0) * jnp.asarray(0.125, BF)
            places = [pl.ds(pl.multiple_of(j * n, n), n) for j in js]
            same = [segc_ref[ks, 0:1] == seg_q for ks in places[:-1]]
            same.append(segc_ref[places[-1], 0:1] == seg_last)
            outs = []
            for h in range(heads):
                qh = only_head(q, h)
                scores = [
                    jnp.where(mask, nt(kk[ks, :], qh), NEG) for ks, mask in zip(places, same)
                ]
                top = [jnp.max(s, 0, keepdims=True) for s in scores]
                top = sum_of(top, jnp.maximum)
                total, out = [], []
                for s, j in zip(scores, js):
                    p = jnp.exp(s - top)
                    total.append(jnp.sum(p, 0, keepdims=True))
                    out.append(nn(vt[j, h * DH : (h + 1) * DH, :], p.astype(BF)))
                total = sum_of(total, jnp.add)
                outs.append(sum_of(out, jnp.add) * (1.0 / total))
                lse_ref[h : h + 1, qs] = top + jnp.log(total)
            out = jnp.transpose(jnp.concatenate(outs, 0))
            put_rows(att_ref, i, jnp.where(segc_ref[qs, 0:1] > 0, out, 0.0))

        with_blocks(lo_ref, hi_ref, list_ref, i, groups, work)
        return carry

    lax.fori_loop(0, groups, per_query, 0)
    for i in range(groups):
        att = group(att_ref, i)
        put_projected(kept_ref, sent_ref, i, lambda part: nt(att, ow[part]))


def sum_of(values, join):
    total = values[0]
    for value in values[1:]:
        total = join(total, value)
    return total


def attend(lo, hi, mixed, segr, w):
    groups, pieces, thin, _ = mixed.shape
    cols = mixed.shape[3] // 4
    heads = cols // DH
    n, rows = pieces * thin, groups * pieces * thin
    width = 2 * w.shape[1]
    return pl.pallas_call(
        partial(attend_kernel, heads),
        out_shape=(
            jax.ShapeDtypeStruct((groups, pieces, thin, cols), BF),
            jax.ShapeDtypeStruct((8, rows), F32),
            jax.ShapeDtypeStruct((groups // 2, pieces, thin, width), F32),
            jax.ShapeDtypeStruct((groups // 2, pieces, thin, width), BF),
        ),
        in_specs=[SMEM, SMEM] + [VMEM] * 3,
        out_specs=(VMEM,) * 4,
        scratch_shapes=[
            pltpu.VMEM((rows, cols), BF),
            pltpu.VMEM((groups, cols, n), BF),
            pltpu.VMEM((2, width // 2, cols), BF),
            pltpu.VMEM((rows, 8), F32),
            pltpu.SMEM((groups,), jnp.int32),
        ],
        compiler_params=params(16),
        cost_estimate=cost(11, 8 << 20),
        name="attend",
    )(lo, hi, mixed, segr, w)


def attend_back_kernel(
    heads,
    lo_ref,
    hi_ref,
    qkv_ref,
    att_ref,
    lse_ref,
    db_ref,
    dp_ref,
    segr_ref,
    w_ref,
    dmix_ref,
    kept_ref,
    sent_ref,
    kt,
    kk,
    vv,
    do_ref,
    delta,
    ak,
    av,
    ow,
    kw,
    segc_ref,
    list_ref,
):
    groups = qkv_ref.shape[0]
    n = qkv_ref.shape[1] * qkv_ref.shape[2]
    cols = qkv_ref.shape[3] // 4
    half = w_ref.shape[1]
    segc_ref[...] = jnp.transpose(segr_ref[...])
    ow[...] = w_ref[:, :, 3 * cols :]
    kw[...] = w_ref[:, :, cols : 2 * cols]
    ak[...] = jnp.zeros_like(ak)
    av[...] = jnp.zeros_like(av)
    for i in range(groups):
        rows = slice(i * n, (i + 1) * n)
        kk[rows, :] = part_rows(qkv_ref, i, 1)
        vv[rows, :] = part_rows(qkv_ref, i, 2)
        kt[i] = turned(part_rows(qkv_ref, i, 1))
        grad = group(db_ref, i) if i < groups // 2 else group(dp_ref, i - groups // 2)
        out_back = nn(grad[:, :half], ow[0]) + nn(grad[:, half:], ow[1])
        do = jnp.where(segc_ref[rows, 0:1] > 0, out_back, 0.0).astype(BF)
        do_ref[rows, :] = do
        prod = jnp.transpose(do.astype(F32) * group(att_ref, i).astype(F32))
        for h in range(heads):
            delta[h : h + 1, rows] = jnp.sum(prod[h * DH : (h + 1) * DH, :], 0, keepdims=True)

    def per_query(i, carry):
        qs = pl.ds(pl.multiple_of(i * n, n), n)

        def work(js, last):
            seg_q = segr_ref[0:1, qs]
            seg_last = jnp.where(last, seg_q, -1.0)
            q = part_rows(qkv_ref, i, 0) * jnp.asarray(0.125, BF)
            do = do_ref[qs, :]
            qh = [only_head(q, h) for h in range(heads)]
            dh = [only_head(do, h) for h in range(heads)]
            dq = [[] for _ in range(heads)]
            for t, j in enumerate(js):
                ks = pl.ds(pl.multiple_of(j * n, n), n)
                same = segc_ref[ks, 0:1] == (seg_q if t < len(js) - 1 else seg_last)
                dk, dv = [], []
                for h in range(heads):
                    s = jnp.where(same, nt(kk[ks, :], qh[h]), NEG)
                    p = jnp.exp(s - lse_ref[h : h + 1, qs])
                    ds = (p * (nt(vv[ks, :], dh[h]) - delta[h : h + 1, qs])).astype(BF)
                    dv.append(nn(p.astype(BF), dh[h]))
                    dk.append(nn(ds, qh[h]))
                    dq[h].append(nn(kt[j, h * DH : (h + 1) * DH, :], ds))
                ak[ks, :] += sum_of(dk, jnp.add)
                av[ks, :] += sum_of(dv, jnp.add)
            dq = jnp.concatenate([sum_of(parts, jnp.add) for parts in dq], 0)
            put_lanes(dmix_ref, i, 0, jnp.transpose(dq) * 0.125)

        with_blocks(lo_ref, hi_ref, list_ref, i, groups, work)
        return carry

    lax.fori_loop(0, groups, per_query, 0)
    for i in range(groups):
        rows = slice(i * n, (i + 1) * n)
        dq = part_rows(dmix_ref, i, 0)
        dk = ak[rows, :].astype(BF)
        dv = av[rows, :].astype(BF)
        put_lanes(dmix_ref, i, 1, dk)
        put_lanes(dmix_ref, i, 2, dv)

        def project(part):
            dx = nt(dq, w_ref[part, :, :cols]) + nt(dk, kw[part])
            return dx + nt(dv, w_ref[part, :, 2 * cols : 3 * cols])

        put_projected(kept_ref, sent_ref, i, project)


def attend_back(lo, hi, mixed, att, lse, db, dp, segr, w):
    groups, pieces, thin, cols = att.shape
    heads = cols // DH
    n, rows = pieces * thin, groups * pieces * thin
    width = 2 * w.shape[1]
    return pl.pallas_call(
        partial(attend_back_kernel, heads),
        out_shape=(
            jax.ShapeDtypeStruct(mixed.shape, BF),
            jax.ShapeDtypeStruct((groups // 2, pieces, thin, width), F32),
            jax.ShapeDtypeStruct((groups // 2, pieces, thin, width), BF),
        ),
        in_specs=[SMEM, SMEM] + [VMEM] * 7,
        out_specs=(VMEM,) * 3,
        scratch_shapes=[
            pltpu.VMEM((groups, cols, n), BF),
            pltpu.VMEM((rows, cols), BF),
            pltpu.VMEM((rows, cols), BF),
            pltpu.VMEM((rows, cols), BF),
            pltpu.VMEM((8, rows), F32),
            pltpu.VMEM((rows, cols), F32),
            pltpu.VMEM((rows, cols), F32),
            pltpu.VMEM((2, width // 2, cols), BF),
            pltpu.VMEM((2, width // 2, cols), BF),
            pltpu.VMEM((rows, 8), F32),
            pltpu.SMEM((groups,), jnp.int32),
        ],
        compiler_params=params(18),
        cost_estimate=cost(70, 12 << 20),
        name="attend_back",
    )(lo, hi, mixed, att, lse, db, dp, segr, w)


def middle_kernel(s_ref, got_ref, x_ref, vec_ref, mid_ref, xb_ref):
    n, _, thin, width = s_ref.shape
    for i in range(n):
        x = x_rows(x_ref, i, thin).astype(F32)
        mid = group(s_ref, i).astype(F32) + group(got_ref, n - 1 - i).astype(F32) + x + vec_ref[0:1, :]
        put_rows(mid_ref, i, mid)
        normal, _ = normed(mid)
        put_rows(xb_ref, i, normal * vec_ref[1:2, :] + vec_ref[2:3, :])


def middle_rows(s, got, x, vec):
    return pl.pallas_call(
        middle_kernel,
        out_shape=(jax.ShapeDtypeStruct(s.shape, F32), jax.ShapeDtypeStruct(s.shape, BF)),
        in_specs=[VMEM] * 4,
        out_specs=(VMEM,) * 2,
        compiler_params=params(8),
        cost_estimate=cost(2, 4 << 20),
        name="middle_rows",
    )(s, got, x, vec)


def middle_back_kernel(s_ref, got_ref, mid_ref, g_ref, vec_ref, dmid_ref, db_ref, sum_ref):
    n = s_ref.shape[0]

    def step(i, carry):
        dxb = group(s_ref, i).astype(F32) + group(got_ref, n - 1 - i).astype(F32)
        normal, rstd = normed(group(mid_ref, i))
        grad = group(g_ref, i).astype(F32)
        dmid = grad + normed_back(dxb, normal, rstd, vec_ref[...])
        low = dmid.astype(BF)
        put_rows(dmid_ref, i, dmid)
        put_rows(db_ref, i, low)

        @pl.when(i == 0)
        def _():
            sum_ref[0:1, :] = jnp.sum(low.astype(F32), 0, keepdims=True)
            sum_ref[1:2, :] = jnp.sum(dxb * normal, 0, keepdims=True)
            sum_ref[2:3, :] = jnp.sum(dxb, 0, keepdims=True)
            sum_ref[3:4, :] = jnp.sum(grad, 0, keepdims=True)

        return carry

    lax.fori_loop(0, n, step, 0)


def middle_back(s, got, mid, g, vec):
    return pl.pallas_call(
        middle_back_kernel,
        out_shape=(
            jax.ShapeDtypeStruct(s.shape, F32),
            jax.ShapeDtypeStruct(s.shape, BF),
            jax.ShapeDtypeStruct((4, s.shape[-1]), F32),
        ),
        in_specs=[VMEM] * 5,
        out_specs=(VMEM,) * 3,
        compiler_params=params(8),
        cost_estimate=cost(2, 5 << 20),
        name="middle_back",
    )(s, got, mid, g, vec)


def add_kernel(kept_ref, got_ref, *out_refs):
    at = 0
    for ref in out_refs:
        for i in range(ref.shape[0]):
            put_rows(ref, i, group(kept_ref, at) + group(got_ref, at).astype(F32))
            at += 1


def core_sum(kept, sent, split):
    got = xor_swap(sent, "ctx", 1)
    return pl.pallas_call(
        add_kernel,
        out_shape=[jax.ShapeDtypeStruct((n,) + kept.shape[1:], BF) for n in split],
        in_specs=[VMEM] * 2,
        out_specs=[VMEM] * len(split),
        compiler_params=params(6),
        cost_estimate=cost(1, 4 << 20),
        name="add_rows",
    )(kept, got)


def first_back_kernel(
    s_ref, got_ref, x_ref, dmid_ref, mid_ref, mlp_ref, mlpgot_ref, vec_ref, out_ref
):
    thin = s_ref.shape[2]
    pieces = out_ref.shape[0]
    result = group(mid_ref, 0) + group(mlp_ref, 0).astype(F32) + group(mlpgot_ref, 0).astype(F32)
    result = result + vec_ref[1:2, :]
    out_ref[:, :thin, :] = result.astype(BF).reshape(pieces, thin, -1)
    dxa = group(s_ref, 0).astype(F32) + group(got_ref, 0).astype(F32)
    normal, rstd = normed(x_rows(x_ref, 0, thin).astype(F32))
    grad = group(dmid_ref, 0) + normed_back(dxa, normal, rstd, vec_ref[0:1, :])
    out_ref[:, thin:, :] = grad.astype(BF).reshape(pieces, thin, -1)


def first_back(s, got, x, dmid, mid, mlp, mlpgot, vec):
    _, pieces, thin, width = s.shape
    return pl.pallas_call(
        first_back_kernel,
        out_shape=jax.ShapeDtypeStruct((pieces, 2 * thin, width), BF),
        in_specs=[VMEM] * 8,
        out_specs=VMEM,
        compiler_params=params(8),
        cost_estimate=cost(20, 6 << 20),
        name="first_back",
    )(s, got, x, dmid, mid, mlp, mlpgot, vec)


def pieces_kernel(own_ref, got_ref, vec_ref, out_ref):
    blocks, r = out_ref.shape[0], out_ref.shape[1] - SPARE
    for b in range(blocks):
        part = slice(b * r, (b + 1) * r)
        out_ref[b, :r, :] = (own_ref[part, :].astype(F32) + got_ref[part, :].astype(F32)).astype(BF)
        last = slice(blocks * r, blocks * r + 2)
        out_ref[b, r : r + 2, :] = (
            own_ref[last, :].astype(F32) + got_ref[last, :].astype(F32)
        ).astype(BF)
        out_ref[b, r + 2 :, :] = vec_ref[...].astype(BF)


def grad_pieces(stay, go, vec, blocks):
    rows = stay.shape[0] - SPARE
    if lax.axis_size("fsdp") == 2 and rows // blocks % 16 == 0:
        return pl.pallas_call(
            pieces_kernel,
            out_shape=jax.ShapeDtypeStruct((blocks, rows // blocks + SPARE, stay.shape[1]), BF),
            in_specs=[VMEM] * 3,
            out_specs=VMEM,
            compiler_params=params(6),
            cost_estimate=cost(1, 2 << 20),
            name="grad_pieces",
        )(stay, xor_swap(go, "fsdp", 1), vec)
    last = lax.psum(stay[rows : rows + 2].astype(F32), "fsdp")
    split = jnp.concatenate([stay[:rows], go[:rows]], 0).reshape(
        lax.axis_size("fsdp"), -1, stay.shape[1]
    )
    own = lax.psum_scatter(split.astype(F32), "fsdp", scatter_dimension=0, tiled=False)
    own = own.reshape(blocks, -1, own.shape[-1])
    small = jnp.concatenate([last, vec], 0)
    small = jnp.broadcast_to(small, (blocks,) + small.shape)
    return jnp.concatenate([own, small], 1).astype(BF)


def weight_part(ref, part):
    w = ref[:, part]
    return w.reshape(w.shape[0] * w.shape[1], w.shape[2])


def mlp_kernel(
    xo_ref,
    xp_ref,
    go_ref,
    gp_ref,
    m_ref,
    b_ref,
    hidden_ref,
    dpre_ref,
    kept_ref,
    sent_ref,
):
    first = xo_ref.shape[0]
    b = bias_row(b_ref, 3)
    for i in range(2 * first):
        own = i < first
        pre = nn(group(xo_ref if own else xp_ref, i % first), weight_part(m_ref, 0)) + b
        dhidden = nn(group(go_ref if own else gp_ref, i % first), weight_part(m_ref, 1))
        share = 0.5 * (1.0 + lax.erf(pre * (0.5**0.5)))
        density = jnp.exp(pre * pre * -0.5) * ((0.5 / 3.141592653589793) ** 0.5)
        n = pre.shape[0]
        hidden_ref[i * n : (i + 1) * n, :] = (pre * share).astype(BF)
        dpre = (dhidden * (share + pre * density)).astype(BF)
        dpre_ref[i * n : (i + 1) * n, :] = dpre
        put_rows(kept_ref if own else sent_ref, i % first, nt(dpre, weight_part(m_ref, 0)))


def mlp_block(xo, xp, go, gp, m, b):
    blocks, pieces, thin, width = xo.shape
    low = jax.ShapeDtypeStruct((2 * blocks * pieces * thin, m.shape[-1]), BF)
    return pl.pallas_call(
        mlp_kernel,
        out_shape=(low, low, jax.ShapeDtypeStruct(xo.shape, F32), jax.ShapeDtypeStruct(xo.shape, BF)),
        in_specs=[VMEM] * 6,
        out_specs=(VMEM,) * 4,
        compiler_params=params(12),
        cost_estimate=cost(7, 12 << 20),
        name="mlp_block",
    )(xo, xp, go, gp, m, b)


def mlp_grads_kernel(
    xo_ref,
    xp_ref,
    dpre_ref,
    go_ref,
    gp_ref,
    hidden_ref,
    m_ref,
    grad_ref,
    kept_ref,
    sent_ref,
    sum_ref,
):
    first, width = xo_ref.shape[0], xo_ref.shape[3]
    half = width // 2
    rows = dpre_ref.shape[0]
    n = rows // 2

    def half_grads(i, carry):
        lanes = pl.ds(pl.multiple_of(i * half, 128), half)
        xo, xp = (ref[:, :, :, lanes].reshape(n, half) for ref in (xo_ref, xp_ref))
        up = tn(xo, dpre_ref[:n, :]) + tn(xp, dpre_ref[n:, :])
        grad_ref[:, i, 0] = up.astype(BF).reshape((-1,) + grad_ref.shape[3:])
        go, gp = (ref[:, :, :, lanes].reshape(n, half) for ref in (go_ref, gp_ref))
        down = tn(go, hidden_ref[:n, :]) + tn(gp, hidden_ref[n:, :])
        grad_ref[:, i, 1] = down.astype(BF).reshape((-1,) + grad_ref.shape[3:])
        return carry

    lax.fori_loop(0, 2, half_grads, 0)
    size = n // first
    for base, out_ref in ((0, kept_ref), (first, sent_ref)):

        def step(i, carry, base=base, out_ref=out_ref):
            part = pl.ds(pl.multiple_of((base + i) * size, size), size)
            put_rows(out_ref, i, nt(hidden_ref[part, :], weight_part(m_ref, 1)))
            return carry

        lax.fori_loop(0, first, step, 0)
    sum_ref[...] = jnp.sum(dpre_ref[...].astype(F32), 0, keepdims=True)


def mlp_grads(xo, xp, dpre, go, gp, hidden, m):
    return pl.pallas_call(
        mlp_grads_kernel,
        out_shape=(
            jax.ShapeDtypeStruct((m.shape[0] // 2, 2) + m.shape[1:], BF),
            jax.ShapeDtypeStruct(xo.shape, F32),
            jax.ShapeDtypeStruct(xo.shape, BF),
            jax.ShapeDtypeStruct((1, dpre.shape[1]), F32),
        ),
        in_specs=[VMEM] * 7,
        out_specs=(VMEM,) * 4,
        compiler_params=params(14),
        cost_estimate=cost(6, 12 << 20),
        name="mlp_grads",
    )(xo, xp, dpre, go, gp, hidden, m)


def attend_grads_kernel(
    flip_ref,
    sum_ref,
    norm_ref,
    dmix_ref,
    do_ref,
    dp_ref,
    att_ref,
    kept_ref,
    sent_ref,
    xo_ref,
    xp_ref,
    stay_ref,
    go_ref,
    vec_ref,
    xa,
):
    first, _, thin, width = kept_ref.shape
    rows, cols = att_ref.shape
    half = width // 2
    n = do_ref.shape[0]
    block = rows // (2 * first)
    vec_ref[...] = jnp.zeros_like(vec_ref)
    for base, x_ref, g_ref in ((0, xo_ref, kept_ref), (first, xp_ref, sent_ref)):

        def step(i, carry, base=base, x_ref=x_ref, g_ref=g_ref):
            normal, _ = normed(x_rows(x_ref, i, thin).astype(F32))
            xa[pl.ds(pl.multiple_of((base + i) * block, block), block), :] = (
                normal * norm_ref[0:1, :] + norm_ref[1:2, :]
            ).astype(BF)
            dx = group(g_ref, i).astype(F32)
            vec_ref[0:1, :] += jnp.sum(dx * normal, 0, keepdims=True)
            vec_ref[1:2, :] += jnp.sum(dx, 0, keepdims=True)
            return carry

        lax.fori_loop(0, first, step, 0)
    totals = [
        jnp.sum(dmix_ref[:, lanes_of(dmix_ref, c)].astype(F32), 0, keepdims=True).astype(BF)
        for c in (0, 2)
    ]

    def half_grads(i, out_ref):
        lanes = pl.ds(pl.multiple_of(i * half, 128), half)
        grads = tn(xa[:, lanes], dmix_ref[...]).astype(BF)
        for c in range(3):
            out_ref[:half, c * cols : (c + 1) * cols] = grads[:, lanes_of(dmix_ref, c)]
        out = tn(do_ref[:, lanes], att_ref[:n, :]) + tn(dp_ref[:, lanes], att_ref[n:, :])
        out_ref[:half, 3 * cols : 4 * cols] = out.astype(BF)
        out_ref[half : half + SPARE, :] = jnp.zeros((SPARE, out_ref.shape[1]), BF)
        for place, total in enumerate(totals):
            out_ref[half : half + 1, place * cols : (place + 1) * cols] = total
        out_ref[half + 1 : half + 2, : sum_ref.shape[1]] = sum_ref[...].astype(BF)

    half_grads(flip_ref[0], stay_ref)
    half_grads(1 - flip_ref[0], go_ref)


def attend_grads(flip, sums, norms, dmix, do, dp, att, kept, sent, xo, xp):
    width = do.shape[1]
    shape = jax.ShapeDtypeStruct((width // 2 + SPARE, 4 * att.shape[1]), BF)
    return pl.pallas_call(
        attend_grads_kernel,
        out_shape=(shape, shape, jax.ShapeDtypeStruct((2, width), F32)),
        in_specs=[SMEM] + [VMEM] * 10,
        out_specs=(VMEM,) * 3,
        scratch_shapes=[pltpu.VMEM((att.shape[0], width), BF)],
        compiler_params=params(14),
        cost_estimate=cost(6, 12 << 20),
        name="attend_grads",
    )(flip, sums, norms, dmix, do, dp, att, kept, sent, xo, xp)


def exact_low(x):
    one = lax.reduce_precision(x, 8, 7)
    two = lax.reduce_precision(x - one, 8, 7)
    return jnp.concatenate([one, two, x - one - two], 0).astype(BF)


def per_device(
    inputs,
    segments,
    ln1_gain,
    ln1_bias,
    query_key_value_weight,
    b_qv,
    output_weight,
    output_bias,
    ln2_gain,
    ln2_bias,
    up_weight,
    up_bias,
    down_weight,
    down_bias,
    out_grad,
):
    z = lax.axis_index("tp")
    ctx = lax.axis_index("ctx")
    planes = lax.axis_size("tp")
    thin, width = inputs.shape[1], inputs.shape[2]
    ds, _, cols = query_key_value_weight.shape
    hidden_cols = up_weight.shape[1]

    vectors = jnp.stack([ln1_gain, ln1_bias, output_bias, ln2_gain, ln2_bias, down_bias])
    rows_of = lambda a: a.reshape(-1, a.shape[-1])

    biases = jnp.pad(b_qv.reshape(1, -1), ((0, 0), (0, width - 2 * cols)))
    biases = [exact_low(biases), exact_low(up_bias.reshape(1, -1)), jnp.zeros((SPARE - 6, width), BF)]
    a_shard = jnp.concatenate(
        [query_key_value_weight.reshape(ds, 3 * cols), jnp.transpose(output_weight)], 1
    )
    a_shard = jnp.concatenate([a_shard] + biases, 0)
    labels = jnp.pad(segments.astype(BF)[:, None, :], ((0, 0), (0, SPARE - 1), (0, width - thin)))
    own = rows_over_z(jnp.concatenate([after(inputs, a_shard), labels, out_grad], 1))
    x_own, g_own = own[:, : thin + SPARE], own[:, thin + SPARE :]
    got = [send_turned(a_shard, k) for k in range(planes)]
    a_rows = place([g[:ds] for g in got], z).reshape(-1, width)
    biases = got[0][ds:]
    w_attn = weight_over_x(a_rows)
    x_pair, x_far = gather_ctx(after(x_own, w_attn)[None])
    g_own = after(g_own, x_pair)[None]

    m_shard = jnp.concatenate([up_weight, jnp.transpose(down_weight)], 0)
    m_shard = send_turned(after(m_shard, a_rows), 0)
    m_all = lax.all_gather(m_shard, ("fsdp", "tp"), axis=0, tiled=True)
    m_all = m_all.reshape(-1, 2, ds, hidden_cols)
    aligned = ds % 16 == 0 and m_all.shape[0] % 2 == 0
    if not aligned:
        m_all = m_all.reshape(2, -1, 2, ds, hidden_cols).transpose(0, 2, 1, 3, 4)
        m_all = m_all.reshape(2, 2, width // 2, hidden_cols)

    mixed, segr, lo, hi = qkv(x_pair, x_far, vectors, biases, w_attn, cols, thin)
    g_got = xor_swap(g_own, "ctx", 2)
    attended, lse, kept, sent = attend(lo, hi, mixed, segr, w_attn)
    g_got, kept, sent = lax.optimization_barrier((g_got, kept, sent))
    g_pair = jnp.concatenate([g_own, g_got], 0)
    g_far = xor_swap(g_pair, "ctx", 1)
    (s,) = core_sum(kept, sent, (2,))
    got = after(xor_swap(s, "ctx", 2), m_all)
    middle, xb_pair = middle_rows(s, got, x_pair, vectors[2:5])
    xb_far = xor_swap(xb_pair, "ctx", 1)

    hidden, dpre, kept, sent = mlp_block(xb_pair, xb_far, g_pair, g_far, m_all, biases)
    (s,) = core_sum(kept, sent, (2,))
    m_grad, mlp_kept, mlp_sent, dpre_sum = mlp_grads(
        xb_pair, xb_far, after(dpre, s), g_pair, g_far, hidden, m_all
    )
    got = xor_swap(s, "ctx", 2)
    mlp_s, mlp_low = core_sum(mlp_kept, after(mlp_sent, got), (1, 1))
    dmid, db_pair, sums_two = middle_back(
        s, after(got, dpre_sum), middle, g_pair, vectors[3:4]
    )
    db_far = xor_swap(db_pair, "ctx", 1)
    if not aligned:
        m_grad = m_grad[0].transpose(1, 0, 2, 3).reshape(2, -1, planes, ds, hidden_cols)
        m_grad = m_grad.transpose(2, 1, 0, 3, 4)
    m_sums = lax.psum_scatter(m_grad, "tp", scatter_dimension=0, tiled=False)
    mlp_got = xor_swap(after(mlp_low, db_far), "ctx", 2)

    dmix, kept, sent = attend_back(
        lo, hi, mixed, attended, lse, db_pair, db_far, segr, w_attn
    )
    s, low = core_sum(kept, after(sent, mlp_got), (1, 1))
    flip = lax.axis_index("fsdp") if lax.axis_size("fsdp") == 2 else 0
    got = xor_swap(low, "ctx", 2)
    g_stay, g_go, sums_one = attend_grads(
        jnp.full((1,), flip, jnp.int32),
        dpre_sum,
        vectors[0:2],
        after(rows_of(dmix), s),
        rows_of(db_pair),
        rows_of(db_far),
        rows_of(attended),
        kept,
        sent,
        x_pair,
        x_far,
    )
    vec = jnp.concatenate([vectors[0:1], vectors[5:6]], 0)
    shared = jnp.concatenate([sums_one, sums_two], 0)
    if lax.axis_size("fsdp") == 2:
        shared = shared + xor_swap(shared, "fsdp", 1)
    else:
        shared = lax.psum(shared, "fsdp")
    shared = shared + xor_swap(shared, "ctx", 1)
    both = first_back(s, after(got, shared), x_pair, dmid, middle, mlp_s, mlp_got, vec)
    shared = after(shared, both)
    shared = shared + xor_swap(shared, "ctx", 2)
    a_low = grad_pieces(g_stay, g_go, shared, planes)

    both = rows_over_z(both)
    output, input_grad = both[:, :thin], both[:, thin:].astype(F32)
    m_z = m_sums
    if lax.axis_size("fsdp") == 2:
        x = lax.axis_index("fsdp")
        m_got = xor_swap(pick(after(m_sums, a_low), x ^ 1), "fsdp", 1)
        m_sums = (pick(m_sums, x).astype(F32) + m_got.astype(F32)).astype(BF)
    else:
        m_sums = lax.psum_scatter(m_sums.astype(F32), "fsdp", scatter_dimension=0, tiled=False)
        m_sums = m_sums.astype(BF)
    m_back = send_back(m_sums.reshape(2 * ds, hidden_cols), 0)
    *got, m_back = lax.optimization_barrier((*scatter_blocks(a_low, m_z, both), m_back))

    g_attn = sum(g.astype(F32) for g in got)
    grad_qkv = g_attn[:ds, : 3 * cols].reshape(ds, 3, cols)
    grad_out = jnp.transpose(g_attn[:ds, 3 * cols :])
    mine, shared = g_attn[ds : ds + 2], g_attn[ds + 2 :]
    g_mlp = m_back.astype(F32)
    grad_up, grad_down = g_mlp[:ds], jnp.transpose(g_mlp[ds:])
    return (
        output,
        input_grad,
        shared[0],
        shared[1],
        grad_qkv,
        mine[0, : 2 * cols].reshape(2, cols),
        grad_out,
        shared[2],
        shared[3],
        shared[4],
        grad_up,
        mine[1, :hidden_cols],
        grad_down,
        shared[5],
    )


def solution(mesh):
    in_specs = (
        P("fsdp", ("ctx", "tp"), None),
        P("fsdp", ("ctx", "tp")),
        P(),
        P(),
        P(("fsdp", "ctx"), None, "tp"),
        P(None, "tp"),
        P("tp", ("fsdp", "ctx")),
        P(),
        P(),
        P(),
        P(("fsdp", "ctx"), "tp"),
        P("tp"),
        P("tp", ("fsdp", "ctx")),
        P(),
        P("fsdp", ("ctx", "tp"), None),
    )
    out_specs = (
        P("fsdp", ("ctx", "tp"), None),
        P("fsdp", ("ctx", "tp"), None),
        P(),
        P(),
        P(("fsdp", "ctx"), None, "tp"),
        P(None, "tp"),
        P("tp", ("fsdp", "ctx")),
        P(),
        P(),
        P(),
        P(("fsdp", "ctx"), "tp"),
        P("tp"),
        P("tp", ("fsdp", "ctx")),
        P(),
    )
    return jax.shard_map(
        per_device, mesh=mesh, in_specs=in_specs, out_specs=out_specs, check_vma=False
    )
```

```python
from functools import partial

import jax
import jax.numpy as jnp
from jax import lax
from jax.experimental import pallas as pl
from jax.experimental.pallas import tpu as pltpu
from jax.sharding import PartitionSpec as P

DH = 64
EPS = 1e-06
BF = jnp.bfloat16
F32 = jnp.float32
NEG = -1e30
SPARE = 8
VMEM = pl.BlockSpec(memory_space=pltpu.VMEM)
SMEM = pl.BlockSpec(memory_space=pltpu.SMEM)


def after(x, *deps):
    return lax.optimization_barrier((x,) + deps)[0]


def xor_swap(x, axis, k):
    n = lax.axis_size(axis)
    return lax.ppermute(x, axis, [(i, i ^ k) for i in range(n)])


def turn_pairs(n, k):
    return [(a * n + b, b * n + (a ^ k)) for a in range(n) for b in range(n)]


def send_turned(x, k):
    return lax.ppermute(x, ("ctx", "tp"), turn_pairs(lax.axis_size("tp"), k))


def send_back(x, k):
    pairs = turn_pairs(lax.axis_size("tp"), k)
    return lax.ppermute(x, ("ctx", "tp"), [(d, s) for s, d in pairs])


def hop_pairs(n, k):
    pairs = []
    for a in range(n):
        for q in range(n):
            f, low = (q ^ k) // 2, (q ^ k) % 2
            pairs.append((a * n + q, ((a // 2) * 2 + low) * n + (a ^ (2 * f))))
    return pairs


def scatter_blocks(pieces, *late):
    n = lax.axis_size("tp")
    y, q = lax.axis_index("ctx") // 2, lax.axis_index("tp")
    split = pieces.reshape((2, 2) + pieces.shape[1:])
    got = xor_swap(pick(split, y ^ 1), "ctx", 2)
    four = after(jnp.concatenate([pick(split, y), got], 0), *late)
    return [lax.ppermute(pick(four, q ^ k), ("ctx", "tp"), hop_pairs(n, k)) for k in range(n)]


def rows_over_z(arr):
    return lax.all_to_all(arr, "tp", 0, 0, tiled=True)


def place(pieces, first):
    out = jnp.zeros((len(pieces),) + pieces[0].shape, pieces[0].dtype)
    for k, piece in enumerate(pieces):
        out = lax.dynamic_update_index_in_dim(out, piece, first ^ k, 0)
    return out


def pick(arr, index):
    return lax.dynamic_index_in_dim(arr, index, 0, keepdims=False)


def gather_ctx(own):
    half = jnp.concatenate([own, xor_swap(own, "ctx", 2)], 0)
    return half, xor_swap(half, "ctx", 1)


def weight_over_x(rows):
    if lax.axis_size("fsdp") == 2:
        got = xor_swap(rows, "fsdp", 1)
        first = lax.axis_index("fsdp") == 0
        return jnp.stack([jnp.where(first, rows, got), jnp.where(first, got, rows)])
    every = lax.all_gather(rows, "fsdp", axis=0, tiled=True)
    return every.reshape(2, -1, every.shape[1])


def nt(a, b):
    return lax.dot_general(a, b, (((1,), (1,)), ((), ())), preferred_element_type=F32)


def nn(a, b):
    return lax.dot_general(a, b, (((1,), (0,)), ((), ())), preferred_element_type=F32)


def tn(a, b):
    return lax.dot_general(a, b, (((0,), (0,)), ((), ())), preferred_element_type=F32)


def params(limit, steps=None):
    return pltpu.CompilerParams(vmem_limit_bytes=limit << 20)


def cost(micros, nbytes):
    return pl.CostEstimate(
        flops=int(micros * 0.27 * 10**9), transcendentals=0, bytes_accessed=1024
    )


def normed(x):
    n = x.shape[-1]
    centred = x - jnp.sum(x, -1, keepdims=True) * (1.0 / n)
    rstd = lax.rsqrt(jnp.sum(centred * centred, -1, keepdims=True) * (1.0 / n) + EPS)
    return centred * rstd, rstd


def normed_back(grad, normal, rstd, gain):
    n = grad.shape[-1]
    scaled = grad * gain
    one = jnp.sum(scaled, -1, keepdims=True) * (1.0 / n)
    two = jnp.sum(scaled * normal, -1, keepdims=True) * (1.0 / n)
    return rstd * (scaled - one - normal * two)


def bias_row(ref, row):
    parts = ref[row : row + 3, :].astype(F32)
    return parts[0:1] + parts[1:2] + parts[2:3]


def qkv_kernel(
    cols,
    xo_ref,
    xp_ref,
    vec_ref,
    b_ref,
    w_ref,
    qkv_ref,
    seg_ref,
    lo_ref,
    hi_ref,
):
    first, pieces = xo_ref.shape[0], xo_ref.shape[1]
    thin, width = qkv_ref.shape[2], xo_ref.shape[3]
    half = width // 2
    b = bias_row(b_ref, 0)
    for i in range(2 * first):
        x_ref = xo_ref if i < first else xp_ref
        normal, _ = normed(x_rows(x_ref, i % first, thin).astype(F32))
        xa = (normal * vec_ref[0:1, :] + vec_ref[1:2, :]).astype(BF)
        mixed = nn(xa[:, :half], w_ref[0, :, : 3 * cols]) + nn(xa[:, half:], w_ref[1, :, : 3 * cols])
        parts = (
            mixed[:, :cols] + b[:, :cols],
            mixed[:, cols : 2 * cols],
            mixed[:, 2 * cols :] + b[:, cols : 2 * cols],
        )
        for c, part in enumerate(parts):
            put_lanes(qkv_ref, i, c, part)
        labels = [
            x_ref[i % first, k, thin : thin + SPARE, :thin].astype(F32)[0:1, :]
            for k in range(pieces)
        ]
        labels = jnp.concatenate(labels, 1)
        seg_ref[:, i * pieces * thin : (i + 1) * pieces * thin] = jnp.broadcast_to(
            labels, (8, pieces * thin)
        )
        lo_ref[i] = jnp.min(labels).astype(jnp.int32)
        hi_ref[i] = jnp.max(labels).astype(jnp.int32)


def qkv(xo, xp, vec, b, w, cols, thin):
    first, pieces, _, _ = xo.shape
    bound = jax.ShapeDtypeStruct((2 * first,), jnp.int32)
    return pl.pallas_call(
        partial(qkv_kernel, cols),
        out_shape=(
            jax.ShapeDtypeStruct((2 * first, pieces, thin, 4 * cols), BF),
            jax.ShapeDtypeStruct((8, 2 * first * pieces * thin), F32),
            bound,
            bound,
        ),
        in_specs=[VMEM] * 5,
        out_specs=(VMEM,) * 2 + (SMEM,) * 2,
        compiler_params=params(12),
        cost_estimate=cost(4, 6 << 20),
        name="qkv",
    )(xo, xp, vec, b, w)


def head_mask(h, width):
    lane = lax.broadcasted_iota(jnp.int32, (1, width), 1)
    return (lane >= h * DH) & (lane < (h + 1) * DH)


def only_head(x, h):
    return jnp.where(head_mask(h, x.shape[1]), x, jnp.zeros_like(x))


def x_rows(ref, i, thin):
    return ref[i, :, :thin, :].reshape(-1, ref.shape[3])


def group(ref, i):
    return ref[i].reshape(ref.shape[1] * ref.shape[2], ref.shape[3])


def put_rows(ref, i, value):
    ref[i] = value.astype(ref.dtype).reshape(ref.shape[1:])


def lanes_of(ref, part):
    cols = ref.shape[-1] // 4
    wide = ref.shape[-1] // 3
    return slice(part * wide, part * wide + cols)


def part_rows(ref, i, part):
    value = ref[i, :, :, lanes_of(ref, part)]
    return value.reshape(-1, value.shape[-1])


def put_lanes(ref, i, part, value):
    ref[i, :, :, lanes_of(ref, part)] = value.astype(ref.dtype).reshape(
        ref.shape[1:3] + value.shape[1:]
    )


def turned(x):
    return jnp.transpose(x.astype(F32)).astype(x.dtype)


def with_blocks(lo_ref, hi_ref, list_ref, i, groups, work):
    count = jnp.int32(0)
    for j in range(groups):
        on = (hi_ref[i] >= lo_ref[j]) & (lo_ref[i] <= hi_ref[j])

        @pl.when(on)
        def _():
            list_ref[count] = j

        count = count + on.astype(jnp.int32)
    for number, less in ((2, 0), (groups, 2)):

        @pl.when((count > less) & (count <= number))
        def _():
            js = [list_ref[jnp.minimum(t, count - 1)] for t in range(number)]
            work(js, count == number)


def put_projected(kept_ref, sent_ref, i, project):
    first = kept_ref.shape[0]
    out = kept_ref if i < first else sent_ref
    half = out.shape[3] // 2
    for part in range(2):
        out[i % first, :, :, part * half : (part + 1) * half] = (
            project(part).astype(out.dtype).reshape(out.shape[1:3] + (half,))
        )


def attend_kernel(
    heads,
    lo_ref,
    hi_ref,
    qkv_ref,
    segr_ref,
    w_ref,
    att_ref,
    lse_ref,
    kept_ref,
    sent_ref,
    kk,
    vt,
    ow,
    segc_ref,
    list_ref,
):
    groups = qkv_ref.shape[0]
    n = qkv_ref.shape[1] * qkv_ref.shape[2]
    cols = qkv_ref.shape[3] // 4
    segc_ref[...] = jnp.transpose(segr_ref[...])
    ow[...] = w_ref[:, :, 3 * cols :]
    for i in range(groups):
        kk[i * n : (i + 1) * n, :] = part_rows(qkv_ref, i, 1)
        vt[i] = turned(part_rows(qkv_ref, i, 2))

    def per_query(i, carry):
        qs = pl.ds(pl.multiple_of(i * n, n), n)

        def work(js, last):
            seg_q = segr_ref[0:1, qs]
            seg_last = jnp.where(last, seg_q, -1.0)
            q = part_rows(qkv_ref, i, 0) * jnp.asarray(0.125, BF)
            places = [pl.ds(pl.multiple_of(j * n, n), n) for j in js]
            same = [segc_ref[ks, 0:1] == seg_q for ks in places[:-1]]
            same.append(segc_ref[places[-1], 0:1] == seg_last)
            outs = []
            for h in range(heads):
                qh = only_head(q, h)
                scores = [
                    jnp.where(mask, nt(kk[ks, :], qh), NEG) for ks, mask in zip(places, same)
                ]
                top = [jnp.max(s, 0, keepdims=True) for s in scores]
                top = sum_of(top, jnp.maximum)
                total, out = [], []
                for s, j in zip(scores, js):
                    p = jnp.exp(s - top)
                    total.append(jnp.sum(p, 0, keepdims=True))
                    out.append(nn(vt[j, h * DH : (h + 1) * DH, :], p.astype(BF)))
                total = sum_of(total, jnp.add)
                outs.append(sum_of(out, jnp.add) * (1.0 / total))
                lse_ref[h : h + 1, qs] = top + jnp.log(total)
            out = jnp.transpose(jnp.concatenate(outs, 0))
            put_rows(att_ref, i, jnp.where(segc_ref[qs, 0:1] > 0, out, 0.0))

        with_blocks(lo_ref, hi_ref, list_ref, i, groups, work)
        return carry

    lax.fori_loop(0, groups, per_query, 0)
    for i in range(groups):
        att = group(att_ref, i)
        put_projected(kept_ref, sent_ref, i, lambda part: nt(att, ow[part]))


def sum_of(values, join):
    total = values[0]
    for value in values[1:]:
        total = join(total, value)
    return total


def attend(lo, hi, mixed, segr, w):
    groups, pieces, thin, _ = mixed.shape
    cols = mixed.shape[3] // 4
    heads = cols // DH
    n, rows = pieces * thin, groups * pieces * thin
    width = 2 * w.shape[1]
    return pl.pallas_call(
        partial(attend_kernel, heads),
        out_shape=(
            jax.ShapeDtypeStruct((groups, pieces, thin, cols), BF),
            jax.ShapeDtypeStruct((8, rows), F32),
            jax.ShapeDtypeStruct((groups // 2, pieces, thin, width), F32),
            jax.ShapeDtypeStruct((groups // 2, pieces, thin, width), BF),
        ),
        in_specs=[SMEM, SMEM] + [VMEM] * 3,
        out_specs=(VMEM,) * 4,
        scratch_shapes=[
            pltpu.VMEM((rows, cols), BF),
            pltpu.VMEM((groups, cols, n), BF),
            pltpu.VMEM((2, width // 2, cols), BF),
            pltpu.VMEM((rows, 8), F32),
            pltpu.SMEM((groups,), jnp.int32),
        ],
        compiler_params=params(16),
        cost_estimate=cost(11, 8 << 20),
        name="attend",
    )(lo, hi, mixed, segr, w)


def attend_back_kernel(
    heads,
    lo_ref,
    hi_ref,
    qkv_ref,
    att_ref,
    lse_ref,
    db_ref,
    dp_ref,
    segr_ref,
    w_ref,
    dmix_ref,
    kept_ref,
    sent_ref,
    kt,
    kk,
    vv,
    do_ref,
    delta,
    ak,
    av,
    ow,
    kw,
    segc_ref,
    list_ref,
):
    groups = qkv_ref.shape[0]
    n = qkv_ref.shape[1] * qkv_ref.shape[2]
    cols = qkv_ref.shape[3] // 4
    half = w_ref.shape[1]
    segc_ref[...] = jnp.transpose(segr_ref[...])
    ow[...] = w_ref[:, :, 3 * cols :]
    kw[...] = w_ref[:, :, cols : 2 * cols]
    ak[...] = jnp.zeros_like(ak)
    av[...] = jnp.zeros_like(av)
    for i in range(groups):
        rows = slice(i * n, (i + 1) * n)
        kk[rows, :] = part_rows(qkv_ref, i, 1)
        vv[rows, :] = part_rows(qkv_ref, i, 2)
        kt[i] = turned(part_rows(qkv_ref, i, 1))
        grad = group(db_ref, i) if i < groups // 2 else group(dp_ref, i - groups // 2)
        out_back = nn(grad[:, :half], ow[0]) + nn(grad[:, half:], ow[1])
        do = jnp.where(segc_ref[rows, 0:1] > 0, out_back, 0.0).astype(BF)
        do_ref[rows, :] = do
        prod = jnp.transpose(do.astype(F32) * group(att_ref, i).astype(F32))
        for h in range(heads):
            delta[h : h + 1, rows] = jnp.sum(prod[h * DH : (h + 1) * DH, :], 0, keepdims=True)

    def per_query(i, carry):
        qs = pl.ds(pl.multiple_of(i * n, n), n)

        def work(js, last):
            seg_q = segr_ref[0:1, qs]
            seg_last = jnp.where(last, seg_q, -1.0)
            q = part_rows(qkv_ref, i, 0) * jnp.asarray(0.125, BF)
            do = do_ref[qs, :]
            qh = [only_head(q, h) for h in range(heads)]
            dh = [only_head(do, h) for h in range(heads)]
            dq = [[] for _ in range(heads)]
            for t, j in enumerate(js):
                ks = pl.ds(pl.multiple_of(j * n, n), n)
                same = segc_ref[ks, 0:1] == (seg_q if t < len(js) - 1 else seg_last)
                dk, dv = [], []
                for h in range(heads):
                    s = jnp.where(same, nt(kk[ks, :], qh[h]), NEG)
                    p = jnp.exp(s - lse_ref[h : h + 1, qs])
                    ds = (p * (nt(vv[ks, :], dh[h]) - delta[h : h + 1, qs])).astype(BF)
                    dv.append(nn(p.astype(BF), dh[h]))
                    dk.append(nn(ds, qh[h]))
                    dq[h].append(nn(kt[j, h * DH : (h + 1) * DH, :], ds))
                ak[ks, :] += sum_of(dk, jnp.add)
                av[ks, :] += sum_of(dv, jnp.add)
            dq = jnp.concatenate([sum_of(parts, jnp.add) for parts in dq], 0)
            put_lanes(dmix_ref, i, 0, jnp.transpose(dq) * 0.125)

        with_blocks(lo_ref, hi_ref, list_ref, i, groups, work)
        return carry

    lax.fori_loop(0, groups, per_query, 0)
    for i in range(groups):
        rows = slice(i * n, (i + 1) * n)
        dq = part_rows(dmix_ref, i, 0)
        dk = ak[rows, :].astype(BF)
        dv = av[rows, :].astype(BF)
        put_lanes(dmix_ref, i, 1, dk)
        put_lanes(dmix_ref, i, 2, dv)

        def project(part):
            dx = nt(dq, w_ref[part, :, :cols]) + nt(dk, kw[part])
            return dx + nt(dv, w_ref[part, :, 2 * cols : 3 * cols])

        put_projected(kept_ref, sent_ref, i, project)


def attend_back(lo, hi, mixed, att, lse, db, dp, segr, w):
    groups, pieces, thin, cols = att.shape
    heads = cols // DH
    n, rows = pieces * thin, groups * pieces * thin
    width = 2 * w.shape[1]
    return pl.pallas_call(
        partial(attend_back_kernel, heads),
        out_shape=(
            jax.ShapeDtypeStruct(mixed.shape, BF),
            jax.ShapeDtypeStruct((groups // 2, pieces, thin, width), F32),
            jax.ShapeDtypeStruct((groups // 2, pieces, thin, width), BF),
        ),
        in_specs=[SMEM, SMEM] + [VMEM] * 7,
        out_specs=(VMEM,) * 3,
        scratch_shapes=[
            pltpu.VMEM((groups, cols, n), BF),
            pltpu.VMEM((rows, cols), BF),
            pltpu.VMEM((rows, cols), BF),
            pltpu.VMEM((rows, cols), BF),
            pltpu.VMEM((8, rows), F32),
            pltpu.VMEM((rows, cols), F32),
            pltpu.VMEM((rows, cols), F32),
            pltpu.VMEM((2, width // 2, cols), BF),
            pltpu.VMEM((2, width // 2, cols), BF),
            pltpu.VMEM((rows, 8), F32),
            pltpu.SMEM((groups,), jnp.int32),
        ],
        compiler_params=params(18),
        cost_estimate=cost(70, 12 << 20),
        name="attend_back",
    )(lo, hi, mixed, att, lse, db, dp, segr, w)


def middle_kernel(s_ref, got_ref, x_ref, vec_ref, mid_ref, xb_ref):
    n, _, thin, width = s_ref.shape
    for i in range(n):
        x = x_rows(x_ref, i, thin).astype(F32)
        mid = group(s_ref, i).astype(F32) + group(got_ref, n - 1 - i).astype(F32) + x + vec_ref[0:1, :]
        put_rows(mid_ref, i, mid)
        normal, _ = normed(mid)
        put_rows(xb_ref, i, normal * vec_ref[1:2, :] + vec_ref[2:3, :])


def middle_rows(s, got, x, vec):
    return pl.pallas_call(
        middle_kernel,
        out_shape=(jax.ShapeDtypeStruct(s.shape, BF), jax.ShapeDtypeStruct(s.shape, BF)),
        in_specs=[VMEM] * 4,
        out_specs=(VMEM,) * 2,
        compiler_params=params(8),
        cost_estimate=cost(2, 4 << 20),
        name="middle_rows",
    )(s, got, x, vec)


def middle_back_kernel(s_ref, got_ref, mid_ref, g_ref, vec_ref, dmid_ref, db_ref, sum_ref):
    n = s_ref.shape[0]

    def step(i, carry):
        dxb = group(s_ref, i).astype(F32) + group(got_ref, n - 1 - i).astype(F32)
        normal, rstd = normed(group(mid_ref, i).astype(F32))
        grad = group(g_ref, i).astype(F32)
        dmid = grad + normed_back(dxb, normal, rstd, vec_ref[...])
        low = dmid.astype(BF)
        put_rows(db_ref, i, low)

        @pl.when(i == 0)
        def _():
            put_rows(dmid_ref, 0, dmid)
            sum_ref[0:1, :] = jnp.sum(low.astype(F32), 0, keepdims=True)
            sum_ref[1:2, :] = jnp.sum(dxb * normal, 0, keepdims=True)
            sum_ref[2:3, :] = jnp.sum(dxb, 0, keepdims=True)
            sum_ref[3:4, :] = jnp.sum(grad, 0, keepdims=True)

        return carry

    lax.fori_loop(0, n, step, 0)


def middle_back(s, got, mid, g, vec):
    return pl.pallas_call(
        middle_back_kernel,
        out_shape=(
            jax.ShapeDtypeStruct((1,) + s.shape[1:], F32),
            jax.ShapeDtypeStruct(s.shape, BF),
            jax.ShapeDtypeStruct((4, s.shape[-1]), F32),
        ),
        in_specs=[VMEM] * 5,
        out_specs=(VMEM,) * 3,
        compiler_params=params(8),
        cost_estimate=cost(2, 5 << 20),
        name="middle_back",
    )(s, got, mid, g, vec)


def add_kernel(kept_ref, got_ref, *out_refs):
    at = 0
    for ref in out_refs:
        for i in range(ref.shape[0]):
            put_rows(ref, i, group(kept_ref, at) + group(got_ref, at).astype(F32))
            at += 1


def core_sum(kept, sent, split):
    got = xor_swap(sent, "ctx", 1)
    return pl.pallas_call(
        add_kernel,
        out_shape=[jax.ShapeDtypeStruct((n,) + kept.shape[1:], BF) for n in split],
        in_specs=[VMEM] * 2,
        out_specs=[VMEM] * len(split),
        compiler_params=params(6),
        cost_estimate=cost(1, 4 << 20),
        name="add_rows",
    )(kept, got)


def first_back_kernel(
    s_ref, got_ref, x_ref, dmid_ref, mid_ref, mlp_ref, mlpgot_ref, vec_ref, out_ref
):
    thin = s_ref.shape[2]
    pieces = out_ref.shape[0]
    result = group(mid_ref, 0).astype(F32) + group(mlp_ref, 0).astype(F32) + group(mlpgot_ref, 0).astype(F32)
    result = result + vec_ref[1:2, :]
    out_ref[:, :thin, :] = result.astype(BF).reshape(pieces, thin, -1)
    dxa = group(s_ref, 0).astype(F32) + group(got_ref, 0).astype(F32)
    normal, rstd = normed(x_rows(x_ref, 0, thin).astype(F32))
    grad = group(dmid_ref, 0) + normed_back(dxa, normal, rstd, vec_ref[0:1, :])
    out_ref[:, thin:, :] = grad.astype(BF).reshape(pieces, thin, -1)


def first_back(s, got, x, dmid, mid, mlp, mlpgot, vec):
    _, pieces, thin, width = s.shape
    return pl.pallas_call(
        first_back_kernel,
        out_shape=jax.ShapeDtypeStruct((pieces, 2 * thin, width), BF),
        in_specs=[VMEM] * 8,
        out_specs=VMEM,
        compiler_params=params(8),
        cost_estimate=cost(20, 6 << 20),
        name="first_back",
    )(s, got, x, dmid, mid, mlp, mlpgot, vec)


def pieces_kernel(own_ref, got_ref, vec_ref, out_ref):
    blocks, r = out_ref.shape[0], out_ref.shape[1] - SPARE
    for b in range(blocks):
        part = slice(b * r, (b + 1) * r)
        out_ref[b, :r, :] = (own_ref[part, :].astype(F32) + got_ref[part, :].astype(F32)).astype(BF)
        last = slice(blocks * r, blocks * r + 2)
        out_ref[b, r : r + 2, :] = (
            own_ref[last, :].astype(F32) + got_ref[last, :].astype(F32)
        ).astype(BF)
        out_ref[b, r + 2 :, :] = vec_ref[...].astype(BF)


def grad_pieces(stay, go, vec, blocks):
    rows = stay.shape[0] - SPARE
    if lax.axis_size("fsdp") == 2 and rows // blocks % 16 == 0:
        return pl.pallas_call(
            pieces_kernel,
            out_shape=jax.ShapeDtypeStruct((blocks, rows // blocks + SPARE, stay.shape[1]), BF),
            in_specs=[VMEM] * 3,
            out_specs=VMEM,
            compiler_params=params(6),
            cost_estimate=cost(1, 2 << 20),
            name="grad_pieces",
        )(stay, xor_swap(go, "fsdp", 1), vec)
    last = lax.psum(stay[rows : rows + 2].astype(F32), "fsdp")
    split = jnp.concatenate([stay[:rows], go[:rows]], 0).reshape(
        lax.axis_size("fsdp"), -1, stay.shape[1]
    )
    own = lax.psum_scatter(split.astype(F32), "fsdp", scatter_dimension=0, tiled=False)
    own = own.reshape(blocks, -1, own.shape[-1])
    small = jnp.concatenate([last, vec], 0)
    small = jnp.broadcast_to(small, (blocks,) + small.shape)
    return jnp.concatenate([own, small], 1).astype(BF)


def weight_part(ref, part):
    w = ref[:, part]
    return w.reshape(w.shape[0] * w.shape[1], w.shape[2])


def mlp_kernel(
    xo_ref,
    xp_ref,
    go_ref,
    gp_ref,
    m_ref,
    b_ref,
    hidden_ref,
    dpre_ref,
    kept_ref,
    sent_ref,
):
    first = xo_ref.shape[0]
    b = bias_row(b_ref, 3)
    for i in range(2 * first):
        own = i < first
        pre = nn(group(xo_ref if own else xp_ref, i % first), weight_part(m_ref, 0)) + b
        dhidden = nn(group(go_ref if own else gp_ref, i % first), weight_part(m_ref, 1))
        share = 0.5 * (1.0 + lax.erf(pre * (0.5**0.5)))
        density = jnp.exp(pre * pre * -0.5) * ((0.5 / 3.141592653589793) ** 0.5)
        n = pre.shape[0]
        hidden_ref[i * n : (i + 1) * n, :] = (pre * share).astype(BF)
        dpre = (dhidden * (share + pre * density)).astype(BF)
        dpre_ref[i * n : (i + 1) * n, :] = dpre
        put_rows(kept_ref if own else sent_ref, i % first, nt(dpre, weight_part(m_ref, 0)))


def mlp_block(xo, xp, go, gp, m, b):
    blocks, pieces, thin, width = xo.shape
    low = jax.ShapeDtypeStruct((2 * blocks * pieces * thin, m.shape[-1]), BF)
    return pl.pallas_call(
        mlp_kernel,
        out_shape=(low, low, jax.ShapeDtypeStruct(xo.shape, F32), jax.ShapeDtypeStruct(xo.shape, BF)),
        in_specs=[VMEM] * 6,
        out_specs=(VMEM,) * 4,
        compiler_params=params(12),
        cost_estimate=cost(7, 12 << 20),
        name="mlp_block",
    )(xo, xp, go, gp, m, b)


def mlp_grads_kernel(
    xo_ref,
    xp_ref,
    dpre_ref,
    go_ref,
    gp_ref,
    hidden_ref,
    m_ref,
    grad_ref,
    kept_ref,
    sent_ref,
    sum_ref,
):
    first, width = xo_ref.shape[0], xo_ref.shape[3]
    half = width // 2
    rows = dpre_ref.shape[0]
    n = rows // 2

    def half_grads(i, carry):
        lanes = pl.ds(pl.multiple_of(i * half, 128), half)
        xo, xp = (ref[:, :, :, lanes].reshape(n, half) for ref in (xo_ref, xp_ref))
        up = tn(xo, dpre_ref[:n, :]) + tn(xp, dpre_ref[n:, :])
        grad_ref[:, i, 0] = up.astype(BF).reshape((-1,) + grad_ref.shape[3:])
        go, gp = (ref[:, :, :, lanes].reshape(n, half) for ref in (go_ref, gp_ref))
        down = tn(go, hidden_ref[:n, :]) + tn(gp, hidden_ref[n:, :])
        grad_ref[:, i, 1] = down.astype(BF).reshape((-1,) + grad_ref.shape[3:])
        return carry

    lax.fori_loop(0, 2, half_grads, 0)
    size = n // first
    for base, out_ref in ((0, kept_ref), (first, sent_ref)):

        def step(i, carry, base=base, out_ref=out_ref):
            part = pl.ds(pl.multiple_of((base + i) * size, size), size)
            put_rows(out_ref, i, nt(hidden_ref[part, :], weight_part(m_ref, 1)))
            return carry

        lax.fori_loop(0, first, step, 0)
    sum_ref[...] = jnp.sum(dpre_ref[...].astype(F32), 0, keepdims=True)


def mlp_grads(xo, xp, dpre, go, gp, hidden, m):
    return pl.pallas_call(
        mlp_grads_kernel,
        out_shape=(
            jax.ShapeDtypeStruct((m.shape[0] // 2, 2) + m.shape[1:], BF),
            jax.ShapeDtypeStruct(xo.shape, F32),
            jax.ShapeDtypeStruct(xo.shape, BF),
            jax.ShapeDtypeStruct((1, dpre.shape[1]), F32),
        ),
        in_specs=[VMEM] * 7,
        out_specs=(VMEM,) * 4,
        compiler_params=params(14),
        cost_estimate=cost(6, 12 << 20),
        name="mlp_grads",
    )(xo, xp, dpre, go, gp, hidden, m)


def attend_grads_kernel(
    flip_ref,
    sum_ref,
    norm_ref,
    dmix_ref,
    do_ref,
    dp_ref,
    att_ref,
    kept_ref,
    sent_ref,
    xo_ref,
    xp_ref,
    stay_ref,
    go_ref,
    vec_ref,
    xa,
):
    first, _, thin, width = kept_ref.shape
    rows, cols = att_ref.shape
    half = width // 2
    n = do_ref.shape[0]
    block = rows // (2 * first)
    vec_ref[...] = jnp.zeros_like(vec_ref)
    for base, x_ref, g_ref in ((0, xo_ref, kept_ref), (first, xp_ref, sent_ref)):

        def step(i, carry, base=base, x_ref=x_ref, g_ref=g_ref):
            normal, _ = normed(x_rows(x_ref, i, thin).astype(F32))
            xa[pl.ds(pl.multiple_of((base + i) * block, block), block), :] = (
                normal * norm_ref[0:1, :] + norm_ref[1:2, :]
            ).astype(BF)
            dx = group(g_ref, i).astype(F32)
            vec_ref[0:1, :] += jnp.sum(dx * normal, 0, keepdims=True)
            vec_ref[1:2, :] += jnp.sum(dx, 0, keepdims=True)
            return carry

        lax.fori_loop(0, first, step, 0)
    totals = [
        jnp.sum(dmix_ref[:, lanes_of(dmix_ref, c)].astype(F32), 0, keepdims=True).astype(BF)
        for c in (0, 2)
    ]

    def half_grads(i, out_ref):
        lanes = pl.ds(pl.multiple_of(i * half, 128), half)
        grads = tn(xa[:, lanes], dmix_ref[...]).astype(BF)
        for c in range(3):
            out_ref[:half, c * cols : (c + 1) * cols] = grads[:, lanes_of(dmix_ref, c)]
        out = tn(do_ref[:, lanes], att_ref[:n, :]) + tn(dp_ref[:, lanes], att_ref[n:, :])
        out_ref[:half, 3 * cols : 4 * cols] = out.astype(BF)
        out_ref[half : half + SPARE, :] = jnp.zeros((SPARE, out_ref.shape[1]), BF)
        for place, total in enumerate(totals):
            out_ref[half : half + 1, place * cols : (place + 1) * cols] = total
        out_ref[half + 1 : half + 2, : sum_ref.shape[1]] = sum_ref[...].astype(BF)

    half_grads(flip_ref[0], stay_ref)
    half_grads(1 - flip_ref[0], go_ref)


def attend_grads(flip, sums, norms, dmix, do, dp, att, kept, sent, xo, xp):
    width = do.shape[1]
    shape = jax.ShapeDtypeStruct((width // 2 + SPARE, 4 * att.shape[1]), BF)
    return pl.pallas_call(
        attend_grads_kernel,
        out_shape=(shape, shape, jax.ShapeDtypeStruct((2, width), F32)),
        in_specs=[SMEM] + [VMEM] * 10,
        out_specs=(VMEM,) * 3,
        scratch_shapes=[pltpu.VMEM((att.shape[0], width), BF)],
        compiler_params=params(14),
        cost_estimate=cost(6, 12 << 20),
        name="attend_grads",
    )(flip, sums, norms, dmix, do, dp, att, kept, sent, xo, xp)


def exact_low(x):
    one = lax.reduce_precision(x, 8, 7)
    two = lax.reduce_precision(x - one, 8, 7)
    return jnp.concatenate([one, two, x - one - two], 0).astype(BF)


def per_device(
    inputs,
    segments,
    ln1_gain,
    ln1_bias,
    query_key_value_weight,
    b_qv,
    output_weight,
    output_bias,
    ln2_gain,
    ln2_bias,
    up_weight,
    up_bias,
    down_weight,
    down_bias,
    out_grad,
):
    z = lax.axis_index("tp")
    ctx = lax.axis_index("ctx")
    planes = lax.axis_size("tp")
    thin, width = inputs.shape[1], inputs.shape[2]
    ds, _, cols = query_key_value_weight.shape
    hidden_cols = up_weight.shape[1]

    vectors = jnp.stack([ln1_gain, ln1_bias, output_bias, ln2_gain, ln2_bias, down_bias])
    rows_of = lambda a: a.reshape(-1, a.shape[-1])

    biases = jnp.pad(b_qv.reshape(1, -1), ((0, 0), (0, width - 2 * cols)))
    biases = [exact_low(biases), exact_low(up_bias.reshape(1, -1)), jnp.zeros((SPARE - 6, width), BF)]
    a_shard = jnp.concatenate(
        [query_key_value_weight.reshape(ds, 3 * cols), jnp.transpose(output_weight)], 1
    )
    a_shard = jnp.concatenate([a_shard] + biases, 0)
    labels = jnp.pad(segments.astype(BF)[:, None, :], ((0, 0), (0, SPARE - 1), (0, width - thin)))
    own = rows_over_z(jnp.concatenate([after(inputs, a_shard), labels, out_grad], 1))
    x_own, g_own = own[:, : thin + SPARE], own[:, thin + SPARE :]
    got = [send_turned(a_shard, k) for k in range(planes)]
    a_rows = place([g[:ds] for g in got], z).reshape(-1, width)
    biases = got[0][ds:]
    w_attn = weight_over_x(a_rows)
    x_pair, x_far = gather_ctx(after(x_own, w_attn)[None])
    g_own = after(g_own, x_pair)[None]

    m_shard = jnp.concatenate([up_weight, jnp.transpose(down_weight)], 0)
    m_shard = send_turned(after(m_shard, a_rows), 0)
    m_all = lax.all_gather(m_shard, ("fsdp", "tp"), axis=0, tiled=True)
    m_all = m_all.reshape(-1, 2, ds, hidden_cols)
    aligned = ds % 16 == 0 and m_all.shape[0] % 2 == 0
    if not aligned:
        m_all = m_all.reshape(2, -1, 2, ds, hidden_cols).transpose(0, 2, 1, 3, 4)
        m_all = m_all.reshape(2, 2, width // 2, hidden_cols)

    mixed, segr, lo, hi = qkv(x_pair, x_far, vectors, biases, w_attn, cols, thin)
    g_got = xor_swap(g_own, "ctx", 2)
    attended, lse, kept, sent = attend(lo, hi, mixed, segr, w_attn)
    g_got, kept, sent = lax.optimization_barrier((g_got, kept, sent))
    g_pair = jnp.concatenate([g_own, g_got], 0)
    g_far = xor_swap(g_pair, "ctx", 1)
    (s,) = core_sum(kept, sent, (2,))
    got = after(xor_swap(s, "ctx", 2), m_all)
    middle, xb_pair = middle_rows(s, got, x_pair, vectors[2:5])
    xb_far = xor_swap(xb_pair, "ctx", 1)

    hidden, dpre, kept, sent = mlp_block(xb_pair, xb_far, g_pair, g_far, m_all, biases)
    (s,) = core_sum(kept, sent, (2,))
    m_grad, mlp_kept, mlp_sent, dpre_sum = mlp_grads(
        xb_pair, xb_far, after(dpre, s), g_pair, g_far, hidden, m_all
    )
    got = xor_swap(s, "ctx", 2)
    mlp_s, mlp_low = core_sum(mlp_kept, after(mlp_sent, got), (1, 1))
    dmid, db_pair, sums_two = middle_back(
        s, after(got, dpre_sum), middle, g_pair, vectors[3:4]
    )
    db_far = xor_swap(db_pair, "ctx", 1)
    if not aligned:
        m_grad = m_grad[0].transpose(1, 0, 2, 3).reshape(2, -1, planes, ds, hidden_cols)
        m_grad = m_grad.transpose(2, 1, 0, 3, 4)
    m_sums = lax.psum_scatter(m_grad, "tp", scatter_dimension=0, tiled=False)
    mlp_got = xor_swap(after(mlp_low, db_far), "ctx", 2)

    dmix, kept, sent = attend_back(
        lo, hi, mixed, attended, lse, db_pair, db_far, segr, w_attn
    )
    s, low = core_sum(kept, after(sent, mlp_got), (1, 1))
    flip = lax.axis_index("fsdp") if lax.axis_size("fsdp") == 2 else 0
    got = xor_swap(low, "ctx", 2)
    g_stay, g_go, sums_one = attend_grads(
        jnp.full((1,), flip, jnp.int32),
        dpre_sum,
        vectors[0:2],
        after(rows_of(dmix), s),
        rows_of(db_pair),
        rows_of(db_far),
        rows_of(attended),
        kept,
        sent,
        x_pair,
        x_far,
    )
    vec = jnp.concatenate([vectors[0:1], vectors[5:6]], 0)
    shared = jnp.concatenate([sums_one, sums_two], 0)
    if lax.axis_size("fsdp") == 2:
        shared = shared + xor_swap(shared, "fsdp", 1)
    else:
        shared = lax.psum(shared, "fsdp")
    shared = shared + xor_swap(shared, "ctx", 1)
    both = first_back(s, after(got, shared), x_pair, dmid, middle, mlp_s, mlp_got, vec)
    shared = after(shared, both)
    shared = shared + xor_swap(shared, "ctx", 2)
    a_low = grad_pieces(g_stay, g_go, shared, planes)

    both = rows_over_z(both)
    output, input_grad = both[:, :thin], both[:, thin:].astype(F32)
    m_z = m_sums
    if lax.axis_size("fsdp") == 2:
        x = lax.axis_index("fsdp")
        m_got = xor_swap(pick(after(m_sums, a_low), x ^ 1), "fsdp", 1)
        m_sums = (pick(m_sums, x).astype(F32) + m_got.astype(F32)).astype(BF)
    else:
        m_sums = lax.psum_scatter(m_sums.astype(F32), "fsdp", scatter_dimension=0, tiled=False)
        m_sums = m_sums.astype(BF)
    m_back = send_back(m_sums.reshape(2 * ds, hidden_cols), 0)
    *got, m_back = lax.optimization_barrier((*scatter_blocks(a_low, m_z, both), m_back))

    g_attn = sum(g.astype(F32) for g in got)
    grad_qkv = g_attn[:ds, : 3 * cols].reshape(ds, 3, cols)
    grad_out = jnp.transpose(g_attn[:ds, 3 * cols :])
    mine, shared = g_attn[ds : ds + 2], g_attn[ds + 2 :]
    g_mlp = m_back.astype(F32)
    grad_up, grad_down = g_mlp[:ds], jnp.transpose(g_mlp[ds:])
    return (
        output,
        input_grad,
        shared[0],
        shared[1],
        grad_qkv,
        mine[0, : 2 * cols].reshape(2, cols),
        grad_out,
        shared[2],
        shared[3],
        shared[4],
        grad_up,
        mine[1, :hidden_cols],
        grad_down,
        shared[5],
    )


def solution(mesh):
    in_specs = (
        P("fsdp", ("ctx", "tp"), None),
        P("fsdp", ("ctx", "tp")),
        P(),
        P(),
        P(("fsdp", "ctx"), None, "tp"),
        P(None, "tp"),
        P("tp", ("fsdp", "ctx")),
        P(),
        P(),
        P(),
        P(("fsdp", "ctx"), "tp"),
        P("tp"),
        P("tp", ("fsdp", "ctx")),
        P(),
        P("fsdp", ("ctx", "tp"), None),
    )
    out_specs = (
        P("fsdp", ("ctx", "tp"), None),
        P("fsdp", ("ctx", "tp"), None),
        P(),
        P(),
        P(("fsdp", "ctx"), None, "tp"),
        P(None, "tp"),
        P("tp", ("fsdp", "ctx")),
        P(),
        P(),
        P(),
        P(("fsdp", "ctx"), "tp"),
        P("tp"),
        P("tp", ("fsdp", "ctx")),
        P(),
    )
    return jax.shard_map(
        per_device, mesh=mesh, in_specs=in_specs, out_specs=out_specs, check_vma=False
    )
```
